32 devices in a mesh: group: 2 (over y), dp: 4 (over x, core), tensor: 4 (over z).
Axes of the slice: x: 2, y: 2, z: 4, core: 2. Of those that a mesh axis runs over, the one named last changes fastest.
Arguments:
- tokens: bfloat16 [8192, 1024], P(('group', 'dp')), parts along dimension 0, may hold values from -6 to 6
- past_states: float32 [256, 8, 128, 128], P(('group', 'dp'), 'tensor'), parts along dimension 0, may hold values from -3 to 3
- attn_weights: bfloat16 [5, 1024, 1024], P(None, 'dp', 'tensor'), may hold values from -0.1875 to 0.1875
- ffn_weights: bfloat16 [2, 1024, 4096], P(None, 'dp', 'tensor'), may hold values from -0.1875 to 0.1875
- norm_gains: float32 [2, 1024], replicated, may hold values from 0.1 to 1.9
- head_rates: float32 [8], replicated, may hold values from 0.004 to 0.15
- end_lengths: int32 [256], P(('group', 'dp')), parts along dimension 0, may hold values from 1 to 64, as said below
- new_slot: int32 [256], P(('group', 'dp')), parts along dimension 0, may hold values from 0 to 127, as said below
Outputs:
- next_tokens: bfloat16 [8192, 1024], P(('group', 'dp'), 'tensor'), parts along dimension 0
- moved_states: float32 [256, 8, 128, 128], P(('group', 'dp'), 'tensor'), parts along dimension 0
The draws below stay inside these ranges and needn't reach their ends.
There are 2 independent parts, one for each index of `group`. The reference program is written for one: setup_inputs(seed, part) draws one part's arguments, and reference() takes and returns one part's arrays. A program takes and returns all parts, laid end to end along the dimension named above; an argument that names none is the same for every part. Nothing has to cross between parts.
Inputs may be any that keep to these rules, and one draw needn't show every extreme that they name: `end_lengths`: of the sessions in one aligned block of 32 sessions whose end lengths exceed 32, at most 16 have new slots in one aligned block of 32 slots, and some pair of blocks has exactly 16. `new_slot`: A permutation of the 128 slots.
All inputs are finite; a program needn't handle non-finite values.
Results may differ from the reference program's by a relative error of at most 0.018.
Values may be sent and summed in bfloat16 or wider, within the bound.
No kernel may reach another device: no remote copies, remote signals or barrier semaphores. Data moves between devices by JAX's collectives and lax.ppermute only.
A program may use at most 64 MiB of HBM per device.

```python
import math
import jax
import jax.numpy as jnp
from jax import lax

D = 1024
HEADS = 8
HD = 128
FF = 4096
EVENTS = 32
SESS_DEV = 32
SESSIONS = 128
TOKENS = 4096
PAIR = 16
N_TENSOR = 4


def joint_draw(key):
    base = jax.random.fold_in(key, 4242)
    subkeys = jax.random.split(base, 6)
    blocks = SESSIONS // SESS_DEV
    groups = SESSIONS // PAIR
    inner = jax.vmap(lambda subkey: jax.random.permutation(subkey, SESS_DEV))(jax.random.split(subkeys[0], blocks))
    session_order = (jnp.arange(blocks, dtype=jnp.int32)[:, None] * SESS_DEV + inner.astype(jnp.int32)).reshape(-1)
    group_dest = jax.random.permutation(subkeys[1], groups).astype(jnp.int32)
    position = jnp.arange(SESSIONS, dtype=jnp.int32)
    slot_at = group_dest[position // PAIR] * PAIR + position % PAIR
    new_slot = jnp.zeros((SESSIONS,), jnp.int32).at[session_order].set(slot_at)
    block_of = position // SESS_DEV
    level = jax.random.randint(subkeys[2], (blocks,), 2, 5)
    candidate = jax.random.randint(subkeys[3], (SESSIONS,), 0, 4) < level[block_of]
    chosen = jax.random.randint(subkeys[4], (), 0, groups)
    forced = jnp.zeros((SESSIONS,), bool).at[session_order].set(position // PAIR == chosen)
    candidate = candidate | forced
    pair_id = block_of * blocks + new_slot // SESS_DEV
    ahead = forced[None, :] & ~forced[:, None] | (forced[None, :] == forced[:, None]) & (position[None, :] < position[:, None])
    pair_rank = jnp.sum(candidate[None, :] & (pair_id[None, :] == pair_id[:, None]) & ahead, axis=1)
    survive = candidate & (pair_rank < PAIR)
    long_len = jax.random.randint(subkeys[5], (SESSIONS,), EVENTS + 1, 2 * EVENTS + 1)
    short_len = jax.random.randint(jax.random.fold_in(subkeys[5], 1), (SESSIONS,), 1, EVENTS + 1)
    lengths = jnp.where(survive, long_len, short_len).astype(jnp.int32)
    return (lengths, new_slot)


def draw_end_lengths(key, part):
    return joint_draw(key)[0]


def draw_new_slot(key, part):
    return joint_draw(key)[1]


def block_levels(stream_key, extent, shards, smallest, high):
    loudness = 1.0
    for axis_at, blocks in shards:
        steps = jax.random.uniform(jax.random.fold_in(jax.random.fold_in(stream_key, 6), axis_at), (blocks,), jnp.float32, smallest / len(shards), high / len(shards))
        loudness = loudness * jnp.repeat(jnp.exp(steps), extent[axis_at] // blocks).reshape((-1,) + (1,) * (len(extent) - 1 - axis_at))
    return loudness


def normal_values(key, shape, width, limit, shards=(), kind=jnp.bfloat16):
    factor_of = block_levels(key, shape, shards, -0.22, 0.18) if shards else 1.0
    entries = jax.random.normal(key, shape, jnp.float32) * width * factor_of
    return jnp.minimum(jnp.maximum(entries, -limit), limit).astype(kind)


def setup_inputs(seed: int = 0, part: int = 0) -> dict:
    arg_keys = jax.random.split(jax.random.key(seed), 9)
    part_splits = jax.random.split(jax.random.fold_in(arg_keys[8], part), 9)
    return {
        "tokens": normal_values(part_splits[0], (TOKENS, D), 1.0, 6.0, ((0, 4),)),
        "past_states": normal_values(part_splits[1], (SESSIONS, HEADS, HD, HD), 0.3, 3.0, ((0, 4), (1, 4)), jnp.float32),
        "attn_weights": normal_values(arg_keys[2], (5, D, HEADS * HD), D ** -0.5, 0.1875, ((1, 4), (2, 4))),
        "ffn_weights": normal_values(arg_keys[3], (2, D, FF), D ** -0.5, 0.1875, ((1, 4), (2, 4))),
        "norm_gains": jnp.clip(1.0 + 0.18 * jax.random.normal(arg_keys[4], (2, D), jnp.float32), 0.1, 1.9),
        "head_rates": jnp.clip(jnp.exp(jax.random.uniform(arg_keys[5], (HEADS,), jnp.float32, math.log(0.004), math.log(0.15))), 0.004, 0.15),
        "end_lengths": draw_end_lengths(jax.random.fold_in(jax.random.fold_in(arg_keys[8], part), 71), part),
        "new_slot": draw_new_slot(jax.random.fold_in(jax.random.fold_in(arg_keys[8], part), 71), part),
    }


def rms_scale(values, gain_row):
    meansq = lax.optimization_barrier(jnp.mean(values * values, axis=-1, keepdims=True))
    return (values * lax.rsqrt(meansq + 1e-05) * gain_row).astype(jnp.bfloat16)

def update_state(past_block, key_rows, value_rows, head_decay):
    event_count = key_rows.shape[2]
    position = jnp.arange(event_count).astype(jnp.float32)
    key_scale = key_rows.shape[3] ** (-0.5)
    factor = jnp.exp(-head_decay[:, None] * (event_count - 1.0 - position)[None, :])
    weighted = key_rows.astype(jnp.float32) * key_scale * factor[:, :, None]
    carried = jnp.exp(-head_decay * event_count)[:, None, None] * past_block
    return carried + jnp.einsum('ghjd,ghje->ghde', weighted, value_rows.astype(jnp.float32), precision=lax.Precision.HIGHEST)

def retain_events(query, key_rows, value_rows, past_block, head_decay):
    event_count = query.shape[2]
    position = jnp.arange(event_count).astype(jnp.float32)
    distance = position[:, None] - position[None, :]
    decay = jnp.where(distance >= 0, jnp.exp(-head_decay[:, None, None] * jnp.maximum(distance, 0.0)), 0.0)
    key_scale = query.shape[3] ** (-0.5)
    scores = jnp.einsum('ghid,ghjd->ghij', query.astype(jnp.float32), key_rows.astype(jnp.float32)) * key_scale
    weights_mix = (scores * decay).astype(jnp.bfloat16)
    intra_term = jnp.einsum('ghij,ghje->ghie', weights_mix.astype(jnp.float32), value_rows.astype(jnp.float32))
    inter_factor = jnp.exp(-head_decay[:, None] * (position[None, :] + 1.0))[:, :, None]
    inter_term = jnp.einsum('ghid,ghde->ghie', query.astype(jnp.float32), past_block, precision=lax.Precision.HIGHEST) * inter_factor
    return intra_term + inter_term

def round_trip(values):
    return lax.optimization_barrier(values.astype(jnp.bfloat16)).astype(jnp.float32)

def reference(tokens, past_states, attn_weights, ffn_weights, norm_gains, head_rates, end_lengths, new_slot):
    live_len = jnp.minimum(end_lengths, EVENTS)
    survive = end_lengths > EVENTS
    float_tokens = tokens.astype(jnp.float32)
    normed = rms_scale(float_tokens, norm_gains[0])
    projected = [jnp.dot(normed, attn_weights[which], preferred_element_type=jnp.float32) for which in range(4)]

    def split_heads(matrix):
        return matrix.reshape(SESSIONS, EVENTS, HEADS, HD).transpose(0, 2, 1, 3)
    query = split_heads(projected[0].astype(jnp.bfloat16))
    key_rows = split_heads(projected[1].astype(jnp.bfloat16))
    value_rows = split_heads(projected[2].astype(jnp.bfloat16))
    gate_rows = projected[3]
    retained = retain_events(query, key_rows, value_rows, past_states, head_rates)
    new_states = update_state(past_states, key_rows, value_rows, head_rates)
    row_mean = lax.optimization_barrier(jnp.mean(retained, axis=-1, keepdims=True))
    centred = retained - row_mean
    row_var = lax.optimization_barrier(jnp.mean(centred * centred, axis=-1, keepdims=True))
    normalised = centred * lax.rsqrt(row_var + 1e-05)
    merged = normalised.transpose(0, 2, 1, 3).reshape(TOKENS, HEADS * HD)
    gated = (jax.nn.silu(gate_rows) * merged).astype(jnp.bfloat16)
    group_cols = HEADS * HD // N_TENSOR
    attended = jnp.zeros((TOKENS, D), jnp.float32)
    for group_idx in range(N_TENSOR):
        start_col = group_idx * group_cols
        term = jnp.dot(gated[:, start_col:start_col + group_cols], attn_weights[4][:, start_col:start_col + group_cols].T, preferred_element_type=jnp.float32)
        attended = attended + round_trip(term)
    residual = float_tokens + attended
    hidden_in = rms_scale(residual, norm_gains[1])
    activated = jax.nn.gelu(jnp.dot(hidden_in, ffn_weights[0], preferred_element_type=jnp.float32), approximate=True).astype(jnp.bfloat16)
    unit_cols = FF // N_TENSOR
    ffn_out = jnp.zeros((TOKENS, D), jnp.float32)
    for group_idx in range(N_TENSOR):
        start_col = group_idx * unit_cols
        term = jnp.dot(activated[:, start_col:start_col + unit_cols], ffn_weights[1][:, start_col:start_col + unit_cols].T, preferred_element_type=jnp.float32)
        ffn_out = ffn_out + round_trip(term)
    keep_rows = (jnp.arange(EVENTS, dtype=jnp.int32)[None, :] < live_len[:, None]).reshape(-1)
    next_tokens = jnp.where(keep_rows[:, None], residual + ffn_out, 0.0).astype(jnp.bfloat16)
    inverse = jnp.zeros((SESSIONS,), jnp.int32).at[new_slot].set(jnp.arange(SESSIONS, dtype=jnp.int32))
    moved_states = jnp.where(survive[inverse][:, None, None, None], new_states[inverse], 0.0)
    return (next_tokens, moved_states)
```

```python
import functools
import jax
import jax.numpy as jnp
from jax import lax
from jax.experimental import pallas as pl
from jax.experimental.pallas import tpu as pltpu
from jax.sharding import PartitionSpec as P

CHUNKS = 2
BLOCK_ROWS = 256
VMEM_LIMIT = 56 * 1024 * 1024


NT = (((1,), (1,)), ((), ()))


def dot_nt(a, b):
    return lax.dot_general(a, b, NT, preferred_element_type=jnp.float32)


def dot_nn(a, b):
    return jnp.dot(a, b, preferred_element_type=jnp.float32)


def rms_scale(values, gain_row):
    meansq = jnp.mean(values * values, axis=-1, keepdims=True)
    return (values * lax.rsqrt(meansq + 1e-05) * gain_row).astype(jnp.bfloat16)


def piece_copies(pieces, dest, sems, me, pick):
    copies = []
    for k, piece in enumerate(pieces):
        rows = piece.shape[-2]
        start = pl.multiple_of(jnp.bitwise_xor(me, k) * rows, rows)
        copies.append(
            pltpu.make_async_copy(pick(piece), dest.at[..., pl.ds(start, rows), :], sems.at[k])
        )
    return copies


def project_kernel(n_dp, heads, event_count, *refs):
    ids_ref, rates_ref, tok_ref, gain_ref, past_ref = refs[:5]
    pieces = refs[5 : 5 + n_dp]
    gated_ref, key_ref, value_ref = refs[5 + n_dp : 8 + n_dp]
    w_ref, decay_ref, sems = refs[8 + n_dp :]
    rows = tok_ref.shape[0]
    head_dim = past_ref.shape[3]
    sessions = rows // event_count
    key_scale = head_dim ** (-0.5)
    first = pl.program_id(0) == 0
    copies = piece_copies(pieces, w_ref, sems, ids_ref[0], lambda piece: piece)

    @pl.when(first)
    def _():
        for copy in copies:
            copy.start()
        at = lax.broadcasted_iota(jnp.int32, (rows, rows), 0)
        to = lax.broadcasted_iota(jnp.int32, (rows, rows), 1)
        allowed = (at // event_count == to // event_count) & (at >= to)
        distance = jnp.maximum(at - to, 0).astype(jnp.float32)
        for h in range(heads):
            rate = rates_ref[ids_ref[1] * heads + h]
            decay_ref[h] = jnp.where(allowed, jnp.exp(-rate * distance), 0.0) * key_scale

    normed = rms_scale(tok_ref[...].astype(jnp.float32), gain_ref[0:1, :])

    @pl.when(first)
    def _():
        for copy in copies:
            copy.wait()

    query = dot_nn(normed, w_ref[0]).astype(jnp.bfloat16)
    keys = dot_nn(normed, w_ref[1]).astype(jnp.bfloat16)
    key_ref[...] = keys
    values = dot_nn(normed, w_ref[2]).astype(jnp.bfloat16)
    value_ref[...] = values
    gate = dot_nn(normed, w_ref[3])
    place = lax.broadcasted_iota(jnp.int32, (rows, head_dim), 0) % event_count
    for h in range(heads):
        cols = slice(h * head_dim, (h + 1) * head_dim)
        qh, kh, vh = query[:, cols], keys[:, cols], values[:, cols]
        mix = (dot_nt(qh, kh) * decay_ref[h]).astype(jnp.bfloat16)
        intra = dot_nn(mix, vh)
        parts = []
        for s in range(sessions):
            parts.append(
                dot_nn(
                    qh[s * event_count : (s + 1) * event_count],
                    past_ref[s, h].astype(jnp.bfloat16),
                )
            )
        rate = rates_ref[ids_ref[1] * heads + h]
        factor = jnp.exp(-rate * (place + 1).astype(jnp.float32))
        retained = intra + jnp.concatenate(parts, axis=0) * factor
        centred = retained - jnp.mean(retained, axis=-1, keepdims=True)
        row_var = jnp.mean(centred * centred, axis=-1, keepdims=True)
        normalised = centred * lax.rsqrt(row_var + 1e-05)
        gated_ref[:, cols] = (jax.nn.silu(gate[:, cols]) * normalised).astype(jnp.bfloat16)


def state_kernel(heads, event_count, *refs):
    ids_ref, rates_ref, pos_ref, key_ref, value_ref, past_ref = refs[:6]
    out_ref = refs[6]
    buf_ref, sems = refs[7:]
    sessions, _, head_dim, _ = past_ref.shape
    step = pl.program_id(0)
    steps = pl.num_programs(0)
    slot = lax.rem(step, 2)
    key_scale = head_dim ** (-0.5)

    def copy_of(which_slot, session, target):
        return pltpu.make_async_copy(
            buf_ref.at[which_slot, session], out_ref.at[target], sems.at[which_slot, session]
        )

    def drain(which_slot, which_step):
        for s in range(sessions):
            pos = pos_ref[which_step * sessions + s]

            @pl.when(pos >= 0)
            def _():
                copy_of(which_slot, s, pos).wait()

    @pl.when(step >= 2)
    def _():
        drain(slot, step - 2)

    place = lax.broadcasted_iota(jnp.int32, (key_ref.shape[0], head_dim), 0) % event_count
    left = (event_count - 1 - place).astype(jnp.float32)
    for h in range(heads):
        rate = rates_ref[ids_ref[1] * heads + h]
        cols = slice(h * head_dim, (h + 1) * head_dim)
        factor = jnp.exp(-rate * left) * key_scale
        weighted = (key_ref[:, cols].astype(jnp.float32) * factor).astype(jnp.bfloat16)
        carry = jnp.exp(jnp.full((head_dim, head_dim), -rate * event_count, jnp.float32))
        for s in range(sessions):
            span = slice(s * event_count, (s + 1) * event_count)
            grown = lax.dot_general(
                weighted[span],
                value_ref[span, cols],
                (((0,), (0,)), ((), ())),
                preferred_element_type=jnp.float32,
            )
            buf_ref[slot, s, h] = (carry * past_ref[s, h] + grown).astype(jnp.bfloat16)
    for s in range(sessions):
        pos = pos_ref[step * sessions + s]

        @pl.when(pos >= 0)
        def _():
            copy_of(slot, s, pos).start()

    @pl.when(step == steps - 1)
    def _():
        @pl.when(step >= 1)
        def _():
            drain(1 - slot, step - 1)

        drain(slot, step)


def unpack_kernel(src_ref, recv_ref, out_ref, buf_ref, sems):
    per_step = out_ref.shape[0]
    step = pl.program_id(0)

    def copy_of(slot):
        return pltpu.make_async_copy(
            recv_ref.at[jnp.maximum(src_ref[slot], 0)], buf_ref.at[slot], sems.at[slot]
        )

    @pl.when(step == 0)
    def _():
        for slot in range(buf_ref.shape[0]):

            @pl.when(src_ref[slot] >= 0)
            def _():
                copy_of(slot).start()

    for i in range(per_step):
        slot = step * per_step + i

        @pl.when(src_ref[slot] >= 0)
        def _():
            copy_of(slot).wait()
            out_ref[i] = buf_ref[slot].astype(jnp.float32)

        @pl.when(src_ref[slot] < 0)
        def _():
            out_ref[i] = jnp.zeros(out_ref.shape[1:], jnp.float32)


def feed_kernel(n_dp, n_tensor, *refs):
    ids_ref, tok_ref, gain_ref = refs[:3]
    gated = refs[3 : 3 + n_tensor]
    at = 3 + n_tensor
    out_pieces = refs[at : at + n_dp]
    ffn_pieces = refs[at + n_dp : at + 2 * n_dp]
    at += 2 * n_dp
    part_ref, own_ref = refs[at : at + 2]
    wo_ref, wf_ref, res_ref, sem_out, sem_up, sem_down = refs[at + 2 :]
    first = pl.program_id(0) == 0
    me = ids_ref[0]
    out_copies = piece_copies(out_pieces, wo_ref, sem_out, me, lambda piece: piece)
    up_copies = piece_copies(ffn_pieces, wf_ref.at[0], sem_up, me, lambda piece: piece.at[0])
    down_copies = piece_copies(ffn_pieces, wf_ref.at[1], sem_down, me, lambda piece: piece.at[1])

    @pl.when(first)
    def _():
        for copy in out_copies + up_copies + down_copies:
            copy.start()
        for copy in out_copies:
            copy.wait()

    attended = dot_nt(gated[0][...], wo_ref[0])
    for k in range(1, n_tensor):
        attended += dot_nt(gated[k][...], wo_ref[k])
    residual = tok_ref[...].astype(jnp.float32) + attended
    res_ref[...] = residual
    width = own_ref.shape[1]
    own_ref[...] = res_ref[:, pl.ds(pl.multiple_of(ids_ref[1] * width, width), width)]
    hidden = rms_scale(residual, gain_ref[1:2, :])

    @pl.when(first)
    def _():
        for copy in up_copies:
            copy.wait()

    activated = jax.nn.gelu(dot_nn(hidden, wf_ref[0]), approximate=True).astype(jnp.bfloat16)

    @pl.when(first)
    def _():
        for copy in down_copies:
            copy.wait()

    for k in range(n_tensor):
        part_ref[k] = dot_nt(activated, wf_ref[1, k * width : (k + 1) * width, :]).astype(
            jnp.bfloat16
        )


def xor_gather(value, axis):
    pieces = [value]
    size = lax.axis_size(axis)
    bit = size // 2
    order = [0]
    while bit:
        pairs = [(i, i ^ bit) for i in range(size)]
        pieces = pieces + [lax.ppermute(piece, axis, pairs) for piece in pieces]
        order = order + [k ^ bit for k in order]
        bit //= 2
    return [pieces[order.index(k)] for k in range(size)]


def ring_pairs(size):
    order = list(range(0, size, 2)) + list(range(1, size, 2))[::-1]
    return [(order[i], order[(i + 1) % size]) for i in range(size)]


def any_spec():
    return pl.BlockSpec(memory_space=pl.ANY)


def smem_spec():
    return pl.BlockSpec(memory_space=pltpu.SMEM)


def per_device(
    tokens, past_states, attn_weights, ffn_weights, norm_gains, head_rates, end_lengths, new_slot
):
    sessions_here = end_lengths.shape[0]
    row_count, width = tokens.shape
    event_count = row_count // sessions_here
    heads_here, head_dim = past_states.shape[1], past_states.shape[3]
    cols_here = heads_here * head_dim
    units_here = ffn_weights.shape[2]
    n_dp, n_tensor = lax.axis_size("dp"), lax.axis_size("tensor")
    dp_at, tensor_at = lax.axis_index("dp"), lax.axis_index("tensor")
    share = width // n_tensor
    pair_cap = max(2, 2 * sessions_here // n_dp)
    slot_count = n_dp * pair_cap
    chunk_rows = row_count // CHUNKS
    block = min(BLOCK_ROWS, chunk_rows)
    block_sessions = block // event_count
    steps = chunk_rows // block
    ring = ring_pairs(n_tensor)
    ids = jnp.stack([dp_at, tensor_at]).astype(jnp.int32)

    with jax.named_scope("w_proj"):
        proj_pieces = xor_gather(attn_weights[:4], "dp")
    with jax.named_scope("w_out_ring"):
        out_blocks = [attn_weights[4]]
        for _ in range(n_tensor - 1):
            out_blocks.append(lax.ppermute(out_blocks[-1], "tensor", ring))
        out_own = jnp.stack(out_blocks)

    with jax.named_scope("meta"):
        meta = lax.all_gather(jnp.stack([end_lengths, new_slot]), "dp")
        survive = end_lengths > event_count
        target_dev = new_slot // sessions_here
        session_ids = jnp.arange(sessions_here, dtype=jnp.int32)
        earlier = (
            (target_dev[None, :] == target_dev[:, None])
            & survive[None, :]
            & (session_ids[None, :] < session_ids[:, None])
        )
        pair_rank = jnp.sum(earlier.astype(jnp.int32), axis=1)
        send_pos = jnp.where(survive, target_dev * pair_cap + pair_rank, -1)
        slot_all = meta[:, 1]
        coming = (meta[:, 0] > event_count) & (slot_all // sessions_here == dp_at)
        ahead = coming[:, None, :] & (session_ids[None, None, :] < session_ids[None, :, None])
        rank_all = jnp.sum(ahead.astype(jnp.int32), axis=2)
        from_pos = jnp.arange(n_dp, dtype=jnp.int32)[:, None] * pair_cap + rank_all + 1
        lands = (slot_all % sessions_here)[None] == session_ids[:, None, None]
        recv_src = jnp.sum(jnp.where(lands & coming[None], from_pos[None], 0), axis=(1, 2)) - 1

    def project(c):
        base = c * steps
        return pl.pallas_call(
            functools.partial(project_kernel, n_dp, heads_here, event_count),
            grid=(steps,),
            in_specs=[
                smem_spec(),
                smem_spec(),
                pl.BlockSpec((block, width), lambda i: (base + i, 0)),
                pl.BlockSpec(norm_gains.shape, lambda i: (0, 0)),
                pl.BlockSpec(
                    (block_sessions, heads_here, head_dim, head_dim),
                    lambda i: (base + i, 0, 0, 0),
                ),
            ]
            + [any_spec()] * n_dp,
            out_specs=[pl.BlockSpec((block, cols_here), lambda i: (i, 0))] * 3,
            out_shape=[jax.ShapeDtypeStruct((chunk_rows, cols_here), jnp.bfloat16)] * 3,
            scratch_shapes=[
                pltpu.VMEM((4, width, cols_here), jnp.bfloat16),
                pltpu.VMEM((heads_here, block, block), jnp.float32),
                pltpu.SemaphoreType.DMA((n_dp,)),
            ],
            compiler_params=pltpu.CompilerParams(vmem_limit_bytes=VMEM_LIMIT),
            cost_estimate=pl.CostEstimate(
                flops=2 * chunk_rows * width * cols_here * 4,
                bytes_accessed=chunk_rows * width * 4,
                transcendentals=0,
            ),
            name="project",
        )(ids, head_rates, tokens, norm_gains, past_states, *proj_pieces)

    gated, keys, values = [], [], []
    for c in range(CHUNKS):
        with jax.named_scope(f"project{c}"):
            g, k, v = project(c)
        gated.append([g])
        keys.append(k)
        values.append(v)
    for _ in range(n_tensor - 1):
        for c in range(CHUNKS):
            with jax.named_scope(f"gated_ring{c}"):
                gated[c].append(lax.ppermute(gated[c][-1], "tensor", ring))

    with jax.named_scope("w_out"):
        out_pieces = xor_gather(out_own, "dp")
    with jax.named_scope("w_ffn"):
        ffn_pieces = xor_gather(ffn_weights, "dp")

    with jax.named_scope("states"):
        all_keys, all_values = jnp.concatenate(keys), jnp.concatenate(values)
        packed = pl.pallas_call(
            functools.partial(state_kernel, heads_here, event_count),
            grid=(row_count // block,),
            in_specs=[smem_spec(), smem_spec(), smem_spec()]
            + [pl.BlockSpec((block, cols_here), lambda i: (i, 0))] * 2
            + [
                pl.BlockSpec(
                    (block_sessions, heads_here, head_dim, head_dim), lambda i: (i, 0, 0, 0)
                )
            ],
            out_specs=any_spec(),
            out_shape=jax.ShapeDtypeStruct(
                (slot_count, heads_here, head_dim, head_dim), jnp.bfloat16
            ),
            scratch_shapes=[
                pltpu.VMEM((2, block_sessions, heads_here, head_dim, head_dim), jnp.bfloat16),
                pltpu.SemaphoreType.DMA((2, block_sessions)),
            ],
            compiler_params=pltpu.CompilerParams(vmem_limit_bytes=VMEM_LIMIT),
            cost_estimate=pl.CostEstimate(
                flops=2 * row_count * head_dim * cols_here,
                bytes_accessed=past_states.size * 6,
                transcendentals=0,
            ),
            name="states",
        )(ids, head_rates, send_pos, all_keys, all_values, past_states)
        received = lax.all_to_all(packed, "dp", split_axis=0, concat_axis=0, tiled=True)

    def feed(c):
        base = c * steps
        row_spec = pl.BlockSpec((block, cols_here), lambda i: (i, 0))
        return pl.pallas_call(
            functools.partial(feed_kernel, n_dp, n_tensor),
            grid=(steps,),
            in_specs=[
                smem_spec(),
                pl.BlockSpec((block, width), lambda i: (base + i, 0)),
                pl.BlockSpec(norm_gains.shape, lambda i: (0, 0)),
            ]
            + [row_spec] * n_tensor
            + [any_spec()] * (2 * n_dp),
            out_specs=[
                pl.BlockSpec((n_tensor, block, share), lambda i: (0, i, 0)),
                pl.BlockSpec((block, share), lambda i: (i, 0)),
            ],
            out_shape=[
                jax.ShapeDtypeStruct((n_tensor, chunk_rows, share), jnp.bfloat16),
                jax.ShapeDtypeStruct((chunk_rows, share), jnp.float32),
            ],
            scratch_shapes=[
                pltpu.VMEM((n_tensor, width, cols_here), jnp.bfloat16),
                pltpu.VMEM((2, width, units_here), jnp.bfloat16),
                pltpu.VMEM((block, width), jnp.float32),
                pltpu.SemaphoreType.DMA((n_dp,)),
                pltpu.SemaphoreType.DMA((n_dp,)),
                pltpu.SemaphoreType.DMA((n_dp,)),
            ],
            compiler_params=pltpu.CompilerParams(vmem_limit_bytes=VMEM_LIMIT),
            cost_estimate=pl.CostEstimate(
                flops=2 * chunk_rows * width * (width + 2 * units_here),
                bytes_accessed=chunk_rows * width * 8,
                transcendentals=0,
            ),
            name="feed",
        )(ids, tokens, norm_gains, *gated[c], *out_pieces, *ffn_pieces)

    live_len = jnp.minimum(end_lengths, event_count)
    chunk_sessions = sessions_here // CHUNKS
    rows_out = []
    for c in range(CHUNKS):
        with jax.named_scope(f"feed{c}"):
            part, own = feed(c)
        with jax.named_scope(f"scatter{c}"):
            terms = lax.all_to_all(part, "tensor", split_axis=0, concat_axis=0, tiled=True)
        with jax.named_scope(f"last{c}"):
            live = live_len[c * chunk_sessions : (c + 1) * chunk_sessions]
            keep = (jnp.arange(event_count, dtype=jnp.int32)[None, :] < live[:, None]).reshape(-1)
            total = own + jnp.sum(terms.astype(jnp.float32), axis=0)
            rows_out.append(jnp.where(keep[:, None], total, 0.0).astype(jnp.bfloat16))
    next_tokens = jnp.concatenate(rows_out)

    with jax.named_scope("unpack"):
        per_step = min(8, sessions_here)
        moved_states = pl.pallas_call(
            unpack_kernel,
            grid=(sessions_here // per_step,),
            in_specs=[smem_spec(), any_spec()],
            out_specs=pl.BlockSpec(
                (per_step, heads_here, head_dim, head_dim), lambda i: (i, 0, 0, 0)
            ),
            out_shape=jax.ShapeDtypeStruct(past_states.shape, jnp.float32),
            scratch_shapes=[
                pltpu.VMEM((sessions_here, heads_here, head_dim, head_dim), jnp.bfloat16),
                pltpu.SemaphoreType.DMA((sessions_here,)),
            ],
            compiler_params=pltpu.CompilerParams(vmem_limit_bytes=VMEM_LIMIT),
            cost_estimate=pl.CostEstimate(
                flops=0, bytes_accessed=past_states.size * 6, transcendentals=0
            ),
            name="unpack",
        )(recv_src, received)
    return (next_tokens, moved_states)


def solution(mesh):
    placed = (
        P(("group", "dp"), None),
        P(("group", "dp"), "tensor", None, None),
        P(None, "dp", "tensor"),
        P(None, "dp", "tensor"),
        P(),
        P(),
        P(("group", "dp")),
        P(("group", "dp")),
    )
    return jax.shard_map(
        per_device,
        mesh=mesh,
        in_specs=placed,
        out_specs=(P(("group", "dp"), "tensor"), P(("group", "dp"), "tensor", None, None)),
        check_vma=False,
    )
```

```python
import functools
import jax
import jax.numpy as jnp
from jax import lax
from jax.experimental import pallas as pl
from jax.experimental.pallas import tpu as pltpu
from jax.sharding import PartitionSpec as P

CHUNKS = 2
BLOCK_ROWS = 256
VMEM_LIMIT = 56 * 1024 * 1024


NT = (((1,), (1,)), ((), ()))


def dot_nt(a, b):
    return lax.dot_general(a, b, NT, preferred_element_type=jnp.float32)


def dot_nn(a, b):
    return jnp.dot(a, b, preferred_element_type=jnp.float32)


def rms_scale(values, gain_row):
    meansq = jnp.mean(values * values, axis=-1, keepdims=True)
    return (values * lax.rsqrt(meansq + 1e-05) * gain_row).astype(jnp.bfloat16)


def piece_copies(pieces, dest, sems, me, pick):
    copies = []
    rows = dest.shape[-2] // len(pieces)
    for k, piece in enumerate(pieces):
        start = pl.multiple_of(jnp.bitwise_xor(me, k) * rows, rows)
        copies.append(
            pltpu.make_async_copy(pick(piece), dest.at[..., pl.ds(start, rows), :], sems.at[k])
        )
    return copies


def project_kernel(n_dp, heads, event_count, *refs):
    ids_ref, rates_ref, tok_ref, gain_ref, past_ref = refs[:5]
    pieces = refs[5 : 5 + n_dp]
    gated_ref, key_ref, value_ref, w_ref, decay_ref, sems = refs[-6:]
    rows = tok_ref.shape[0]
    head_dim = past_ref.shape[3]
    sessions = rows // event_count
    key_scale = head_dim ** (-0.5)
    first = pl.program_id(0) == 0
    depth = w_ref.shape[1] // n_dp
    copies = []
    for m in range(4):
        span = pl.ds(m * depth, depth)
        copies += piece_copies(
            pieces, w_ref.at[m], sems.at[m], ids_ref[0], lambda piece: piece.at[span]
        )

    @pl.when(first)
    def _():
        for copy in copies:
            copy.start()
        at = lax.broadcasted_iota(jnp.int32, (rows, rows), 0)
        to = lax.broadcasted_iota(jnp.int32, (rows, rows), 1)
        allowed = (at // event_count == to // event_count) & (at >= to)
        distance = jnp.maximum(at - to, 0).astype(jnp.float32)
        for h in range(heads):
            rate = rates_ref[ids_ref[1] * heads + h]
            decay_ref[h] = jnp.where(allowed, jnp.exp(-rate * distance), 0.0) * key_scale

    normed = rms_scale(tok_ref[...].astype(jnp.float32), gain_ref[0:1, :])

    @pl.when(first)
    def _():
        for copy in copies:
            copy.wait()

    query = dot_nn(normed, w_ref[0]).astype(jnp.bfloat16)
    keys = dot_nn(normed, w_ref[1]).astype(jnp.bfloat16)
    key_ref[...] = keys
    values = dot_nn(normed, w_ref[2]).astype(jnp.bfloat16)
    value_ref[...] = values
    gate = dot_nn(normed, w_ref[3])
    place = lax.broadcasted_iota(jnp.int32, (rows, head_dim), 0) % event_count
    for h in range(heads):
        cols = slice(h * head_dim, (h + 1) * head_dim)
        qh, kh, vh = query[:, cols], keys[:, cols], values[:, cols]
        mix = (dot_nt(qh, kh) * decay_ref[h]).astype(jnp.bfloat16)
        intra = dot_nn(mix, vh)
        parts = []
        for s in range(sessions):
            parts.append(
                dot_nn(
                    qh[s * event_count : (s + 1) * event_count],
                    past_ref[s, h].astype(jnp.bfloat16),
                )
            )
        rate = rates_ref[ids_ref[1] * heads + h]
        factor = jnp.exp(-rate * (place + 1).astype(jnp.float32))
        retained = intra + jnp.concatenate(parts, axis=0) * factor
        centred = retained - jnp.mean(retained, axis=-1, keepdims=True)
        row_var = jnp.mean(centred * centred, axis=-1, keepdims=True)
        normalised = centred * lax.rsqrt(row_var + 1e-05)
        gated_ref[:, cols] = (jax.nn.silu(gate[:, cols]) * normalised).astype(jnp.bfloat16)


def state_kernel(heads, event_count, *refs):
    ids_ref, rates_ref, pos_ref, key_ref, value_ref, past_ref = refs[:6]
    out_ref = refs[6]
    buf_ref, sems = refs[7:]
    sessions, _, head_dim, _ = past_ref.shape
    step = pl.program_id(0)
    steps = pl.num_programs(0)
    slot = lax.rem(step, 2)
    key_scale = head_dim ** (-0.5)

    def copy_of(which_slot, session, target):
        return pltpu.make_async_copy(
            buf_ref.at[which_slot, session], out_ref.at[target], sems.at[which_slot, session]
        )

    def drain(which_slot, which_step):
        for s in range(sessions):
            pos = pos_ref[which_step * sessions + s]

            @pl.when(pos >= 0)
            def _():
                copy_of(which_slot, s, pos).wait()

    @pl.when(step >= 2)
    def _():
        drain(slot, step - 2)

    place = lax.broadcasted_iota(jnp.int32, (key_ref.shape[0], head_dim), 0) % event_count
    left = (event_count - 1 - place).astype(jnp.float32)
    for h in range(heads):
        rate = rates_ref[ids_ref[1] * heads + h]
        cols = slice(h * head_dim, (h + 1) * head_dim)
        factor = jnp.exp(-rate * left) * key_scale
        weighted = (key_ref[:, cols].astype(jnp.float32) * factor).astype(jnp.bfloat16)
        carry = jnp.exp(jnp.full((head_dim, head_dim), -rate * event_count, jnp.float32))
        for s in range(sessions):
            span = slice(s * event_count, (s + 1) * event_count)
            grown = lax.dot_general(
                weighted[span],
                value_ref[span, cols],
                (((0,), (0,)), ((), ())),
                preferred_element_type=jnp.float32,
            )
            buf_ref[slot, s, h] = (carry * past_ref[s, h] + grown).astype(jnp.bfloat16)
    for s in range(sessions):
        pos = pos_ref[step * sessions + s]

        @pl.when(pos >= 0)
        def _():
            copy_of(slot, s, pos).start()

    @pl.when(step == steps - 1)
    def _():
        @pl.when(step >= 1)
        def _():
            drain(1 - slot, step - 1)

        drain(slot, step)


def unpack_kernel(src_ref, recv_ref, out_ref, buf_ref, sems):
    per_step = out_ref.shape[0]
    step = pl.program_id(0)

    def copy_of(slot):
        return pltpu.make_async_copy(
            recv_ref.at[jnp.maximum(src_ref[slot], 0)], buf_ref.at[slot], sems.at[slot]
        )

    @pl.when(step == 0)
    def _():
        for slot in range(buf_ref.shape[0]):

            @pl.when(src_ref[slot] >= 0)
            def _():
                copy_of(slot).start()

    for i in range(per_step):
        slot = step * per_step + i

        @pl.when(src_ref[slot] >= 0)
        def _():
            copy_of(slot).wait()
            out_ref[i] = buf_ref[slot].astype(jnp.float32)

        @pl.when(src_ref[slot] < 0)
        def _():
            out_ref[i] = jnp.zeros(out_ref.shape[1:], jnp.float32)


def feed_kernel(n_dp, n_tensor, *refs):
    ids_ref, tok_ref, gain_ref = refs[:3]
    gated = refs[3 : 3 + n_tensor]
    at = 3 + n_tensor
    out_pieces = refs[at : at + n_dp]
    ffn_pieces = refs[at + n_dp : at + 2 * n_dp]
    at += 2 * n_dp
    own_ref = refs[at]
    part_refs = refs[at + 1 : at + n_tensor]
    wo_ref, wf_ref, res_ref, sem_out, sem_up, sem_down = refs[at + n_tensor :]
    first = pl.program_id(0) == 0
    me = ids_ref[0]
    out_copies = piece_copies(out_pieces, wo_ref, sem_out, me, lambda piece: piece)
    up_copies = piece_copies(ffn_pieces, wf_ref.at[0], sem_up, me, lambda piece: piece.at[0])
    down_copies = piece_copies(ffn_pieces, wf_ref.at[1], sem_down, me, lambda piece: piece.at[1])

    @pl.when(first)
    def _():
        for copy in out_copies + up_copies + down_copies:
            copy.start()
        for copy in out_copies:
            copy.wait()

    attended = dot_nt(gated[0][...], wo_ref[ids_ref[2]])
    for k in range(1, n_tensor):
        attended += dot_nt(gated[k][...], wo_ref[ids_ref[2 + k]])
    residual = tok_ref[...].astype(jnp.float32) + attended
    res_ref[...] = residual
    width = own_ref.shape[1]
    hidden = rms_scale(residual, gain_ref[1:2, :])

    @pl.when(first)
    def _():
        for copy in up_copies:
            copy.wait()

    activated = jax.nn.gelu(dot_nn(hidden, wf_ref[0]), approximate=True).astype(jnp.bfloat16)

    @pl.when(first)
    def _():
        for copy in down_copies:
            copy.wait()

    def term(k):
        owner = lax.rem(ids_ref[1] + k, n_tensor)
        span = pl.ds(pl.multiple_of(owner * width, width), width)
        return dot_nt(activated, wf_ref[1, span, :])

    for k in range(1, n_tensor):
        part_refs[k - 1][...] = term(k).astype(jnp.bfloat16)
    mine = pl.ds(pl.multiple_of(ids_ref[1] * width, width), width)
    own_ref[...] = res_ref[:, mine] + term(0)


def xor_gather(value, axis):
    pieces = [value]
    size = lax.axis_size(axis)
    bit = size // 2
    order = [0]
    while bit:
        pairs = [(i, i ^ bit) for i in range(size)]
        arrived = []
        for piece in pieces:
            arrived.append(lax.ppermute(piece, axis, pairs))
        pieces = pieces + arrived
        order = order + [k ^ bit for k in order]
        bit //= 2
    return [pieces[order.index(k)] for k in range(size)]


def ring_order(size):
    return list(range(0, size, 2)) + list(range(1, size, 2))[::-1]


def ring_pairs(size):
    order = ring_order(size)
    return [(order[i], order[(i + 1) % size]) for i in range(size)]


def ring_sources(size):
    order = ring_order(size)
    return [[order[(order.index(at) - k) % size] for k in range(size)] for at in range(size)]


def any_spec():
    return pl.BlockSpec(memory_space=pl.ANY)


def smem_spec():
    return pl.BlockSpec(memory_space=pltpu.SMEM)


def per_device(
    tokens, past_states, attn_weights, ffn_weights, norm_gains, head_rates, end_lengths, new_slot
):
    sessions_here = end_lengths.shape[0]
    row_count, width = tokens.shape
    event_count = row_count // sessions_here
    heads_here, head_dim = past_states.shape[1], past_states.shape[3]
    cols_here = heads_here * head_dim
    units_here = ffn_weights.shape[2]
    n_dp, n_tensor = lax.axis_size("dp"), lax.axis_size("tensor")
    dp_at, tensor_at = lax.axis_index("dp"), lax.axis_index("tensor")
    share = width // n_tensor
    pair_cap = max(2, 2 * sessions_here // n_dp)
    slot_count = n_dp * pair_cap
    chunk_rows = row_count // CHUNKS
    block = min(BLOCK_ROWS, chunk_rows)
    block_sessions = block // event_count
    steps = chunk_rows // block
    ring = ring_pairs(n_tensor)
    sources = jnp.array(ring_sources(n_tensor), jnp.int32)[tensor_at]
    ids = jnp.concatenate([jnp.stack([dp_at, tensor_at]).astype(jnp.int32), sources])

    survive = end_lengths > event_count
    target_dev = new_slot // sessions_here
    session_ids = jnp.arange(sessions_here, dtype=jnp.int32)
    proj_rows = attn_weights.shape[1]
    notes = jnp.stack([jnp.where(survive, target_dev, -1), new_slot % sessions_here])
    notes = jnp.pad(notes.astype(jnp.bfloat16), ((0, 6), (0, cols_here - sessions_here)))
    proj_own = jnp.concatenate([attn_weights[:4].reshape(4 * proj_rows, cols_here), notes])
    proj_pieces = xor_gather(proj_own, "dp")
    out_own = lax.all_to_all(
        jnp.broadcast_to(attn_weights[4:], (n_tensor, proj_rows, cols_here)),
        "tensor",
        split_axis=0,
        concat_axis=0,
        tiled=True,
    )

    meta = jnp.stack([piece[4 * proj_rows :, :sessions_here] for piece in proj_pieces])
    meta = meta.astype(jnp.int32)
    from_dev = jnp.bitwise_xor(dp_at, jnp.arange(n_dp, dtype=jnp.int32))
    earlier = (
        (target_dev[None, :] == target_dev[:, None])
        & survive[None, :]
        & (session_ids[None, :] < session_ids[:, None])
    )
    pair_rank = jnp.sum(earlier.astype(jnp.int32), axis=1)
    send_pos = jnp.where(survive, target_dev * pair_cap + pair_rank, -1)
    coming = meta[:, 0] == dp_at
    ahead = coming[:, None, :] & (session_ids[None, None, :] < session_ids[None, :, None])
    rank_all = jnp.sum(ahead.astype(jnp.int32), axis=2)
    from_pos = from_dev[:, None] * pair_cap + rank_all + 1
    lands = meta[:, 1][None] == session_ids[:, None, None]
    recv_src = jnp.sum(jnp.where(lands & coming[None], from_pos[None], 0), axis=(1, 2)) - 1

    live_len = jnp.minimum(end_lengths, event_count)
    keep = jnp.arange(event_count, dtype=jnp.int32)[None, :] < live_len[:, None]
    keep = jnp.broadcast_to(keep.reshape(-1)[:, None], (row_count, share)).astype(jnp.bfloat16)
    send_pos, recv_src, keep = lax.optimization_barrier((send_pos, recv_src, keep))

    def project(c, so_far):
        base = c * steps
        rows_spec = pl.BlockSpec((block, cols_here), lambda i: (base + i, 0))
        rows_shape = jax.ShapeDtypeStruct((row_count, cols_here), jnp.bfloat16)
        return pl.pallas_call(
            functools.partial(project_kernel, n_dp, heads_here, event_count),
            grid=(steps,),
            in_specs=[
                smem_spec(),
                smem_spec(),
                pl.BlockSpec((block, width), lambda i: (base + i, 0)),
                pl.BlockSpec(norm_gains.shape, lambda i: (0, 0)),
                pl.BlockSpec(
                    (block_sessions, heads_here, head_dim, head_dim),
                    lambda i: (base + i, 0, 0, 0),
                ),
            ]
            + [any_spec()] * (n_dp + len(so_far)),
            out_specs=[pl.BlockSpec((block, cols_here), lambda i: (i, 0)), rows_spec, rows_spec],
            out_shape=[
                jax.ShapeDtypeStruct((chunk_rows, cols_here), jnp.bfloat16),
                rows_shape,
                rows_shape,
            ],
            input_output_aliases={5 + n_dp + k: 1 + k for k in range(len(so_far))},
            scratch_shapes=[
                pltpu.VMEM((4, width, cols_here), jnp.bfloat16),
                pltpu.VMEM((heads_here, block, block), jnp.float32),
                pltpu.SemaphoreType.DMA((4, n_dp)),
            ],
            compiler_params=pltpu.CompilerParams(vmem_limit_bytes=VMEM_LIMIT),
            cost_estimate=pl.CostEstimate(
                flops=2 * chunk_rows * width * cols_here * 4,
                bytes_accessed=chunk_rows * width * 4,
                transcendentals=0,
            ),
            name="project",
        )(ids, head_rates, tokens, norm_gains, past_states, *proj_pieces, *so_far)

    gated, kept = [], []
    for c in range(CHUNKS):
        g, *kept = project(c, kept)
        gated.append([g])
    for _ in range(n_tensor - 1):
        for c in range(CHUNKS):
            gated[c].append(lax.ppermute(gated[c][-1], "tensor", ring))

    out_pieces = xor_gather(out_own, "dp")
    ffn_pieces = xor_gather(ffn_weights, "dp")

    packed = pl.pallas_call(
        functools.partial(state_kernel, heads_here, event_count),
        grid=(row_count // block,),
        in_specs=[smem_spec(), smem_spec(), smem_spec()]
        + [pl.BlockSpec((block, cols_here), lambda i: (i, 0))] * 2
        + [pl.BlockSpec((block_sessions, heads_here, head_dim, head_dim), lambda i: (i, 0, 0, 0))],
        out_specs=any_spec(),
        out_shape=jax.ShapeDtypeStruct((slot_count, heads_here, head_dim, head_dim), jnp.bfloat16),
        scratch_shapes=[
            pltpu.VMEM((2, block_sessions, heads_here, head_dim, head_dim), jnp.bfloat16),
            pltpu.SemaphoreType.DMA((2, block_sessions)),
        ],
        compiler_params=pltpu.CompilerParams(vmem_limit_bytes=VMEM_LIMIT),
        cost_estimate=pl.CostEstimate(
            flops=2 * row_count * head_dim * cols_here,
            bytes_accessed=past_states.size * 6,
            transcendentals=0,
        ),
        name="states",
    )(ids, head_rates, send_pos, *kept, past_states)
    received = lax.all_to_all(packed, "dp", split_axis=0, concat_axis=0, tiled=True)

    def feed(c):
        base = c * steps
        row_spec = pl.BlockSpec((block, cols_here), lambda i: (i, 0))
        return pl.pallas_call(
            functools.partial(feed_kernel, n_dp, n_tensor),
            grid=(steps,),
            in_specs=[
                smem_spec(),
                pl.BlockSpec((block, width), lambda i: (base + i, 0)),
                pl.BlockSpec(norm_gains.shape, lambda i: (0, 0)),
            ]
            + [row_spec] * n_tensor
            + [any_spec()] * (2 * n_dp),
            out_specs=[pl.BlockSpec((block, share), lambda i: (i, 0))] * n_tensor,
            out_shape=[jax.ShapeDtypeStruct((chunk_rows, share), jnp.float32)]
            + [jax.ShapeDtypeStruct((chunk_rows, share), jnp.bfloat16)] * (n_tensor - 1),
            scratch_shapes=[
                pltpu.VMEM((n_tensor, width, cols_here), jnp.bfloat16),
                pltpu.VMEM((2, width, units_here), jnp.bfloat16),
                pltpu.VMEM((block, width), jnp.float32),
                pltpu.SemaphoreType.DMA((n_dp,)),
                pltpu.SemaphoreType.DMA((n_dp,)),
                pltpu.SemaphoreType.DMA((n_dp,)),
            ],
            compiler_params=pltpu.CompilerParams(vmem_limit_bytes=VMEM_LIMIT),
            cost_estimate=pl.CostEstimate(
                flops=2 * chunk_rows * width * (width + 2 * units_here),
                bytes_accessed=chunk_rows * width * 8,
                transcendentals=0,
            ),
            name="feed",
        )(ids, tokens, norm_gains, *gated[c], *out_pieces, *ffn_pieces)

    rows_out = []
    for c in range(CHUNKS):
        own, *parts = feed(c)
        terms = []
        for k, part in enumerate(parts):
            pairs = [(i, (i + k + 1) % n_tensor) for i in range(n_tensor)]
            terms.append(lax.ppermute(part, "tensor", pairs))
        total = own
        for term in terms:
            total = total + term.astype(jnp.float32)
        keep_here = keep[c * chunk_rows : (c + 1) * chunk_rows] > 0
        rows_out.append(jnp.where(keep_here, total, 0.0).astype(jnp.bfloat16))
    next_tokens = jnp.concatenate(rows_out)

    per_step = min(8, sessions_here)
    moved_states = pl.pallas_call(
        unpack_kernel,
        grid=(sessions_here // per_step,),
        in_specs=[smem_spec(), any_spec()],
        out_specs=pl.BlockSpec((per_step, heads_here, head_dim, head_dim), lambda i: (i, 0, 0, 0)),
        out_shape=jax.ShapeDtypeStruct(past_states.shape, jnp.float32),
        scratch_shapes=[
            pltpu.VMEM((sessions_here, heads_here, head_dim, head_dim), jnp.bfloat16),
            pltpu.SemaphoreType.DMA((sessions_here,)),
        ],
        compiler_params=pltpu.CompilerParams(vmem_limit_bytes=VMEM_LIMIT),
        cost_estimate=pl.CostEstimate(
            flops=0, bytes_accessed=past_states.size * 6, transcendentals=0
        ),
        name="unpack",
    )(recv_src, received)
    return (next_tokens, moved_states)


def solution(mesh):
    placed = (
        P(("group", "dp"), None),
        P(("group", "dp"), "tensor", None, None),
        P(None, "dp", "tensor"),
        P(None, "dp", "tensor"),
        P(),
        P(),
        P(("group", "dp")),
        P(("group", "dp")),
    )

    return jax.shard_map(
        per_device,
        mesh=mesh,
        in_specs=placed,
        out_specs=(P(("group", "dp"), "tensor"), P(("group", "dp"), "tensor", None, None)),
        check_vma=False,
    )
```

```python
import functools
import jax
import jax.numpy as jnp
from jax import lax
from jax.experimental import pallas as pl
from jax.experimental.pallas import tpu as pltpu
from jax.sharding import PartitionSpec as P

CHUNKS = 2
BLOCK_ROWS = 256


NT = (((1,), (1,)), ((), ()))


def dot_nt(a, b):
    return lax.dot_general(a, b, NT, preferred_element_type=jnp.float32)


def dot_nn(a, b):
    return jnp.dot(a, b, preferred_element_type=jnp.float32)


def rms_scale(values, gain_row):
    meansq = jnp.mean(values * values, axis=-1, keepdims=True)
    return (values * lax.rsqrt(meansq + 1e-05) * gain_row).astype(jnp.bfloat16)


def piece_copies(pieces, dest, sems, me, pick):
    copies = []
    rows = dest.shape[-2] // len(pieces)
    for k, piece in enumerate(pieces):
        start = pl.multiple_of(jnp.bitwise_xor(me, k) * rows, rows)
        copies.append(
            pltpu.make_async_copy(pick(piece), dest.at[..., pl.ds(start, rows), :], sems.at[k])
        )
    return copies


def project_kernel(n_dp, heads, event_count, block, base, *refs):
    ids_ref, rates_ref, tok_ref, gain_ref, past_hbm = refs[:5]
    pieces = refs[5 : 5 + n_dp]
    gated_ref, key_hbm, value_hbm = refs[5 + n_dp : 8 + n_dp]
    w_ref, past_ref, decay_ref, key_ref, value_ref, sems, own_sems = refs[8 + n_dp :]
    depth = w_ref.shape[1] // n_dp
    copies = []
    for m in range(4):
        span = pl.ds(m * depth, depth)
        copies += piece_copies(
            pieces, w_ref.at[m], sems.at[m], ids_ref[0], lambda piece: piece.at[span]
        )
    for copy in copies:
        copy.start()
    past_copy = pltpu.make_async_copy(
        past_hbm.at[pl.ds(base // event_count, past_ref.shape[0])], past_ref, own_sems.at[0]
    )
    past_copy.start()
    out_copies = [
        pltpu.make_async_copy(key_ref, key_hbm, own_sems.at[1]),
        pltpu.make_async_copy(value_ref, value_hbm, own_sems.at[2]),
    ]
    rows = gated_ref.shape[0]
    head_dim = past_ref.shape[3]
    sessions = block // event_count
    key_scale = head_dim ** (-0.5)
    at = lax.broadcasted_iota(jnp.int32, (block, block), 0)
    to = lax.broadcasted_iota(jnp.int32, (block, block), 1)
    allowed = (at // event_count == to // event_count) & (at >= to)
    distance = jnp.maximum(at - to, 0).astype(jnp.float32)
    place = lax.broadcasted_iota(jnp.int32, (block, head_dim), 0) % event_count
    since = (place + 1).astype(jnp.float32)
    factors = []
    for h in range(heads):
        rate = rates_ref[ids_ref[1] * heads + h]
        decay_ref[h] = jnp.where(allowed, jnp.exp(-rate * distance), 0.0) * key_scale
        factors.append(jnp.exp(-rate * since))
    spans = [slice(r, r + block) for r in range(0, rows, block)]
    normed = [
        rms_scale(
            tok_ref[base + span.start : base + span.stop].astype(jnp.float32), gain_ref[0:1, :]
        )
        for span in spans
    ]
    for copy in copies:
        copy.wait()
    past_copy.wait()
    for span, rows_in in zip(spans, normed):
        query = dot_nn(rows_in, w_ref[0]).astype(jnp.bfloat16)
        keys = dot_nn(rows_in, w_ref[1]).astype(jnp.bfloat16)
        key_ref[span] = keys
        values = dot_nn(rows_in, w_ref[2]).astype(jnp.bfloat16)
        value_ref[span] = values
        gate = dot_nn(rows_in, w_ref[3])
        first_session = span.start // event_count
        for h in range(heads):
            cols = slice(h * head_dim, (h + 1) * head_dim)
            qh, kh, vh = query[:, cols], keys[:, cols], values[:, cols]
            mix = (dot_nt(qh, kh) * decay_ref[h]).astype(jnp.bfloat16)
            intra = dot_nn(mix, vh)
            parts = []
            for s in range(sessions):
                parts.append(
                    dot_nn(
                        qh[s * event_count : (s + 1) * event_count],
                        past_ref[first_session + s, h].astype(jnp.bfloat16),
                    )
                )
            retained = intra + jnp.concatenate(parts, axis=0) * factors[h]
            centred = retained - jnp.mean(retained, axis=-1, keepdims=True)
            row_var = jnp.mean(centred * centred, axis=-1, keepdims=True)
            normalised = centred * lax.rsqrt(row_var + 1e-05)
            gated_ref[span, cols] = (jax.nn.silu(gate[:, cols]) * normalised).astype(jnp.bfloat16)
    for copy in out_copies:
        copy.start()
    for copy in out_copies:
        copy.wait()


def state_kernel(chunks, heads, event_count, *refs):
    ids_ref, rates_ref, pos_ref, past_hbm = refs[:4]
    sources = refs[4 : 4 + 2 * chunks]
    out_ref, buf_ref, past_ref, kv_ref, sems, past_sems, kv_sems = refs[4 + 2 * chunks :]
    kv_copies = [
        pltpu.make_async_copy(source, kv_ref.at[k], kv_sems.at[k])
        for k, source in enumerate(sources)
    ]
    for copy in kv_copies:
        copy.start()
    sessions, _, head_dim, _ = past_ref.shape
    groups = past_sems.shape[0]
    group = sessions // groups
    past_copies = [
        pltpu.make_async_copy(
            past_hbm.at[pl.ds(k * group, group)],
            past_ref.at[pl.ds(k * group, group)],
            past_sems.at[k],
        )
        for k in range(groups)
    ]
    for copy in past_copies:
        copy.start()
    rows = kv_ref.shape[1]
    key_scale = head_dim ** (-0.5)

    def copy_of(session):
        return pltpu.make_async_copy(
            buf_ref.at[session], out_ref.at[pos_ref[session]], sems.at[session]
        )

    place = lax.broadcasted_iota(jnp.int32, (rows, head_dim), 0) % event_count
    left = (event_count - 1 - place).astype(jnp.float32)
    factors, carries = [], []
    for h in range(heads):
        rate = rates_ref[ids_ref[1] * heads + h]
        factors.append(jnp.exp(-rate * left) * key_scale)
        carries.append(jnp.exp(jnp.full((head_dim, head_dim), -rate * event_count, jnp.float32)))
    for c in range(chunks):
        kv_copies[c].wait()
        kv_copies[chunks + c].wait()
        weighted = []
        for h in range(heads):
            cols = slice(h * head_dim, (h + 1) * head_dim)
            weighted.append(
                (kv_ref[c, :, cols].astype(jnp.float32) * factors[h]).astype(jnp.bfloat16)
            )
        for s in range(rows // event_count):
            session = c * (rows // event_count) + s
            if session % group == 0:
                past_copies[session // group].wait()
            span = slice(s * event_count, (s + 1) * event_count)
            for h in range(heads):
                cols = slice(h * head_dim, (h + 1) * head_dim)
                grown = lax.dot_general(
                    weighted[h][span],
                    kv_ref[chunks + c, span, cols],
                    (((0,), (0,)), ((), ())),
                    preferred_element_type=jnp.float32,
                )
                buf_ref[session, h] = (carries[h] * past_ref[session, h] + grown).astype(
                    jnp.bfloat16
                )

            @pl.when(pos_ref[session] >= 0)
            def _():
                copy_of(session).start()

    for session in range(sessions):

        @pl.when(pos_ref[session] >= 0)
        def _():
            copy_of(session).wait()


def unpack_kernel(src_ref, recv_ref, out_ref, buf_ref, sems):
    per_step = out_ref.shape[0]
    step = pl.program_id(0)

    def copy_of(slot):
        return pltpu.make_async_copy(
            recv_ref.at[jnp.maximum(src_ref[slot], 0)], buf_ref.at[slot], sems.at[slot]
        )

    @pl.when(step == 0)
    def _():
        for slot in range(buf_ref.shape[0]):

            @pl.when(src_ref[slot] >= 0)
            def _():
                copy_of(slot).start()

    for i in range(per_step):
        slot = step * per_step + i

        @pl.when(src_ref[slot] >= 0)
        def _():
            copy_of(slot).wait()
            out_ref[i] = buf_ref[slot].astype(jnp.float32)

        @pl.when(src_ref[slot] < 0)
        def _():
            out_ref[i] = jnp.zeros(out_ref.shape[1:], jnp.float32)


def feed_kernel(n_dp, n_tensor, block, base, *refs):
    ids_ref, tok_ref, gain_ref = refs[:3]
    gated = refs[3 : 3 + n_tensor]
    at = 3 + n_tensor
    out_pieces = refs[at : at + n_dp]
    ffn_pieces = refs[at + n_dp : at + 2 * n_dp]
    at += 2 * n_dp
    own_ref = refs[at]
    part_refs = refs[at + 1 : at + n_tensor]
    wo_ref, up_ref, down_ref, res_ref, sems = refs[at + n_tensor :]
    me = ids_ref[0]
    out_copies = piece_copies(out_pieces, wo_ref, sems.at[0], me, lambda piece: piece)
    up_copies = piece_copies(ffn_pieces, up_ref, sems.at[1], me, lambda piece: piece.at[0])
    down_copies = piece_copies(ffn_pieces, down_ref, sems.at[2], me, lambda piece: piece.at[1])
    for copy in out_copies + up_copies + down_copies:
        copy.start()
    for copy in out_copies:
        copy.wait()
    rows, width = own_ref.shape
    for r in range(0, rows, block):
        span = slice(r, r + block)
        attended = dot_nt(gated[0][span], wo_ref[ids_ref[2]])
        for k in range(1, n_tensor):
            attended += dot_nt(gated[k][span], wo_ref[ids_ref[2 + k]])
        residual = tok_ref[base + r : base + r + block].astype(jnp.float32) + attended
        res_ref[span] = residual
        hidden = rms_scale(residual, gain_ref[1:2, :])
        if r == 0:
            for copy in up_copies:
                copy.wait()
        activated = jax.nn.gelu(dot_nn(hidden, up_ref[...]), approximate=True)
        activated = activated.astype(jnp.bfloat16)
        if r == 0:
            for copy in down_copies:
                copy.wait()

        def term(k):
            start = pl.multiple_of(ids_ref[2 + k] * width, width)
            return dot_nt(activated, down_ref[pl.ds(start, width), :])

        for k in range(1, n_tensor):
            part_refs[k - 1][span] = term(k).astype(jnp.bfloat16)
        mine = pl.ds(pl.multiple_of(ids_ref[1] * width, width), width)
        own_ref[span] = res_ref[span, mine] + term(0)


def add_kernel(a_ref, b_ref, out_ref):
    total = a_ref[...].astype(jnp.float32) + b_ref[...].astype(jnp.float32)
    out_ref[...] = total.astype(jnp.bfloat16)


def last_kernel(chunks, event_count, *refs):
    lengths_ref = refs[0]
    owns = refs[1 : 1 + chunks]
    terms = refs[1 + chunks : 1 + 2 * chunks]
    out_ref = refs[-1]
    rows, width = owns[0].shape
    place = lax.broadcasted_iota(jnp.int32, (event_count, width), 0)
    for c in range(chunks):
        for s in range(rows // event_count):
            span = slice(s * event_count, (s + 1) * event_count)
            total = owns[c][span] + terms[c][span].astype(jnp.float32)
            session = c * (rows // event_count) + s
            keep = place < lengths_ref[session]
            out_ref[session * event_count : (session + 1) * event_count] = jnp.where(
                keep, total, 0.0
            ).astype(jnp.bfloat16)


def xor_gather(value, axis):
    pieces = [value]
    size = lax.axis_size(axis)
    bit = size // 2
    order = [0]
    while bit:
        pairs = [(i, i ^ bit) for i in range(size)]
        arrived = []
        for piece in pieces:
            arrived.append(lax.ppermute(piece, axis, pairs))
        pieces = pieces + arrived
        order = order + [k ^ bit for k in order]
        bit //= 2
    return [pieces[order.index(k)] for k in range(size)]


def ring_order(size):
    return list(range(0, size, 2)) + list(range(1, size, 2))[::-1]


def ring_pairs(size):
    order = ring_order(size)
    return [(order[i], order[(i + 1) % size]) for i in range(size)]


def ring_sources(size):
    order = ring_order(size)
    return [[order[(order.index(at) - k) % size] for k in range(size)] for at in range(size)]


def any_spec():
    return pl.BlockSpec(memory_space=pl.ANY)


def smem_spec():
    return pl.BlockSpec(memory_space=pltpu.SMEM)


def hbm_spec():
    return pl.BlockSpec(memory_space=pltpu.HBM)


def in_hbm(arrays):
    return [pltpu.with_memory_space_constraint(array, pltpu.HBM) for array in arrays]


def vmem_spec():
    return pl.BlockSpec(memory_space=pltpu.VMEM)


def kernel_call(kernel, in_specs, out_specs, out_shape, scratch, flops, limit_mib=24):
    return pl.pallas_call(
        kernel,
        in_specs=in_specs,
        out_specs=out_specs,
        out_shape=out_shape,
        scratch_shapes=scratch,
        compiler_params=pltpu.CompilerParams(vmem_limit_bytes=limit_mib * 1024 * 1024),
        cost_estimate=pl.CostEstimate(
            flops=flops, bytes_accessed=4 * 1024 * 1024, transcendentals=0
        ),
    )


def per_device(
    tokens, past_states, attn_weights, ffn_weights, norm_gains, head_rates, end_lengths, new_slot
):
    sessions_here = end_lengths.shape[0]
    row_count, width = tokens.shape
    event_count = row_count // sessions_here
    heads_here, head_dim = past_states.shape[1], past_states.shape[3]
    cols_here = heads_here * head_dim
    units_here = ffn_weights.shape[2]
    n_dp, n_tensor = lax.axis_size("dp"), lax.axis_size("tensor")
    dp_at, tensor_at = lax.axis_index("dp"), lax.axis_index("tensor")
    share = width // n_tensor
    pair_cap = max(2, 2 * sessions_here // n_dp)
    slot_count = n_dp * pair_cap
    chunk_rows = row_count // CHUNKS
    block = min(BLOCK_ROWS, chunk_rows)
    ring = ring_pairs(n_tensor)
    bf16, f32 = jnp.bfloat16, jnp.float32
    shape_of = jax.ShapeDtypeStruct

    survive = end_lengths > event_count
    target_dev = new_slot // sessions_here
    session_ids = jnp.arange(sessions_here, dtype=jnp.int32)
    proj_rows = attn_weights.shape[1]
    notes = jnp.stack([jnp.where(survive, target_dev, -1), new_slot % sessions_here])
    notes = jnp.pad(notes.astype(bf16), ((0, 6), (0, cols_here - sessions_here)))
    proj_own = jnp.concatenate([attn_weights[:4].reshape(4 * proj_rows, cols_here), notes])
    proj_pieces = xor_gather(proj_own, "dp")
    out_own = lax.all_to_all(
        jnp.broadcast_to(attn_weights[4:], (n_tensor, proj_rows, cols_here)),
        "tensor",
        split_axis=0,
        concat_axis=0,
        tiled=True,
    )
    sources = jnp.array(ring_sources(n_tensor), jnp.int32)[tensor_at]
    ids = jnp.concatenate([jnp.stack([dp_at, tensor_at]).astype(jnp.int32), sources])

    meta = jnp.stack([piece[4 * proj_rows :, :sessions_here] for piece in proj_pieces])
    meta = meta.astype(jnp.int32)
    from_dev = jnp.bitwise_xor(dp_at, jnp.arange(n_dp, dtype=jnp.int32))
    earlier = (
        (target_dev[None, :] == target_dev[:, None])
        & survive[None, :]
        & (session_ids[None, :] < session_ids[:, None])
    )
    pair_rank = jnp.sum(earlier.astype(jnp.int32), axis=1)
    send_pos = jnp.where(survive, target_dev * pair_cap + pair_rank, -1)
    coming = meta[:, 0] == dp_at
    ahead = coming[:, None, :] & (session_ids[None, None, :] < session_ids[None, :, None])
    rank_all = jnp.sum(ahead.astype(jnp.int32), axis=2)
    from_pos = from_dev[:, None] * pair_cap + rank_all + 1
    lands = meta[:, 1][None] == session_ids[:, None, None]
    recv_src = jnp.sum(jnp.where(lands & coming[None], from_pos[None], 0), axis=(1, 2)) - 1
    send_pos, recv_src = lax.optimization_barrier((send_pos, recv_src))

    rows_shape = shape_of((chunk_rows, cols_here), bf16)
    decay_shape = pltpu.VMEM((heads_here, block, block), f32)
    chunk_sessions = chunk_rows // event_count
    gated, keys, values = [], [], []
    for c in range(CHUNKS):
        g, k, v = kernel_call(
            functools.partial(project_kernel, n_dp, heads_here, event_count, block, c * chunk_rows),
            [smem_spec()] * 2 + [vmem_spec()] * 2 + [hbm_spec()] + [any_spec()] * n_dp,
            [vmem_spec()] + [hbm_spec()] * 2,
            [rows_shape] + [pltpu.HBM((chunk_rows, cols_here), bf16)] * 2,
            [
                pltpu.VMEM((4, width, cols_here), bf16),
                pltpu.VMEM((chunk_sessions, heads_here, head_dim, head_dim), f32),
                decay_shape,
                pltpu.VMEM((chunk_rows, cols_here), bf16),
                pltpu.VMEM((chunk_rows, cols_here), bf16),
                pltpu.SemaphoreType.DMA((4, n_dp)),
                pltpu.SemaphoreType.DMA((3,)),
            ],
            2 * chunk_rows * width * cols_here * 4,
        )(ids, head_rates, tokens, norm_gains, *in_hbm([past_states]), *proj_pieces)
        gated.append([g])
        keys.append(k)
        values.append(v)
    for _ in range(n_tensor - 1):
        for c in range(CHUNKS):
            gated[c].append(lax.ppermute(gated[c][-1], "tensor", ring))

    out_pieces = xor_gather(out_own, "dp")
    ffn_pieces = xor_gather(ffn_weights, "dp")
    packed = kernel_call(
        functools.partial(state_kernel, CHUNKS, heads_here, event_count),
        [smem_spec()] * 3 + [hbm_spec()] * (1 + 2 * CHUNKS),
        hbm_spec(),
        pltpu.HBM((slot_count, heads_here, head_dim, head_dim), bf16),
        [
            pltpu.VMEM((sessions_here, heads_here, head_dim, head_dim), bf16),
            pltpu.VMEM((sessions_here, heads_here, head_dim, head_dim), f32),
            pltpu.VMEM((2 * CHUNKS, chunk_rows, cols_here), bf16),
            pltpu.SemaphoreType.DMA((sessions_here,)),
            pltpu.SemaphoreType.DMA((4,)),
            pltpu.SemaphoreType.DMA((2 * CHUNKS,)),
        ],
        2 * row_count * head_dim * cols_here,
    )(ids, head_rates, send_pos, *in_hbm([past_states, *keys, *values]))
    received = lax.all_to_all(packed, "dp", split_axis=0, concat_axis=0, tiled=True)

    owns, parts, sums = [], [], []
    for c in range(CHUNKS):
        own, *part = kernel_call(
            functools.partial(feed_kernel, n_dp, n_tensor, block, c * chunk_rows),
            [smem_spec()] + [vmem_spec()] * (2 + n_tensor) + [hbm_spec()] * (2 * n_dp),
            [vmem_spec()] * n_tensor,
            [shape_of((chunk_rows, share), f32)]
            + [shape_of((chunk_rows, share), bf16)] * (n_tensor - 1),
            [
                pltpu.VMEM((n_tensor, width, cols_here), bf16),
                pltpu.VMEM((width, units_here), bf16),
                pltpu.VMEM((width, units_here), bf16),
                pltpu.VMEM((chunk_rows, width), f32),
                pltpu.SemaphoreType.DMA((3, n_dp)),
            ],
            2 * chunk_rows * width * (width + 2 * units_here),
        )(ids, tokens, norm_gains, *gated[c], *in_hbm(out_pieces + ffn_pieces))
        owns.append(own)
        parts.append(part)
        sums.append(None)
    for hop in range(n_tensor - 1):
        for c in range(CHUNKS):
            mine = parts[c][hop]
            if hop:
                mine = kernel_call(
                    add_kernel,
                    [vmem_spec()] * 2,
                    vmem_spec(),
                    shape_of((chunk_rows, share), bf16),
                    [],
                    0,
                    limit_mib=4,
                )(sums[c], mine)
            sums[c] = lax.ppermute(mine, "tensor", ring)

    next_tokens = kernel_call(
        functools.partial(last_kernel, CHUNKS, event_count),
        [smem_spec()] + [vmem_spec()] * (2 * CHUNKS),
        vmem_spec(),
        shape_of((row_count, share), bf16),
        [],
        0,
        limit_mib=8,
    )(end_lengths, *owns, *sums)

    per_step = min(8, sessions_here)
    moved_states = pl.pallas_call(
        unpack_kernel,
        grid=(sessions_here // per_step,),
        in_specs=[smem_spec(), any_spec()],
        out_specs=pl.BlockSpec((per_step, heads_here, head_dim, head_dim), lambda i: (i, 0, 0, 0)),
        out_shape=shape_of(past_states.shape, f32),
        scratch_shapes=[
            pltpu.VMEM((sessions_here, heads_here, head_dim, head_dim), bf16),
            pltpu.SemaphoreType.DMA((sessions_here,)),
        ],
        compiler_params=pltpu.CompilerParams(vmem_limit_bytes=16 * 1024 * 1024),
        cost_estimate=pl.CostEstimate(
            flops=0, bytes_accessed=past_states.size * 6, transcendentals=0
        ),
        name="unpack",
    )(recv_src, received)
    return (next_tokens, moved_states)


def solution(mesh):
    placed = (
        P(("group", "dp"), None),
        P(("group", "dp"), "tensor", None, None),
        P(None, "dp", "tensor"),
        P(None, "dp", "tensor"),
        P(),
        P(),
        P(("group", "dp")),
        P(("group", "dp")),
    )

    return jax.shard_map(
        per_device,
        mesh=mesh,
        in_specs=placed,
        out_specs=(P(("group", "dp"), "tensor"), P(("group", "dp"), "tensor", None, None)),
        check_vma=False,
    )
```

```python
import functools
import jax
import jax.numpy as jnp
from jax import lax
from jax.experimental import pallas as pl
from jax.experimental.pallas import tpu as pltpu
from jax.sharding import PartitionSpec as P

CHUNKS = 2
BLOCK_ROWS = 256


NT = (((1,), (1,)), ((), ()))


def dot_nt(a, b):
    return lax.dot_general(a, b, NT, preferred_element_type=jnp.float32)


def dot_nn(a, b):
    return jnp.dot(a, b, preferred_element_type=jnp.float32)


def rms_scale(values, gain_row):
    meansq = jnp.mean(values * values, axis=-1, keepdims=True)
    return (values * lax.rsqrt(meansq + 1e-05) * gain_row).astype(jnp.bfloat16)


def piece_copies(pieces, dest, sems, me, pick):
    copies = []
    rows = dest.shape[-2] // len(pieces)
    for k, piece in enumerate(pieces):
        start = pl.multiple_of(jnp.bitwise_xor(me, k) * rows, rows)
        copies.append(
            pltpu.make_async_copy(pick(piece), dest.at[..., pl.ds(start, rows), :], sems.at[k])
        )
    return copies


def project_kernel(n_dp, heads, event_count, block, base, *refs):
    ids_ref, small_ref, tok_ref, past_hbm = refs[:4]
    pieces = refs[4 : 4 + n_dp]
    gated_ref, key_hbm, value_hbm = refs[4 + n_dp : 7 + n_dp]
    normed_ref, past_ref, decay_ref, key_ref, value_ref, w_ref, sems = refs[7 + n_dp :]
    past_copy = pltpu.make_async_copy(
        past_hbm.at[pl.ds(base // event_count, past_ref.shape[0])], past_ref, sems.at[0]
    )
    past_copy.start()
    out_copies = [
        pltpu.make_async_copy(key_ref, key_hbm, sems.at[1]),
        pltpu.make_async_copy(value_ref, value_hbm, sems.at[2]),
    ]
    rows, _ = gated_ref.shape
    head_dim = past_ref.shape[3]
    sessions = block // event_count
    key_scale = head_dim ** (-0.5)
    depth = tok_ref.shape[1] // n_dp
    starts = [pl.multiple_of(jnp.bitwise_xor(ids_ref[0], k) * depth, depth) for k in range(n_dp)]
    split = depth % 128 == 0
    if not split:
        for m in range(4):
            for k in range(n_dp):
                w_ref[m, pl.ds(starts[k], depth), :] = pieces[k][m * depth : (m + 1) * depth]
    at = lax.broadcasted_iota(jnp.int32, (block, block), 0)
    to = lax.broadcasted_iota(jnp.int32, (block, block), 1)
    allowed = (at // event_count == to // event_count) & (at >= to)
    distance = jnp.maximum(at - to, 0).astype(jnp.float32)
    place = lax.broadcasted_iota(jnp.int32, (block, head_dim), 0) % event_count
    since = (place + 1).astype(jnp.float32)
    factors = []
    for h in range(heads):
        rate = small_ref[2 + h : 3 + h, :]
        decay_ref[h] = jnp.where(allowed, jnp.exp(-rate[:, :block] * distance), 0.0) * key_scale
        factors.append(jnp.exp(-rate[:, :head_dim] * since))

    def product(span, m):
        if not split:
            return dot_nn(normed_ref[span], w_ref[m])
        total = None
        for k in range(n_dp):
            term = dot_nn(
                normed_ref[span, pl.ds(starts[k], depth)], pieces[k][m * depth : (m + 1) * depth]
            )
            total = term if total is None else total + term
        return total

    for r in range(0, rows, block):
        span = slice(r, r + block)
        normed_ref[span] = rms_scale(
            tok_ref[base + r : base + r + block].astype(jnp.float32), small_ref[0:1, :]
        )
        query = product(span, 0).astype(jnp.bfloat16)
        keys = product(span, 1).astype(jnp.bfloat16)
        key_ref[span] = keys
        values = product(span, 2).astype(jnp.bfloat16)
        value_ref[span] = values
        gate = product(span, 3)
        if r == 0:
            past_copy.wait()
        if r + block == rows:
            for copy in out_copies:
                copy.start()
        first_session = r // event_count
        for h in range(heads):
            cols = slice(h * head_dim, (h + 1) * head_dim)
            qh, kh, vh = query[:, cols], keys[:, cols], values[:, cols]
            mix = (dot_nt(qh, kh) * decay_ref[h]).astype(jnp.bfloat16)
            intra = dot_nn(mix, vh)
            parts = []
            for s in range(sessions):
                parts.append(
                    dot_nn(
                        qh[s * event_count : (s + 1) * event_count],
                        past_ref[first_session + s, h].astype(jnp.bfloat16),
                    )
                )
            retained = intra + jnp.concatenate(parts, axis=0) * factors[h]
            centred = retained - jnp.mean(retained, axis=-1, keepdims=True)
            row_var = jnp.mean(centred * centred, axis=-1, keepdims=True)
            normalised = centred * lax.rsqrt(row_var + 1e-05)
            gated_ref[span, cols] = (jax.nn.silu(gate[:, cols]) * normalised).astype(jnp.bfloat16)
    for copy in out_copies:
        copy.wait()


def state_kernel(chunks, heads, event_count, *refs):
    small_ref, pos_ref, past_hbm = refs[:3]
    sources = refs[3 : 3 + 2 * chunks]
    out_ref, buf_ref, past_ref, kv_ref, sems, past_sems, kv_sems = refs[3 + 2 * chunks :]
    kv_copies = [
        pltpu.make_async_copy(source, kv_ref.at[k], kv_sems.at[k])
        for k, source in enumerate(sources)
    ]
    for copy in kv_copies:
        copy.start()
    sessions, _, head_dim, _ = past_ref.shape
    groups = past_sems.shape[0]
    group = sessions // groups
    past_copies = [
        pltpu.make_async_copy(
            past_hbm.at[pl.ds(k * group, group)],
            past_ref.at[pl.ds(k * group, group)],
            past_sems.at[k],
        )
        for k in range(groups)
    ]
    for copy in past_copies:
        copy.start()
    rows = kv_ref.shape[1]
    key_scale = head_dim ** (-0.5)

    def copy_of(session):
        return pltpu.make_async_copy(
            buf_ref.at[session], out_ref.at[pos_ref[session]], sems.at[session]
        )

    place = lax.broadcasted_iota(jnp.int32, (rows, head_dim), 0) % event_count
    left = (event_count - 1 - place).astype(jnp.float32)
    factors, carries = [], []
    for h in range(heads):
        rate = small_ref[2 + h : 3 + h, :head_dim]
        factors.append(jnp.exp(-rate * left) * key_scale)
        carries.append(jnp.exp(-rate * event_count))
    for c in range(chunks):
        kv_copies[c].wait()
        kv_copies[chunks + c].wait()
        weighted = []
        for h in range(heads):
            cols = slice(h * head_dim, (h + 1) * head_dim)
            weighted.append(
                (kv_ref[c, :, cols].astype(jnp.float32) * factors[h]).astype(jnp.bfloat16)
            )
        for s in range(rows // event_count):
            session = c * (rows // event_count) + s
            if session % group == 0:
                past_copies[session // group].wait()
            span = slice(s * event_count, (s + 1) * event_count)
            for h in range(heads):
                cols = slice(h * head_dim, (h + 1) * head_dim)
                grown = lax.dot_general(
                    weighted[h][span],
                    kv_ref[chunks + c, span, cols],
                    (((0,), (0,)), ((), ())),
                    preferred_element_type=jnp.float32,
                )
                buf_ref[session, h] = (carries[h] * past_ref[session, h] + grown).astype(
                    jnp.bfloat16
                )

            @pl.when(pos_ref[session] >= 0)
            def _():
                copy_of(session).start()

    for session in range(sessions):

        @pl.when(pos_ref[session] >= 0)
        def _():
            copy_of(session).wait()


def unpack_kernel(src_ref, recv_ref, out_ref, buf_ref, sems):
    per_step = out_ref.shape[0]
    step = pl.program_id(0)

    def copy_of(slot):
        return pltpu.make_async_copy(
            recv_ref.at[jnp.maximum(src_ref[slot], 0)], buf_ref.at[slot], sems.at[slot]
        )

    @pl.when(step == 0)
    def _():
        for slot in range(buf_ref.shape[0]):

            @pl.when(src_ref[slot] >= 0)
            def _():
                copy_of(slot).start()

    for i in range(per_step):
        slot = step * per_step + i

        @pl.when(src_ref[slot] >= 0)
        def _():
            copy_of(slot).wait()
            out_ref[i] = buf_ref[slot].astype(jnp.float32)

        @pl.when(src_ref[slot] < 0)
        def _():
            out_ref[i] = jnp.zeros(out_ref.shape[1:], jnp.float32)


def feed_kernel(n_dp, n_tensor, block, base, *refs):
    ids_ref, small_ref, tok_ref = refs[:3]
    gated_hbm = refs[3 : 3 + n_tensor]
    at = 3 + n_tensor
    out_pieces = refs[at : at + n_dp]
    ffn_pieces = refs[at + n_dp : at + 2 * n_dp]
    at += 2 * n_dp
    own_hbm, *part_hbm = refs[at : at + n_tensor]
    wo_ref, up_ref, down_ref, res_ref, gated, own_ref, part_ref = refs[at + n_tensor : -3]
    sems, gated_sems, done_sems = refs[-3:]
    rows, width = own_ref.shape
    me = ids_ref[0]
    out_copies = piece_copies(out_pieces, wo_ref, sems.at[0], me, lambda piece: piece)
    up_copies = piece_copies(ffn_pieces, up_ref, sems.at[1], me, lambda piece: piece.at[0])
    down_copies = piece_copies(ffn_pieces, down_ref, sems.at[2], me, lambda piece: piece.at[1])
    gated_copies = [
        pltpu.make_async_copy(source, gated.at[k], gated_sems.at[k])
        for k, source in enumerate(gated_hbm)
    ]
    for copy in gated_copies + out_copies + up_copies + down_copies:
        copy.start()
    for copy in gated_copies + out_copies:
        copy.wait()
    done_copies = [pltpu.make_async_copy(own_ref, own_hbm, done_sems.at[0])]
    for k in range(1, n_tensor):
        done_copies.append(
            pltpu.make_async_copy(part_ref.at[k - 1], part_hbm[k - 1], done_sems.at[k])
        )
    for r in range(0, rows, block):
        span = slice(r, r + block)
        attended = dot_nt(gated[0, span], wo_ref[ids_ref[2]])
        for k in range(1, n_tensor):
            attended += dot_nt(gated[k, span], wo_ref[ids_ref[2 + k]])
        residual = tok_ref[base + r : base + r + block].astype(jnp.float32) + attended
        res_ref[span] = residual
        hidden = rms_scale(residual, small_ref[1:2, :])
        if r == 0:
            for copy in up_copies:
                copy.wait()
        activated = jax.nn.gelu(dot_nn(hidden, up_ref[...]), approximate=True)
        activated = activated.astype(jnp.bfloat16)
        if r == 0:
            for copy in down_copies:
                copy.wait()
        final = r + block == rows

        def term(k):
            start = pl.multiple_of(ids_ref[2 + k] * width, width)
            return dot_nt(activated, down_ref[pl.ds(start, width), :])

        for k in range(1, n_tensor):
            part_ref[k - 1, span] = term(k).astype(jnp.bfloat16)
            if final:
                done_copies[k].start()
        mine = pl.ds(pl.multiple_of(ids_ref[1] * width, width), width)
        own_ref[span] = res_ref[span, mine] + term(0)
        if final:
            done_copies[0].start()
    for copy in done_copies:
        copy.wait()


def add_kernel(a_ref, b_ref, out_ref):
    total = a_ref[...].astype(jnp.float32) + b_ref[...].astype(jnp.float32)
    out_ref[...] = total.astype(jnp.bfloat16)


def last_kernel(event_count, base, *refs):
    lengths_ref, own_ref, term_ref = refs[:3]
    out_hbm, out_ref, sem = refs[-3:]
    rows, width = own_ref.shape
    place = lax.broadcasted_iota(jnp.int32, (event_count, width), 0)
    for s in range(rows // event_count):
        span = slice(s * event_count, (s + 1) * event_count)
        total = own_ref[span] + term_ref[span].astype(jnp.float32)
        keep = place < lengths_ref[base // event_count + s]
        out_ref[span] = jnp.where(keep, total, 0.0).astype(jnp.bfloat16)
    copy = pltpu.make_async_copy(out_ref, out_hbm.at[pl.ds(base, rows)], sem)
    copy.start()
    copy.wait()


def xor_gather(value, axis):
    pieces = [value]
    size = lax.axis_size(axis)
    bit = size // 2
    order = [0]
    while bit:
        pairs = [(i, i ^ bit) for i in range(size)]
        arrived = []
        for piece in pieces:
            arrived.append(lax.ppermute(piece, axis, pairs))
        pieces = pieces + arrived
        order = order + [k ^ bit for k in order]
        bit //= 2
    return [pieces[order.index(k)] for k in range(size)]


def ring_order(size):
    return list(range(0, size, 2)) + list(range(1, size, 2))[::-1]


def ring_pairs(size):
    order = ring_order(size)
    return [(order[i], order[(i + 1) % size]) for i in range(size)]


def ring_sources(size):
    order = ring_order(size)
    return [[order[(order.index(at) - k) % size] for k in range(size)] for at in range(size)]


def any_spec():
    return pl.BlockSpec(memory_space=pl.ANY)


def smem_spec():
    return pl.BlockSpec(memory_space=pltpu.SMEM)


def hbm_spec():
    return pl.BlockSpec(memory_space=pltpu.HBM)


def in_hbm(arrays):
    return [pltpu.with_memory_space_constraint(array, pltpu.HBM) for array in arrays]


def vmem_spec():
    return pl.BlockSpec(memory_space=pltpu.VMEM)


def kernel_call(kernel, in_specs, out_specs, out_shape, scratch, flops, limit_mib=24):
    return pl.pallas_call(
        kernel,
        in_specs=in_specs,
        out_specs=out_specs,
        out_shape=out_shape,
        scratch_shapes=scratch,
        compiler_params=pltpu.CompilerParams(vmem_limit_bytes=limit_mib * 1024 * 1024),
        cost_estimate=pl.CostEstimate(
            flops=flops, bytes_accessed=4 * 1024 * 1024, transcendentals=0
        ),
    )


def per_device(
    tokens, past_states, attn_weights, ffn_weights, norm_gains, head_rates, end_lengths, new_slot
):
    sessions_here = end_lengths.shape[0]
    row_count, width = tokens.shape
    event_count = row_count // sessions_here
    heads_here, head_dim = past_states.shape[1], past_states.shape[3]
    cols_here = heads_here * head_dim
    units_here = ffn_weights.shape[2]
    n_dp, n_tensor = lax.axis_size("dp"), lax.axis_size("tensor")
    dp_at, tensor_at = lax.axis_index("dp"), lax.axis_index("tensor")
    share = width // n_tensor
    pair_cap = max(2, 2 * sessions_here // n_dp)
    slot_count = n_dp * pair_cap
    chunk_rows = row_count // CHUNKS
    block = min(BLOCK_ROWS, chunk_rows)
    ring = ring_pairs(n_tensor)
    bf16, f32 = jnp.bfloat16, jnp.float32
    shape_of = jax.ShapeDtypeStruct

    survive = end_lengths > event_count
    target_dev = new_slot // sessions_here
    session_ids = jnp.arange(sessions_here, dtype=jnp.int32)
    proj_rows = attn_weights.shape[1]
    notes = jnp.stack([jnp.where(survive, target_dev, -1), new_slot % sessions_here])
    notes = jnp.pad(notes.astype(bf16), ((0, 6), (0, cols_here - sessions_here)))
    proj_own = jnp.concatenate([attn_weights[:4].reshape(4 * proj_rows, cols_here), notes])
    proj_pieces = xor_gather(proj_own, "dp")
    out_own = lax.all_to_all(
        jnp.broadcast_to(attn_weights[4:], (n_tensor, proj_rows, cols_here)),
        "tensor",
        split_axis=0,
        concat_axis=0,
        tiled=True,
    )
    sources = jnp.array(ring_sources(n_tensor), jnp.int32)[tensor_at]
    ids = jnp.concatenate([jnp.stack([dp_at, tensor_at]).astype(jnp.int32), sources])

    meta = jnp.stack([piece[4 * proj_rows :, :sessions_here] for piece in proj_pieces])
    meta = meta.astype(jnp.int32)
    from_dev = jnp.bitwise_xor(dp_at, jnp.arange(n_dp, dtype=jnp.int32))
    earlier = (
        (target_dev[None, :] == target_dev[:, None])
        & survive[None, :]
        & (session_ids[None, :] < session_ids[:, None])
    )
    pair_rank = jnp.sum(earlier.astype(jnp.int32), axis=1)
    send_pos = jnp.where(survive, target_dev * pair_cap + pair_rank, -1)
    coming = meta[:, 0] == dp_at
    ahead = coming[:, None, :] & (session_ids[None, None, :] < session_ids[None, :, None])
    rank_all = jnp.sum(ahead.astype(jnp.int32), axis=2)
    from_pos = from_dev[:, None] * pair_cap + rank_all + 1
    lands = meta[:, 1][None] == session_ids[:, None, None]
    recv_src = jnp.sum(jnp.where(lands & coming[None], from_pos[None], 0), axis=(1, 2)) - 1
    send_pos, recv_src = lax.optimization_barrier((send_pos, recv_src))

    rows_shape = shape_of((chunk_rows, cols_here), bf16)
    decay_shape = pltpu.VMEM((heads_here, block, block), f32)
    head_decay = lax.dynamic_slice_in_dim(head_rates, tensor_at * heads_here, heads_here)
    small = jnp.concatenate(
        [norm_gains, jnp.broadcast_to(head_decay[:, None], (heads_here, width))]
    )
    chunk_sessions = chunk_rows // event_count
    gated, keys, values = [], [], []
    for c in range(CHUNKS):
        g, k, v = kernel_call(
            functools.partial(project_kernel, n_dp, heads_here, event_count, block, c * chunk_rows),
            [smem_spec()] + [vmem_spec()] * 2 + [hbm_spec()] + [vmem_spec()] * n_dp,
            [vmem_spec()] + [hbm_spec()] * 2,
            [rows_shape] + [pltpu.HBM((chunk_rows, cols_here), bf16)] * 2,
            [
                pltpu.VMEM((chunk_rows, width), bf16),
                pltpu.VMEM((chunk_sessions, heads_here, head_dim, head_dim), f32),
                decay_shape,
                pltpu.VMEM((chunk_rows, cols_here), bf16),
                pltpu.VMEM((chunk_rows, cols_here), bf16),
                pltpu.VMEM((4, width, cols_here), bf16),
                pltpu.SemaphoreType.DMA((3,)),
            ],
            2 * chunk_rows * width * cols_here * 4,
        )(ids, small, tokens, *in_hbm([past_states]), *proj_pieces)
        gated.append([g])
        keys.append(k)
        values.append(v)
    for _ in range(n_tensor - 1):
        for c in range(CHUNKS):
            gated[c].append(lax.ppermute(gated[c][-1], "tensor", ring))

    out_pieces = xor_gather(out_own, "dp")
    ffn_pieces = xor_gather(ffn_weights, "dp")
    packed = kernel_call(
        functools.partial(state_kernel, CHUNKS, heads_here, event_count),
        [vmem_spec(), smem_spec()] + [hbm_spec()] * (1 + 2 * CHUNKS),
        hbm_spec(),
        pltpu.HBM((slot_count, heads_here, head_dim, head_dim), bf16),
        [
            pltpu.VMEM((sessions_here, heads_here, head_dim, head_dim), bf16),
            pltpu.VMEM((sessions_here, heads_here, head_dim, head_dim), f32),
            pltpu.VMEM((2 * CHUNKS, chunk_rows, cols_here), bf16),
            pltpu.SemaphoreType.DMA((sessions_here,)),
            pltpu.SemaphoreType.DMA((4,)),
            pltpu.SemaphoreType.DMA((2 * CHUNKS,)),
        ],
        2 * row_count * head_dim * cols_here,
    )(small, send_pos, *in_hbm([past_states, *keys, *values]))
    received = lax.all_to_all(packed, "dp", split_axis=0, concat_axis=0, tiled=True)

    owns, parts, sums = [], [], []
    for c in range(CHUNKS):
        own, *part = kernel_call(
            functools.partial(feed_kernel, n_dp, n_tensor, block, c * chunk_rows),
            [smem_spec()] + [vmem_spec()] * 2 + [hbm_spec()] * (n_tensor + 2 * n_dp),
            [hbm_spec()] * n_tensor,
            [pltpu.HBM((chunk_rows, share), f32)]
            + [pltpu.HBM((chunk_rows, share), bf16)] * (n_tensor - 1),
            [
                pltpu.VMEM((n_tensor, width, cols_here), bf16),
                pltpu.VMEM((width, units_here), bf16),
                pltpu.VMEM((width, units_here), bf16),
                pltpu.VMEM((chunk_rows, width), f32),
                pltpu.VMEM((n_tensor, chunk_rows, cols_here), bf16),
                pltpu.VMEM((chunk_rows, share), f32),
                pltpu.VMEM((n_tensor - 1, chunk_rows, share), bf16),
                pltpu.SemaphoreType.DMA((3, n_dp)),
                pltpu.SemaphoreType.DMA((n_tensor,)),
                pltpu.SemaphoreType.DMA((n_tensor,)),
            ],
            2 * chunk_rows * width * (width + 2 * units_here),
        )(ids, small, tokens, *in_hbm(gated[c] + out_pieces + ffn_pieces))
        owns.append(own)
        parts.append(part)
        sums.append(None)
    for hop in range(n_tensor - 1):
        for c in range(CHUNKS):
            mine = parts[c][hop]
            if hop:
                mine = kernel_call(
                    add_kernel,
                    [vmem_spec()] * 2,
                    vmem_spec(),
                    shape_of((chunk_rows, share), bf16),
                    [],
                    0,
                    limit_mib=4,
                )(sums[c], mine)
            sums[c] = lax.ppermute(mine, "tensor", ring)

    so_far = []
    for c in range(CHUNKS):
        so_far = [
            pl.pallas_call(
                functools.partial(last_kernel, event_count, c * chunk_rows),
                in_specs=[smem_spec()] + [vmem_spec()] * 2 + [hbm_spec()] * len(so_far),
                out_specs=hbm_spec(),
                out_shape=shape_of((row_count, share), bf16),
                scratch_shapes=[
                    pltpu.VMEM((chunk_rows, share), bf16),
                    pltpu.SemaphoreType.DMA,
                ],
                input_output_aliases={3: 0} if so_far else {},
                compiler_params=pltpu.CompilerParams(vmem_limit_bytes=8 * 1024 * 1024),
                cost_estimate=pl.CostEstimate(
                    flops=0, bytes_accessed=chunk_rows * share * 8, transcendentals=0
                ),
                name="last",
            )(end_lengths, owns[c], sums[c], *so_far)
        ]
    (next_tokens,) = so_far

    per_step = min(8, sessions_here)
    moved_states = pl.pallas_call(
        unpack_kernel,
        grid=(sessions_here // per_step,),
        in_specs=[smem_spec(), any_spec()],
        out_specs=pl.BlockSpec((per_step, heads_here, head_dim, head_dim), lambda i: (i, 0, 0, 0)),
        out_shape=shape_of(past_states.shape, f32),
        scratch_shapes=[
            pltpu.VMEM((sessions_here, heads_here, head_dim, head_dim), bf16),
            pltpu.SemaphoreType.DMA((sessions_here,)),
        ],
        compiler_params=pltpu.CompilerParams(vmem_limit_bytes=16 * 1024 * 1024),
        cost_estimate=pl.CostEstimate(
            flops=0, bytes_accessed=past_states.size * 6, transcendentals=0
        ),
        name="unpack",
    )(recv_src, received)
    return (next_tokens, moved_states)


def solution(mesh):
    placed = (
        P(("group", "dp"), None),
        P(("group", "dp"), "tensor", None, None),
        P(None, "dp", "tensor"),
        P(None, "dp", "tensor"),
        P(),
        P(),
        P(("group", "dp")),
        P(("group", "dp")),
    )

    return jax.shard_map(
        per_device,
        mesh=mesh,
        in_specs=placed,
        out_specs=(P(("group", "dp"), "tensor"), P(("group", "dp"), "tensor", None, None)),
        check_vma=False,
    )
```

```python
import functools
import jax
import jax.numpy as jnp
from jax import lax
from jax.experimental import pallas as pl
from jax.experimental.pallas import tpu as pltpu
from jax.sharding import PartitionSpec as P

CHUNKS = 2
BLOCK_ROWS = 256


NT = (((1,), (1,)), ((), ()))


def dot_nt(a, b):
    return lax.dot_general(a, b, NT, preferred_element_type=jnp.float32)


def dot_nn(a, b):
    return jnp.dot(a, b, preferred_element_type=jnp.float32)


def rms_scale(values, gain_row):
    meansq = jnp.mean(values * values, axis=-1, keepdims=True)
    return (values * lax.rsqrt(meansq + 1e-05) * gain_row).astype(jnp.bfloat16)


def piece_copies(pieces, dest, sems, me, pick):
    copies = []
    rows = dest.shape[-2] // len(pieces)
    for k, piece in enumerate(pieces):
        start = pl.multiple_of(jnp.bitwise_xor(me, k) * rows, rows)
        copies.append(
            pltpu.make_async_copy(pick(piece), dest.at[..., pl.ds(start, rows), :], sems.at[k])
        )
    return copies


def project_kernel(n_dp, heads, event_count, block, base, *refs):
    ids_ref, small_ref, tok_ref, past_hbm = refs[:4]
    pieces = refs[4 : 4 + n_dp]
    gated_ref, key_hbm, value_hbm = refs[4 + n_dp : 7 + n_dp]
    normed_ref, past_ref, decay_ref, key_ref, value_ref, w_ref, sems = refs[7 + n_dp :]
    past_copy = pltpu.make_async_copy(
        past_hbm.at[pl.ds(base // event_count, past_ref.shape[0])], past_ref, sems.at[0]
    )
    past_copy.start()
    out_copies = [
        pltpu.make_async_copy(key_ref, key_hbm, sems.at[1]),
        pltpu.make_async_copy(value_ref, value_hbm, sems.at[2]),
    ]
    rows, _ = gated_ref.shape
    head_dim = past_ref.shape[3]
    sessions = block // event_count
    key_scale = head_dim ** (-0.5)
    depth = tok_ref.shape[1] // n_dp
    starts = [pl.multiple_of(jnp.bitwise_xor(ids_ref[0], k) * depth, depth) for k in range(n_dp)]
    split = depth % 128 == 0
    if not split:
        for m in range(4):
            for k in range(n_dp):
                w_ref[m, pl.ds(starts[k], depth), :] = pieces[k][m * depth : (m + 1) * depth]
    at = lax.broadcasted_iota(jnp.int32, (block, block), 0)
    to = lax.broadcasted_iota(jnp.int32, (block, block), 1)
    allowed = (at // event_count == to // event_count) & (at >= to)
    distance = jnp.maximum(at - to, 0).astype(jnp.float32)
    place = lax.broadcasted_iota(jnp.int32, (block, head_dim), 0) % event_count
    since = (place + 1).astype(jnp.float32)
    factors = []
    for h in range(heads):
        rate = small_ref[2 + h : 3 + h, :]
        decay_ref[h] = jnp.where(allowed, jnp.exp(-rate[:, :block] * distance), 0.0) * key_scale
        factors.append(jnp.exp(-rate[:, :head_dim] * since))

    def product(span, m):
        if not split:
            return dot_nn(normed_ref[span], w_ref[m])
        total = None
        for k in range(n_dp):
            term = dot_nn(
                normed_ref[span, pl.ds(starts[k], depth)], pieces[k][m * depth : (m + 1) * depth]
            )
            total = term if total is None else total + term
        return total

    for r in range(0, rows, block):
        span = slice(r, r + block)
        normed_ref[span] = rms_scale(
            tok_ref[base + r : base + r + block].astype(jnp.float32), small_ref[0:1, :]
        )
        query = product(span, 0).astype(jnp.bfloat16)
        keys = product(span, 1).astype(jnp.bfloat16)
        key_ref[span] = keys
        values = product(span, 2).astype(jnp.bfloat16)
        value_ref[span] = values
        gate = product(span, 3)
        if r == 0:
            past_copy.wait()
        if r + block == rows:
            for copy in out_copies:
                copy.start()
        first_session = r // event_count
        for h in range(heads):
            cols = slice(h * head_dim, (h + 1) * head_dim)
            qh, kh, vh = query[:, cols], keys[:, cols], values[:, cols]
            mix = (dot_nt(qh, kh) * decay_ref[h]).astype(jnp.bfloat16)
            intra = dot_nn(mix, vh)
            parts = []
            for s in range(sessions):
                parts.append(
                    dot_nn(
                        qh[s * event_count : (s + 1) * event_count],
                        past_ref[first_session + s, h].astype(jnp.bfloat16),
                    )
                )
            retained = intra + jnp.concatenate(parts, axis=0) * factors[h]
            centred = retained - jnp.mean(retained, axis=-1, keepdims=True)
            row_var = jnp.mean(centred * centred, axis=-1, keepdims=True)
            normalised = centred * lax.rsqrt(row_var + 1e-05)
            gated_ref[span, cols] = (jax.nn.silu(gate[:, cols]) * normalised).astype(jnp.bfloat16)
    for copy in out_copies:
        copy.wait()


def state_kernel(chunks, heads, event_count, *refs):
    small_ref, pos_ref, past_hbm = refs[:3]
    sources = refs[3 : 3 + 2 * chunks]
    out_ref, buf_ref, past_ref, kv_ref, sems, past_sems, kv_sems = refs[3 + 2 * chunks :]
    kv_copies = [
        pltpu.make_async_copy(source, kv_ref.at[k], kv_sems.at[k])
        for k, source in enumerate(sources)
    ]
    for copy in kv_copies:
        copy.start()
    sessions, _, head_dim, _ = past_ref.shape
    groups = past_sems.shape[0]
    group = sessions // groups
    past_copies = [
        pltpu.make_async_copy(
            past_hbm.at[pl.ds(k * group, group)],
            past_ref.at[pl.ds(k * group, group)],
            past_sems.at[k],
        )
        for k in range(groups)
    ]
    for copy in past_copies:
        copy.start()
    rows = kv_ref.shape[1]
    key_scale = head_dim ** (-0.5)

    def copy_of(session):
        return pltpu.make_async_copy(
            buf_ref.at[session], out_ref.at[pos_ref[session]], sems.at[session]
        )

    place = lax.broadcasted_iota(jnp.int32, (rows, head_dim), 0) % event_count
    left = (event_count - 1 - place).astype(jnp.float32)
    factors, carries = [], []
    for h in range(heads):
        rate = small_ref[2 + h : 3 + h, :head_dim]
        factors.append(jnp.exp(-rate * left) * key_scale)
        carries.append(jnp.exp(-rate * event_count))
    for c in range(chunks):
        kv_copies[c].wait()
        kv_copies[chunks + c].wait()
        weighted = []
        for h in range(heads):
            cols = slice(h * head_dim, (h + 1) * head_dim)
            weighted.append(
                (kv_ref[c, :, cols].astype(jnp.float32) * factors[h]).astype(jnp.bfloat16)
            )
        for s in range(rows // event_count):
            session = c * (rows // event_count) + s
            if session % group == 0:
                past_copies[session // group].wait()
            span = slice(s * event_count, (s + 1) * event_count)
            for h in range(heads):
                cols = slice(h * head_dim, (h + 1) * head_dim)
                grown = lax.dot_general(
                    weighted[h][span],
                    kv_ref[chunks + c, span, cols],
                    (((0,), (0,)), ((), ())),
                    preferred_element_type=jnp.float32,
                )
                buf_ref[session, h] = (carries[h] * past_ref[session, h] + grown).astype(
                    jnp.bfloat16
                )

            @pl.when(pos_ref[session] >= 0)
            def _():
                copy_of(session).start()

    for session in range(sessions):

        @pl.when(pos_ref[session] >= 0)
        def _():
            copy_of(session).wait()


def unpack_kernel(src_ref, recv_ref, out_ref, buf_ref, sems):
    per_step = out_ref.shape[0]
    step = pl.program_id(0)

    def copy_of(slot):
        return pltpu.make_async_copy(
            recv_ref.at[jnp.maximum(src_ref[slot], 0)], buf_ref.at[slot], sems.at[slot]
        )

    @pl.when(step == 0)
    def _():
        for slot in range(buf_ref.shape[0]):

            @pl.when(src_ref[slot] >= 0)
            def _():
                copy_of(slot).start()

    for i in range(per_step):
        slot = step * per_step + i

        @pl.when(src_ref[slot] >= 0)
        def _():
            copy_of(slot).wait()
            out_ref[i] = buf_ref[slot].astype(jnp.float32)

        @pl.when(src_ref[slot] < 0)
        def _():
            out_ref[i] = jnp.zeros(out_ref.shape[1:], jnp.float32)


def feed_kernel(n_dp, n_tensor, block, base, *refs):
    ids_ref, small_ref, tok_ref = refs[:3]
    gated_hbm = refs[3 : 3 + n_tensor]
    at = 3 + n_tensor
    out_pieces = refs[at : at + n_dp]
    at += n_dp
    pairs = refs[at : at + 2]
    near = refs[at + 2 : at + n_dp]
    far = refs[at + n_dp : at + 2 * n_dp - 2]
    at += 2 * n_dp - 2
    own_hbm, *part_hbm = refs[at : at + n_tensor]
    wo_ref, ffn_ref, res_ref, gated, own_ref, part_ref, hid_ref, act_ref = refs[
        at + n_tensor : -3
    ]
    sems, gated_sems, done_sems = refs[-3:]
    rows, width = own_ref.shape
    me, group = ids_ref[0], ids_ref[2 + n_tensor]
    out_copies = piece_copies(
        out_pieces, wo_ref, sems.at[0], me, lambda piece: piece.at[:, pl.ds(0, wo_ref.shape[1] // n_dp)]
    )
    depth = ffn_ref.shape[1] // n_dp

    def ffn_copy(source, half, k):
        start = pl.multiple_of(jnp.bitwise_xor(me, k) * depth, depth)
        return pltpu.make_async_copy(
            source, ffn_ref.at[half, pl.ds(start, depth)], sems.at[1 + half, k]
        )

    up_copies = [ffn_copy(pairs[k].at[0], 0, k) for k in range(2)]
    down_copies = [ffn_copy(pairs[k].at[1], 1, k) for k in range(2)]
    rest = []
    for k in range(2, n_dp):
        rest.append(ffn_copy(near[k - 2], group, k))
        rest.append(ffn_copy(far[k - 2], 1 - group, k))
        up_copies.append(ffn_copy(near[k - 2], 0, k))
        down_copies.append(ffn_copy(near[k - 2], 1, k))
    gated_copies = [
        pltpu.make_async_copy(source, gated.at[k], gated_sems.at[k])
        for k, source in enumerate(gated_hbm)
    ]
    done_copies = [pltpu.make_async_copy(own_ref, own_hbm, done_sems.at[0])]
    for k in range(1, n_tensor):
        done_copies.append(
            pltpu.make_async_copy(part_ref.at[k - 1], part_hbm[k - 1], done_sems.at[k])
        )
    for copy in out_copies + gated_copies:
        copy.start()
    for copy in up_copies[:2] + rest:
        copy.start()
    for copy in out_copies + gated_copies:
        copy.wait()
    for copy in down_copies[:2]:
        copy.start()
    for r in range(0, rows, block):
        span = slice(r, r + block)
        attended = dot_nt(gated[0, span], wo_ref[ids_ref[2]])
        for k in range(1, n_tensor):
            attended += dot_nt(gated[k, span], wo_ref[ids_ref[2 + k]])
        residual = tok_ref[base + r : base + r + block].astype(jnp.float32) + attended
        res_ref[span] = residual
        hid_ref[span] = rms_scale(residual, small_ref[1:2, :])
    for copy in up_copies:
        copy.wait()
    for r in range(0, rows, block):
        span = slice(r, r + block)
        activated = jax.nn.gelu(dot_nn(hid_ref[span], ffn_ref[0]), approximate=True)
        act_ref[span] = activated.astype(jnp.bfloat16)
    for copy in down_copies:
        copy.wait()

    def term(k):
        start = pl.multiple_of(ids_ref[2 + k] * width, width)
        return dot_nt(act_ref[...], ffn_ref[1, pl.ds(start, width), :])

    mine = pl.ds(pl.multiple_of(ids_ref[1] * width, width), width)
    own_ref[...] = res_ref[:, mine] + term(0)
    done_copies[0].start()
    for k in list(range(2, n_tensor)) + [1]:
        part_ref[k - 1] = term(k).astype(jnp.bfloat16)
        done_copies[k].start()
    for copy in done_copies:
        copy.wait()


def add_kernel(a_ref, b_ref, out_ref):
    total = a_ref[...].astype(jnp.float32) + b_ref[...].astype(jnp.float32)
    out_ref[...] = total.astype(jnp.bfloat16)


def last_kernel(event_count, base, *refs):
    lengths_ref, own_ref, term_ref = refs[:3]
    out_hbm, out_ref, sem = refs[-3:]
    rows, width = own_ref.shape
    place = lax.broadcasted_iota(jnp.int32, (event_count, width), 0)
    for s in range(rows // event_count):
        span = slice(s * event_count, (s + 1) * event_count)
        total = own_ref[span] + term_ref[span].astype(jnp.float32)
        keep = place < lengths_ref[base // event_count + s]
        out_ref[span] = jnp.where(keep, total, 0.0).astype(jnp.bfloat16)
    copy = pltpu.make_async_copy(out_ref, out_hbm.at[pl.ds(base, rows)], sem)
    copy.start()
    copy.wait()


def xor_gather(value, axis, last_bit=1):
    pieces = [value]
    size = lax.axis_size(axis)
    bit = size // 2
    order = [0]
    while bit >= last_bit:
        pairs = [(i, i ^ bit) for i in range(size)]
        arrived = []
        for piece in pieces:
            arrived.append(lax.ppermute(piece, axis, pairs))
        pieces = pieces + arrived
        order = order + [k ^ bit for k in order]
        bit //= 2
    return [pieces[order.index(k)] for k in range(0, size, last_bit)]


def ring_order(size):
    return list(range(0, size, 2)) + list(range(1, size, 2))[::-1]


def ring_pairs(size):
    order = ring_order(size)
    return [(order[i], order[(i + 1) % size]) for i in range(size)]


def ring_sources(size):
    order = ring_order(size)
    return [[order[(order.index(at) - k) % size] for k in range(size)] for at in range(size)]


def any_spec():
    return pl.BlockSpec(memory_space=pl.ANY)


def smem_spec():
    return pl.BlockSpec(memory_space=pltpu.SMEM)


def hbm_spec():
    return pl.BlockSpec(memory_space=pltpu.HBM)


def in_hbm(arrays):
    return [pltpu.with_memory_space_constraint(array, pltpu.HBM) for array in arrays]


def vmem_spec():
    return pl.BlockSpec(memory_space=pltpu.VMEM)


def kernel_call(kernel, in_specs, out_specs, out_shape, scratch, flops, limit_mib=24):
    return pl.pallas_call(
        kernel,
        in_specs=in_specs,
        out_specs=out_specs,
        out_shape=out_shape,
        scratch_shapes=scratch,
        compiler_params=pltpu.CompilerParams(vmem_limit_bytes=limit_mib * 1024 * 1024),
        cost_estimate=pl.CostEstimate(
            flops=flops, bytes_accessed=4 * 1024 * 1024, transcendentals=0
        ),
    )


def per_device(
    tokens, past_states, attn_weights, ffn_weights, norm_gains, head_rates, end_lengths, new_slot
):
    sessions_here = end_lengths.shape[0]
    row_count, width = tokens.shape
    event_count = row_count // sessions_here
    heads_here, head_dim = past_states.shape[1], past_states.shape[3]
    cols_here = heads_here * head_dim
    units_here = ffn_weights.shape[2]
    n_dp, n_tensor = lax.axis_size("dp"), lax.axis_size("tensor")
    dp_at, tensor_at = lax.axis_index("dp"), lax.axis_index("tensor")
    share = width // n_tensor
    pair_cap = max(2, 2 * sessions_here // n_dp)
    slot_count = n_dp * pair_cap
    chunk_rows = row_count // CHUNKS
    block = min(BLOCK_ROWS, chunk_rows)
    ring = ring_pairs(n_tensor)
    bf16, f32 = jnp.bfloat16, jnp.float32
    shape_of = jax.ShapeDtypeStruct

    survive = end_lengths > event_count
    target_dev = new_slot // sessions_here
    session_ids = jnp.arange(sessions_here, dtype=jnp.int32)
    proj_rows = attn_weights.shape[1]
    proj_pieces = xor_gather(attn_weights[:4].reshape(-1, cols_here), "dp")
    notes = jnp.stack([jnp.where(survive, target_dev, -1), new_slot % sessions_here])
    note_rows = 16
    notes = jnp.pad(
        notes.astype(bf16), ((0, note_rows - 2), (0, cols_here - sessions_here))
    )
    out_own = lax.all_to_all(
        jnp.broadcast_to(
            jnp.concatenate([attn_weights[4], notes])[None],
            (n_tensor, proj_rows + note_rows, cols_here),
        ),
        "tensor",
        split_axis=0,
        concat_axis=0,
        tiled=True,
    )
    half_own = lax.dynamic_index_in_dim(ffn_weights, lax.axis_index("group"), 0, keepdims=False)
    sources = jnp.array(ring_sources(n_tensor), jnp.int32)[tensor_at]
    places = jnp.stack([dp_at, tensor_at]).astype(jnp.int32)
    ids = jnp.concatenate([places, sources, lax.axis_index("group").astype(jnp.int32)[None]])
    out_pieces = xor_gather(out_own, "dp")

    earlier = (
        (target_dev[None, :] == target_dev[:, None])
        & survive[None, :]
        & (session_ids[None, :] < session_ids[:, None])
    )
    pair_rank = jnp.sum(earlier.astype(jnp.int32), axis=1)
    send_pos = jnp.where(survive, target_dev * pair_cap + pair_rank, -1)
    meta = jnp.stack([piece[0, proj_rows:, :sessions_here] for piece in out_pieces])
    meta = meta.astype(jnp.int32)
    from_dev = jnp.bitwise_xor(dp_at, jnp.arange(n_dp, dtype=jnp.int32))
    coming = meta[:, 0] == dp_at
    ahead = coming[:, None, :] & (session_ids[None, None, :] < session_ids[None, :, None])
    rank_all = jnp.sum(ahead.astype(jnp.int32), axis=2)
    from_pos = from_dev[:, None] * pair_cap + rank_all + 1
    lands = meta[:, 1][None] == session_ids[:, None, None]
    recv_src = jnp.sum(jnp.where(lands & coming[None], from_pos[None], 0), axis=(1, 2)) - 1

    rows_shape = shape_of((chunk_rows, cols_here), bf16)
    decay_shape = pltpu.VMEM((heads_here, block, block), f32)
    head_decay = lax.dynamic_slice_in_dim(head_rates, tensor_at * heads_here, heads_here)
    small = jnp.concatenate(
        [norm_gains, jnp.broadcast_to(head_decay[:, None], (heads_here, width))]
    )
    chunk_sessions = chunk_rows // event_count
    split = (width // n_dp) % 128 == 0
    gated, keys, values = [], [], []
    for c in range(CHUNKS):
        g, k, v = kernel_call(
            functools.partial(project_kernel, n_dp, heads_here, event_count, block, c * chunk_rows),
            [smem_spec()] + [vmem_spec()] * 2 + [hbm_spec()] + [vmem_spec()] * n_dp,
            [vmem_spec()] + [hbm_spec()] * 2,
            [rows_shape] + [pltpu.HBM((chunk_rows, cols_here), bf16)] * 2,
            [
                pltpu.VMEM((chunk_rows, width), bf16),
                pltpu.VMEM((chunk_sessions, heads_here, head_dim, head_dim), f32),
                decay_shape,
                pltpu.VMEM((chunk_rows, cols_here), bf16),
                pltpu.VMEM((chunk_rows, cols_here), bf16),
                pltpu.VMEM((4, 16 if split else width, cols_here), bf16),
                pltpu.SemaphoreType.DMA((3,)),
            ],
            2 * chunk_rows * width * cols_here * 4,
        )(ids, small, tokens, *in_hbm([past_states]), *proj_pieces)
        gated.append([g])
        keys.append(k)
        values.append(v)
    for _ in range(n_tensor - 1):
        for c in range(CHUNKS):
            gated[c].append(lax.ppermute(gated[c][-1], "tensor", ring))

    near = xor_gather(half_own, "dp", last_bit=2)[1:]
    swap = [(0, 1), (1, 0)]
    far = []
    for k, piece in enumerate(near):
        far.append(lax.ppermute(piece, "group", swap))
    beside = [(i, i ^ 1) for i in range(n_dp)]

    def to_beside(value):
        return lax.ppermute(value, "dp", beside)

    ffn_pieces = [ffn_weights, to_beside(ffn_weights)]
    for side in (near, far):
        for k, piece in enumerate(side):
            ffn_pieces += [piece, to_beside(piece)]
    packed = kernel_call(
        functools.partial(state_kernel, CHUNKS, heads_here, event_count),
        [vmem_spec(), smem_spec()] + [hbm_spec()] * (1 + 2 * CHUNKS),
        hbm_spec(),
        pltpu.HBM((slot_count, heads_here, head_dim, head_dim), bf16),
        [
            pltpu.VMEM((sessions_here, heads_here, head_dim, head_dim), bf16),
            pltpu.VMEM((sessions_here, heads_here, head_dim, head_dim), f32),
            pltpu.VMEM((2 * CHUNKS, chunk_rows, cols_here), bf16),
            pltpu.SemaphoreType.DMA((sessions_here,)),
            pltpu.SemaphoreType.DMA((4,)),
            pltpu.SemaphoreType.DMA((2 * CHUNKS,)),
        ],
        2 * row_count * head_dim * cols_here,
    )(small, send_pos, *in_hbm([past_states, *keys, *values]))
    received = lax.all_to_all(packed, "dp", split_axis=0, concat_axis=0, tiled=True)

    owns, parts, sums = [], [], []
    for c in range(CHUNKS):
        own, *part = kernel_call(
            functools.partial(feed_kernel, n_dp, n_tensor, block, c * chunk_rows),
            [smem_spec()] + [vmem_spec()] * 2 + [hbm_spec()] * (n_tensor + n_dp + 2 * n_dp - 2),
            [hbm_spec()] * n_tensor,
            [pltpu.HBM((chunk_rows, share), f32)]
            + [pltpu.HBM((chunk_rows, share), bf16)] * (n_tensor - 1),
            [
                pltpu.VMEM((n_tensor, width, cols_here), bf16),
                pltpu.VMEM((2, width, units_here), bf16),
                pltpu.VMEM((chunk_rows, width), f32),
                pltpu.VMEM((n_tensor, chunk_rows, cols_here), bf16),
                pltpu.VMEM((chunk_rows, share), f32),
                pltpu.VMEM((n_tensor - 1, chunk_rows, share), bf16),
                pltpu.VMEM((chunk_rows, width), bf16),
                pltpu.VMEM((chunk_rows, units_here), bf16),
                pltpu.SemaphoreType.DMA((3, n_dp)),
                pltpu.SemaphoreType.DMA((n_tensor,)),
                pltpu.SemaphoreType.DMA((n_tensor,)),
            ],
            2 * chunk_rows * width * (width + 2 * units_here),
        )(ids, small, tokens, *in_hbm(gated[c] + out_pieces + ffn_pieces))
        owns.append(own)
        parts.append(part)
        sums.append(None)
    for hop in range(n_tensor - 1):
        for c in range(CHUNKS):
            mine = parts[c][hop]
            if hop:
                mine = kernel_call(
                    add_kernel,
                    [vmem_spec()] * 2,
                    vmem_spec(),
                    shape_of((chunk_rows, share), bf16),
                    [],
                    0,
                    limit_mib=4,
                )(sums[c], mine)
            sums[c] = lax.ppermute(mine, "tensor", ring)

    so_far = []
    for c in range(CHUNKS):
        so_far = [
            pl.pallas_call(
                functools.partial(last_kernel, event_count, c * chunk_rows),
                in_specs=[smem_spec()] + [vmem_spec()] * 2 + [hbm_spec()] * len(so_far),
                out_specs=hbm_spec(),
                out_shape=shape_of((row_count, share), bf16),
                scratch_shapes=[
                    pltpu.VMEM((chunk_rows, share), bf16),
                    pltpu.SemaphoreType.DMA,
                ],
                input_output_aliases={3: 0} if so_far else {},
                compiler_params=pltpu.CompilerParams(vmem_limit_bytes=8 * 1024 * 1024),
                cost_estimate=pl.CostEstimate(
                    flops=0, bytes_accessed=chunk_rows * share * 8, transcendentals=0
                ),
                name="last",
            )(end_lengths, owns[c], sums[c], *so_far)
        ]
    (next_tokens,) = so_far

    per_step = min(8, sessions_here)
    moved_states = pl.pallas_call(
        unpack_kernel,
        grid=(sessions_here // per_step,),
        in_specs=[smem_spec(), any_spec()],
        out_specs=pl.BlockSpec((per_step, heads_here, head_dim, head_dim), lambda i: (i, 0, 0, 0)),
        out_shape=shape_of(past_states.shape, f32),
        scratch_shapes=[
            pltpu.VMEM((sessions_here, heads_here, head_dim, head_dim), bf16),
            pltpu.SemaphoreType.DMA((sessions_here,)),
        ],
        compiler_params=pltpu.CompilerParams(vmem_limit_bytes=16 * 1024 * 1024),
        cost_estimate=pl.CostEstimate(
            flops=0, bytes_accessed=past_states.size * 6, transcendentals=0
        ),
        name="unpack",
    )(recv_src, received)
    return (next_tokens, moved_states)


def solution(mesh):
    placed = (
        P(("group", "dp"), None),
        P(("group", "dp"), "tensor", None, None),
        P(None, "dp", "tensor"),
        P(None, "dp", "tensor"),
        P(),
        P(),
        P(("group", "dp")),
        P(("group", "dp")),
    )

    return jax.shard_map(
        per_device,
        mesh=mesh,
        in_specs=placed,
        out_specs=(P(("group", "dp"), "tensor"), P(("group", "dp"), "tensor", None, None)),
        check_vma=False,
    )
```

```python
import functools
import jax
import jax.numpy as jnp
from jax import lax
from jax.experimental import pallas as pl
from jax.experimental.pallas import tpu as pltpu
from jax.sharding import PartitionSpec as P

CHUNKS = 2
BLOCK_ROWS = 256


NT = (((1,), (1,)), ((), ()))


def dot_nt(a, b):
    return lax.dot_general(a, b, NT, preferred_element_type=jnp.float32)


def dot_nn(a, b):
    return jnp.dot(a, b, preferred_element_type=jnp.float32)


def rms_scale(values, gain_row):
    meansq = jnp.mean(values * values, axis=-1, keepdims=True)
    return (values * lax.rsqrt(meansq + 1e-05) * gain_row).astype(jnp.bfloat16)


def piece_copies(pieces, dest, sems, me, pick):
    copies = []
    rows = dest.shape[-2] // len(pieces)
    for k, piece in enumerate(pieces):
        start = pl.multiple_of(jnp.bitwise_xor(me, k) * rows, rows)
        copies.append(
            pltpu.make_async_copy(pick(piece), dest.at[..., pl.ds(start, rows), :], sems.at[k])
        )
    return copies


def project_kernel(n_dp, heads, event_count, block, base, *refs):
    ids_ref, small_ref, tok_ref, past_hbm = refs[:4]
    pieces = refs[4 : 4 + n_dp]
    gated_ref, key_hbm, value_hbm = refs[4 + n_dp : 7 + n_dp]
    normed_ref, past_ref, decay_ref, key_ref, value_ref, w_ref, sems = refs[7 + n_dp :]
    past_copy = pltpu.make_async_copy(
        past_hbm.at[pl.ds(base // event_count, past_ref.shape[0])], past_ref, sems.at[0]
    )
    past_copy.start()
    out_copies = [
        pltpu.make_async_copy(key_ref, key_hbm, sems.at[1]),
        pltpu.make_async_copy(value_ref, value_hbm, sems.at[2]),
    ]
    rows, _ = gated_ref.shape
    head_dim = past_ref.shape[3]
    sessions = block // event_count
    key_scale = head_dim ** (-0.5)
    depth = tok_ref.shape[1] // n_dp
    starts = [pl.multiple_of(jnp.bitwise_xor(ids_ref[0], k) * depth, depth) for k in range(n_dp)]
    split = depth % 128 == 0
    if not split:
        for m in range(4):
            for k in range(n_dp):
                w_ref[m, pl.ds(starts[k], depth), :] = pieces[k][m * depth : (m + 1) * depth]
    at = lax.broadcasted_iota(jnp.int32, (block, block), 0)
    to = lax.broadcasted_iota(jnp.int32, (block, block), 1)
    allowed = (at // event_count == to // event_count) & (at >= to)
    distance = jnp.maximum(at - to, 0).astype(jnp.float32)
    place = lax.broadcasted_iota(jnp.int32, (block, head_dim), 0) % event_count
    since = (place + 1).astype(jnp.float32)
    factors = []
    for h in range(heads):
        rate = small_ref[2 + h : 3 + h, :]
        decay_ref[h] = jnp.where(allowed, jnp.exp(-rate[:, :block] * distance), 0.0) * key_scale
        factors.append(jnp.exp(-rate[:, :head_dim] * since))

    def product(span, m):
        if not split:
            return dot_nn(normed_ref[span], w_ref[m])
        total = None
        for k in range(n_dp):
            term = dot_nn(
                normed_ref[span, pl.ds(starts[k], depth)], pieces[k][m * depth : (m + 1) * depth]
            )
            total = term if total is None else total + term
        return total

    for r in range(0, rows, block):
        span = slice(r, r + block)
        normed_ref[span] = rms_scale(
            tok_ref[base + r : base + r + block].astype(jnp.float32), small_ref[0:1, :]
        )
        query = product(span, 0).astype(jnp.bfloat16)
        keys = product(span, 1).astype(jnp.bfloat16)
        key_ref[span] = keys
        values = product(span, 2).astype(jnp.bfloat16)
        value_ref[span] = values
        gate = product(span, 3)
        if r == 0:
            past_copy.wait()
        if r + block == rows:
            for copy in out_copies:
                copy.start()
        first_session = r // event_count
        for h in range(heads):
            cols = slice(h * head_dim, (h + 1) * head_dim)
            qh, kh, vh = query[:, cols], keys[:, cols], values[:, cols]
            mix = (dot_nt(qh, kh) * decay_ref[h]).astype(jnp.bfloat16)
            intra = dot_nn(mix, vh)
            parts = []
            for s in range(sessions):
                parts.append(
                    dot_nn(
                        qh[s * event_count : (s + 1) * event_count],
                        past_ref[first_session + s, h].astype(jnp.bfloat16),
                    )
                )
            retained = intra + jnp.concatenate(parts, axis=0) * factors[h]
            centred = retained - jnp.mean(retained, axis=-1, keepdims=True)
            row_var = jnp.mean(centred * centred, axis=-1, keepdims=True)
            normalised = centred * lax.rsqrt(row_var + 1e-05)
            gated_ref[span, cols] = (jax.nn.silu(gate[:, cols]) * normalised).astype(jnp.bfloat16)
    for copy in out_copies:
        copy.wait()


def state_kernel(chunks, heads, event_count, *refs):
    small_ref, pos_ref, past_hbm = refs[:3]
    sources = refs[3 : 3 + 2 * chunks]
    out_ref, buf_ref, past_ref, kv_ref, sems, past_sems, kv_sems = refs[3 + 2 * chunks :]
    kv_copies = [
        pltpu.make_async_copy(source, kv_ref.at[k], kv_sems.at[k])
        for k, source in enumerate(sources)
    ]
    for copy in kv_copies:
        copy.start()
    sessions, _, head_dim, _ = past_ref.shape
    groups = past_sems.shape[0]
    group = sessions // groups
    past_copies = [
        pltpu.make_async_copy(
            past_hbm.at[pl.ds(k * group, group)],
            past_ref.at[pl.ds(k * group, group)],
            past_sems.at[k],
        )
        for k in range(groups)
    ]
    for copy in past_copies:
        copy.start()
    rows = kv_ref.shape[1]
    key_scale = head_dim ** (-0.5)

    def copy_of(session):
        return pltpu.make_async_copy(
            buf_ref.at[session], out_ref.at[pos_ref[session]], sems.at[session]
        )

    place = lax.broadcasted_iota(jnp.int32, (rows, head_dim), 0) % event_count
    left = (event_count - 1 - place).astype(jnp.float32)
    factors, carries = [], []
    for h in range(heads):
        rate = small_ref[2 + h : 3 + h, :head_dim]
        factors.append(jnp.exp(-rate * left) * key_scale)
        carries.append(jnp.exp(-rate * event_count))
    for c in range(chunks):
        kv_copies[c].wait()
        kv_copies[chunks + c].wait()
        weighted = []
        for h in range(heads):
            cols = slice(h * head_dim, (h + 1) * head_dim)
            weighted.append(
                (kv_ref[c, :, cols].astype(jnp.float32) * factors[h]).astype(jnp.bfloat16)
            )
        for s in range(rows // event_count):
            session = c * (rows // event_count) + s
            if session % group == 0:
                past_copies[session // group].wait()
            span = slice(s * event_count, (s + 1) * event_count)
            for h in range(heads):
                cols = slice(h * head_dim, (h + 1) * head_dim)
                grown = lax.dot_general(
                    weighted[h][span],
                    kv_ref[chunks + c, span, cols],
                    (((0,), (0,)), ((), ())),
                    preferred_element_type=jnp.float32,
                )
                buf_ref[session, h] = (carries[h] * past_ref[session, h] + grown).astype(
                    jnp.bfloat16
                )

            @pl.when(pos_ref[session] >= 0)
            def _():
                copy_of(session).start()

    for session in range(sessions):

        @pl.when(pos_ref[session] >= 0)
        def _():
            copy_of(session).wait()


def unpack_kernel(src_ref, recv_ref, out_ref, buf_ref, sems):
    per_step = out_ref.shape[0]
    step = pl.program_id(0)

    def copy_of(slot):
        return pltpu.make_async_copy(
            recv_ref.at[jnp.maximum(src_ref[slot], 0)], buf_ref.at[slot], sems.at[slot]
        )

    @pl.when(step == 0)
    def _():
        for slot in range(buf_ref.shape[0]):

            @pl.when(src_ref[slot] >= 0)
            def _():
                copy_of(slot).start()

    for i in range(per_step):
        slot = step * per_step + i

        @pl.when(src_ref[slot] >= 0)
        def _():
            copy_of(slot).wait()
            out_ref[i] = buf_ref[slot].astype(jnp.float32)

        @pl.when(src_ref[slot] < 0)
        def _():
            out_ref[i] = jnp.zeros(out_ref.shape[1:], jnp.float32)


def feed_kernel(n_dp, n_tensor, block, base, *refs):
    ids_ref, small_ref, tok_ref = refs[:3]
    gated_hbm = refs[3 : 3 + n_tensor]
    at = 3 + n_tensor
    out_pieces = refs[at : at + n_dp]
    at += n_dp
    pairs = refs[at : at + 2]
    near = refs[at + 2 : at + n_dp]
    far = refs[at + n_dp : at + 2 * n_dp - 2]
    at += 2 * n_dp - 2
    own_hbm, *part_hbm = refs[at : at + n_tensor]
    wo_ref, ffn_ref, res_ref, gated, own_ref, part_ref, hid_ref, act_ref = refs[
        at + n_tensor : -3
    ]
    sems, gated_sems, done_sems = refs[-3:]
    rows, width = own_ref.shape
    me, group = ids_ref[0], ids_ref[2 + n_tensor]
    out_copies = piece_copies(
        out_pieces, wo_ref, sems.at[0], me, lambda piece: piece.at[:, pl.ds(0, wo_ref.shape[1] // n_dp)]
    )
    depth = ffn_ref.shape[1] // n_dp

    def ffn_copy(source, half, k):
        start = pl.multiple_of(jnp.bitwise_xor(me, k) * depth, depth)
        return pltpu.make_async_copy(
            source, ffn_ref.at[half, pl.ds(start, depth)], sems.at[1 + half, k]
        )

    up_copies = [ffn_copy(pairs[k].at[0], 0, k) for k in range(2)]
    down_copies = [ffn_copy(pairs[k].at[1], 1, k) for k in range(2)]
    rest = []
    for k in range(2, n_dp):
        rest.append(ffn_copy(near[k - 2], group, k))
        rest.append(ffn_copy(far[k - 2], 1 - group, k))
        up_copies.append(ffn_copy(near[k - 2], 0, k))
        down_copies.append(ffn_copy(near[k - 2], 1, k))
    gated_copies = [
        pltpu.make_async_copy(source, gated.at[k], gated_sems.at[k])
        for k, source in enumerate(gated_hbm[:-1])
    ]
    done_copies = [pltpu.make_async_copy(own_ref, own_hbm, done_sems.at[0])]
    for k in range(1, n_tensor):
        done_copies.append(
            pltpu.make_async_copy(part_ref.at[k - 1], part_hbm[k - 1], done_sems.at[k])
        )
    here = [gated.at[k] for k in range(n_tensor - 1)] + [gated_hbm[-1]]
    for copy in out_copies + gated_copies:
        copy.start()
    for copy in up_copies[:2] + rest:
        copy.start()
    for copy in out_copies + gated_copies:
        copy.wait()
    for copy in down_copies[:2]:
        copy.start()
    for r in range(0, rows, block):
        span = slice(r, r + block)
        attended = dot_nt(here[0][span], wo_ref[ids_ref[2]])
        for k in range(1, n_tensor):
            attended += dot_nt(here[k][span], wo_ref[ids_ref[2 + k]])
        residual = tok_ref[base + r : base + r + block].astype(jnp.float32) + attended
        res_ref[span] = residual
        hid_ref[span] = rms_scale(residual, small_ref[1:2, :])
    for copy in up_copies:
        copy.wait()
    for r in range(0, rows, block):
        span = slice(r, r + block)
        activated = jax.nn.gelu(dot_nn(hid_ref[span], ffn_ref[0]), approximate=True)
        act_ref[span] = activated.astype(jnp.bfloat16)
    for copy in down_copies:
        copy.wait()

    def term(k):
        start = pl.multiple_of(ids_ref[2 + k] * width, width)
        return dot_nt(act_ref[...], ffn_ref[1, pl.ds(start, width), :])

    mine = pl.ds(pl.multiple_of(ids_ref[1] * width, width), width)
    own_ref[...] = res_ref[:, mine] + term(0)
    done_copies[0].start()
    for k in list(range(2, n_tensor)) + [1]:
        part_ref[k - 1] = term(k).astype(jnp.bfloat16)
        done_copies[k].start()
    for copy in done_copies:
        copy.wait()


def add_kernel(a_ref, b_ref, out_ref):
    total = a_ref[...].astype(jnp.float32) + b_ref[...].astype(jnp.float32)
    out_ref[...] = total.astype(jnp.bfloat16)


def last_kernel(event_count, base, *refs):
    lengths_ref, own_ref, term_ref = refs[:3]
    out_hbm, out_ref, sem = refs[-3:]
    rows, width = own_ref.shape
    place = lax.broadcasted_iota(jnp.int32, (event_count, width), 0)
    for s in range(rows // event_count):
        span = slice(s * event_count, (s + 1) * event_count)
        total = own_ref[span] + term_ref[span].astype(jnp.float32)
        keep = place < lengths_ref[base // event_count + s]
        out_ref[span] = jnp.where(keep, total, 0.0).astype(jnp.bfloat16)
    copy = pltpu.make_async_copy(out_ref, out_hbm.at[pl.ds(base, rows)], sem)
    copy.start()
    copy.wait()


def xor_gather(value, axis, last_bit=1):
    pieces = [value]
    size = lax.axis_size(axis)
    bit = size // 2
    order = [0]
    while bit >= last_bit:
        pairs = [(i, i ^ bit) for i in range(size)]
        arrived = []
        for piece in pieces:
            arrived.append(lax.ppermute(piece, axis, pairs))
        pieces = pieces + arrived
        order = order + [k ^ bit for k in order]
        bit //= 2
    return [pieces[order.index(k)] for k in range(0, size, last_bit)]


def ring_order(size):
    return list(range(0, size, 2)) + list(range(1, size, 2))[::-1]


def ring_pairs(size):
    order = ring_order(size)
    return [(order[i], order[(i + 1) % size]) for i in range(size)]


def ring_sources(size):
    order = ring_order(size)
    return [[order[(order.index(at) - k) % size] for k in range(size)] for at in range(size)]


def any_spec():
    return pl.BlockSpec(memory_space=pl.ANY)


def smem_spec():
    return pl.BlockSpec(memory_space=pltpu.SMEM)


def hbm_spec():
    return pl.BlockSpec(memory_space=pltpu.HBM)


def in_hbm(arrays):
    return [pltpu.with_memory_space_constraint(array, pltpu.HBM) for array in arrays]


def vmem_spec():
    return pl.BlockSpec(memory_space=pltpu.VMEM)


def kernel_call(kernel, in_specs, out_specs, out_shape, scratch, flops, limit_mib=24):
    return pl.pallas_call(
        kernel,
        in_specs=in_specs,
        out_specs=out_specs,
        out_shape=out_shape,
        scratch_shapes=scratch,
        compiler_params=pltpu.CompilerParams(vmem_limit_bytes=limit_mib * 1024 * 1024),
        cost_estimate=pl.CostEstimate(
            flops=flops, bytes_accessed=4 * 1024 * 1024, transcendentals=0
        ),
    )


def per_device(
    tokens, past_states, attn_weights, ffn_weights, norm_gains, head_rates, end_lengths, new_slot
):
    sessions_here = end_lengths.shape[0]
    row_count, width = tokens.shape
    event_count = row_count // sessions_here
    heads_here, head_dim = past_states.shape[1], past_states.shape[3]
    cols_here = heads_here * head_dim
    units_here = ffn_weights.shape[2]
    n_dp, n_tensor = lax.axis_size("dp"), lax.axis_size("tensor")
    dp_at, tensor_at = lax.axis_index("dp"), lax.axis_index("tensor")
    share = width // n_tensor
    pair_cap = max(2, 2 * sessions_here // n_dp)
    slot_count = n_dp * pair_cap
    chunk_rows = row_count // CHUNKS
    block = min(BLOCK_ROWS, chunk_rows)
    ring = ring_pairs(n_tensor)
    bf16, f32 = jnp.bfloat16, jnp.float32
    shape_of = jax.ShapeDtypeStruct

    survive = end_lengths > event_count
    target_dev = new_slot // sessions_here
    session_ids = jnp.arange(sessions_here, dtype=jnp.int32)
    proj_rows = attn_weights.shape[1]
    notes = jnp.stack([jnp.where(survive, target_dev, -1), new_slot % sessions_here])
    notes = jnp.pad(notes.astype(bf16), ((0, 6), (0, cols_here - sessions_here)))
    proj_own = jnp.concatenate([attn_weights[:4].reshape(4 * proj_rows, cols_here), notes])
    proj_pieces = xor_gather(proj_own, "dp")
    out_own = lax.all_to_all(
        jnp.broadcast_to(attn_weights[4:], (n_tensor, proj_rows, cols_here)),
        "tensor",
        split_axis=0,
        concat_axis=0,
        tiled=True,
    )
    half_own = lax.dynamic_index_in_dim(
        ffn_weights, lax.axis_index("group"), 0, keepdims=False
    )
    sources = jnp.array(ring_sources(n_tensor), jnp.int32)[tensor_at]
    places = jnp.stack([dp_at, tensor_at]).astype(jnp.int32)
    group_at = lax.axis_index("group").astype(jnp.int32)
    ids = jnp.concatenate([places, sources, group_at[None]])
    head_decay = lax.dynamic_slice_in_dim(head_rates, tensor_at * heads_here, heads_here)
    small = jnp.concatenate(
        [norm_gains, jnp.broadcast_to(head_decay[:, None], (heads_here, width))]
    )
    out_pieces = xor_gather(out_own, "dp")

    earlier = (
        (target_dev[None, :] == target_dev[:, None])
        & survive[None, :]
        & (session_ids[None, :] < session_ids[:, None])
    )
    pair_rank = jnp.sum(earlier.astype(jnp.int32), axis=1)
    send_pos = jnp.where(survive, target_dev * pair_cap + pair_rank, -1)
    meta = jnp.stack([piece[4 * proj_rows :, :sessions_here] for piece in proj_pieces])
    meta = meta.astype(jnp.int32)
    from_dev = jnp.bitwise_xor(dp_at, jnp.arange(n_dp, dtype=jnp.int32))
    coming = meta[:, 0] == dp_at
    ahead = coming[:, None, :] & (session_ids[None, None, :] < session_ids[None, :, None])
    rank_all = jnp.sum(ahead.astype(jnp.int32), axis=2)
    from_pos = from_dev[:, None] * pair_cap + rank_all + 1
    lands = meta[:, 1][None] == session_ids[:, None, None]
    recv_src = jnp.sum(jnp.where(lands & coming[None], from_pos[None], 0), axis=(1, 2)) - 1

    rows_shape = shape_of((chunk_rows, cols_here), bf16)
    decay_shape = pltpu.VMEM((heads_here, block, block), f32)
    chunk_sessions = chunk_rows // event_count
    split = (width // n_dp) % 128 == 0
    gated, keys, values = [], [], []
    for c in range(CHUNKS):
        g, k, v = kernel_call(
            functools.partial(project_kernel, n_dp, heads_here, event_count, block, c * chunk_rows),
            [smem_spec()] + [vmem_spec()] * 2 + [hbm_spec()] + [vmem_spec()] * n_dp,
            [vmem_spec()] + [hbm_spec()] * 2,
            [rows_shape] + [pltpu.HBM((chunk_rows, cols_here), bf16)] * 2,
            [
                pltpu.VMEM((chunk_rows, width), bf16),
                pltpu.VMEM((chunk_sessions, heads_here, head_dim, head_dim), f32),
                decay_shape,
                pltpu.VMEM((chunk_rows, cols_here), bf16),
                pltpu.VMEM((chunk_rows, cols_here), bf16),
                pltpu.VMEM((4, 16 if split else width, cols_here), bf16),
                pltpu.SemaphoreType.DMA((3,)),
            ],
            2 * chunk_rows * width * cols_here * 4,
            limit_mib=12,
        )(ids, small, tokens, *in_hbm([past_states]), *proj_pieces)
        gated.append([g])
        keys.append(k)
        values.append(v)
    for _ in range(n_tensor - 1):
        for c in range(CHUNKS):
            gated[c].append(lax.ppermute(gated[c][-1], "tensor", ring))

    near = xor_gather(half_own, "dp", last_bit=2)[1:]
    swap = [(0, 1), (1, 0)]
    far = []
    for k, piece in enumerate(near):
        far.append(lax.ppermute(piece, "group", swap))
    beside = [(i, i ^ 1) for i in range(n_dp)]

    def to_beside(value):
        return lax.ppermute(value, "dp", beside)

    ffn_pieces = [ffn_weights, to_beside(ffn_weights)]
    for side in (near, far):
        for k, piece in enumerate(side):
            ffn_pieces += [piece, to_beside(piece)]
    packed = kernel_call(
        functools.partial(state_kernel, CHUNKS, heads_here, event_count),
        [vmem_spec(), smem_spec()] + [hbm_spec()] * (1 + 2 * CHUNKS),
        hbm_spec(),
        pltpu.HBM((slot_count, heads_here, head_dim, head_dim), bf16),
        [
            pltpu.VMEM((sessions_here, heads_here, head_dim, head_dim), bf16),
            pltpu.VMEM((sessions_here, heads_here, head_dim, head_dim), f32),
            pltpu.VMEM((2 * CHUNKS, chunk_rows, cols_here), bf16),
            pltpu.SemaphoreType.DMA((sessions_here,)),
            pltpu.SemaphoreType.DMA((4,)),
            pltpu.SemaphoreType.DMA((2 * CHUNKS,)),
        ],
        2 * row_count * head_dim * cols_here,
    )(small, send_pos, *in_hbm([past_states, *keys, *values]))
    received = lax.all_to_all(packed, "dp", split_axis=0, concat_axis=0, tiled=True)

    owns, parts, sums = [], [], []
    for c in range(CHUNKS):
        own, *part = kernel_call(
            functools.partial(feed_kernel, n_dp, n_tensor, block, c * chunk_rows),
            [smem_spec()]
            + [vmem_spec()] * 2
            + [hbm_spec()] * (n_tensor - 1)
            + [vmem_spec()]
            + [hbm_spec()] * (3 * n_dp - 2),
            [hbm_spec()] * n_tensor,
            [pltpu.HBM((chunk_rows, share), f32)]
            + [pltpu.HBM((chunk_rows, share), bf16)] * (n_tensor - 1),
            [
                pltpu.VMEM((n_tensor, width, cols_here), bf16),
                pltpu.VMEM((2, width, units_here), bf16),
                pltpu.VMEM((chunk_rows, width), f32),
                pltpu.VMEM((n_tensor - 1, chunk_rows, cols_here), bf16),
                pltpu.VMEM((chunk_rows, share), f32),
                pltpu.VMEM((n_tensor - 1, chunk_rows, share), bf16),
                pltpu.VMEM((chunk_rows, width), bf16),
                pltpu.VMEM((chunk_rows, units_here), bf16),
                pltpu.SemaphoreType.DMA((3, n_dp)),
                pltpu.SemaphoreType.DMA((n_tensor,)),
                pltpu.SemaphoreType.DMA((n_tensor,)),
            ],
            2 * chunk_rows * width * (width + 2 * units_here),
        )(
            ids,
            small,
            tokens,
            *in_hbm(gated[c][:-1]),
            gated[c][-1],
            *in_hbm(out_pieces + ffn_pieces),
        )
        owns.append(own)
        parts.append(part)
        sums.append(None)
    for hop in range(n_tensor - 1):
        for c in range(CHUNKS):
            mine = parts[c][hop]
            if hop:
                mine = kernel_call(
                    add_kernel,
                    [vmem_spec()] * 2,
                    vmem_spec(),
                    shape_of((chunk_rows, share), bf16),
                    [],
                    0,
                    limit_mib=4,
                )(sums[c], mine)
            sums[c] = lax.ppermute(mine, "tensor", ring)

    so_far = []
    for c in range(CHUNKS):
        so_far = [
            pl.pallas_call(
                functools.partial(last_kernel, event_count, c * chunk_rows),
                in_specs=[smem_spec()] + [vmem_spec()] * 2 + [hbm_spec()] * len(so_far),
                out_specs=hbm_spec(),
                out_shape=shape_of((row_count, share), bf16),
                scratch_shapes=[
                    pltpu.VMEM((chunk_rows, share), bf16),
                    pltpu.SemaphoreType.DMA,
                ],
                input_output_aliases={3: 0} if so_far else {},
                compiler_params=pltpu.CompilerParams(vmem_limit_bytes=8 * 1024 * 1024),
                cost_estimate=pl.CostEstimate(
                    flops=0, bytes_accessed=chunk_rows * share * 8, transcendentals=0
                ),
                name="last",
            )(end_lengths, owns[c], sums[c], *so_far)
        ]
    (next_tokens,) = so_far

    per_step = min(8, sessions_here)
    moved_states = pl.pallas_call(
        unpack_kernel,
        grid=(sessions_here // per_step,),
        in_specs=[smem_spec(), any_spec()],
        out_specs=pl.BlockSpec((per_step, heads_here, head_dim, head_dim), lambda i: (i, 0, 0, 0)),
        out_shape=shape_of(past_states.shape, f32),
        scratch_shapes=[
            pltpu.VMEM((sessions_here, heads_here, head_dim, head_dim), bf16),
            pltpu.SemaphoreType.DMA((sessions_here,)),
        ],
        compiler_params=pltpu.CompilerParams(vmem_limit_bytes=16 * 1024 * 1024),
        cost_estimate=pl.CostEstimate(
            flops=0, bytes_accessed=past_states.size * 6, transcendentals=0
        ),
        name="unpack",
    )(recv_src, received)
    return (next_tokens, moved_states)


def solution(mesh):
    placed = (
        P(("group", "dp"), None),
        P(("group", "dp"), "tensor", None, None),
        P(None, "dp", "tensor"),
        P(None, "dp", "tensor"),
        P(),
        P(),
        P(("group", "dp")),
        P(("group", "dp")),
    )

    return jax.shard_map(
        per_device,
        mesh=mesh,
        in_specs=placed,
        out_specs=(P(("group", "dp"), "tensor"), P(("group", "dp"), "tensor", None, None)),
        check_vma=False,
    )
```

```python
import functools
import jax
import jax.numpy as jnp
from jax import lax
from jax.experimental import pallas as pl
from jax.experimental.pallas import tpu as pltpu
from jax.sharding import PartitionSpec as P

CHUNKS = 2
BLOCK_ROWS = 256


NT = (((1,), (1,)), ((), ()))


def dot_nt(a, b):
    return lax.dot_general(a, b, NT, preferred_element_type=jnp.float32)


def dot_nn(a, b):
    return jnp.dot(a, b, preferred_element_type=jnp.float32)


def rms_scale(values, gain_row):
    meansq = jnp.mean(values * values, axis=-1, keepdims=True)
    return (values * lax.rsqrt(meansq + 1e-05) * gain_row).astype(jnp.bfloat16)


def piece_copies(pieces, dest, sems, me, pick):
    copies = []
    rows = dest.shape[-2] // len(pieces)
    for k, piece in enumerate(pieces):
        start = pl.multiple_of(jnp.bitwise_xor(me, k) * rows, rows)
        copies.append(
            pltpu.make_async_copy(pick(piece), dest.at[..., pl.ds(start, rows), :], sems.at[k])
        )
    return copies


def project_kernel(n_dp, heads, event_count, block, base, *refs):
    ids_ref, small_ref, tok_ref, past_hbm = refs[:4]
    pieces = refs[4 : 4 + n_dp]
    gated_ref, key_hbm, value_hbm = refs[4 + n_dp : 7 + n_dp]
    normed_ref, past_ref, decay_ref, key_ref, value_ref, w_ref, sems = refs[7 + n_dp :]
    past_copy = pltpu.make_async_copy(
        past_hbm.at[pl.ds(base // event_count, past_ref.shape[0])], past_ref, sems.at[0]
    )
    past_copy.start()
    out_copies = [
        pltpu.make_async_copy(key_ref, key_hbm, sems.at[1]),
        pltpu.make_async_copy(value_ref, value_hbm, sems.at[2]),
    ]
    rows, _ = gated_ref.shape
    head_dim = past_ref.shape[3]
    sessions = block // event_count
    key_scale = head_dim ** (-0.5)
    depth = tok_ref.shape[1] // n_dp
    starts = [pl.multiple_of(jnp.bitwise_xor(ids_ref[0], k) * depth, depth) for k in range(n_dp)]
    split = depth % 128 == 0
    if not split:
        for m in range(4):
            for k in range(n_dp):
                w_ref[m, pl.ds(starts[k], depth), :] = pieces[k][m * depth : (m + 1) * depth]
    at = lax.broadcasted_iota(jnp.int32, (block, block), 0)
    to = lax.broadcasted_iota(jnp.int32, (block, block), 1)
    allowed = (at // event_count == to // event_count) & (at >= to)
    distance = jnp.maximum(at - to, 0).astype(jnp.float32)
    place = lax.broadcasted_iota(jnp.int32, (block, head_dim), 0) % event_count
    since = (place + 1).astype(jnp.float32)
    factors = []
    for h in range(heads):
        rate = small_ref[2 + h : 3 + h, :]
        decay_ref[h] = jnp.where(allowed, jnp.exp(-rate[:, :block] * distance), 0.0) * key_scale
        factors.append(jnp.exp(-rate[:, :head_dim] * since))

    def product(span, m):
        if not split:
            return dot_nn(normed_ref[span], w_ref[m])
        total = None
        for k in range(n_dp):
            term = dot_nn(
                normed_ref[span, pl.ds(starts[k], depth)], pieces[k][m * depth : (m + 1) * depth]
            )
            total = term if total is None else total + term
        return total

    for r in range(0, rows, block):
        span = slice(r, r + block)
        normed_ref[span] = rms_scale(
            tok_ref[base + r : base + r + block].astype(jnp.float32), small_ref[0:1, :]
        )
        query = product(span, 0).astype(jnp.bfloat16)
        keys = product(span, 1).astype(jnp.bfloat16)
        key_ref[span] = keys
        values = product(span, 2).astype(jnp.bfloat16)
        value_ref[span] = values
        gate = product(span, 3)
        if r == 0:
            past_copy.wait()
        if r + block == rows:
            for copy in out_copies:
                copy.start()
        first_session = r // event_count
        for h in range(heads):
            cols = slice(h * head_dim, (h + 1) * head_dim)
            qh, kh, vh = query[:, cols], keys[:, cols], values[:, cols]
            mix = (dot_nt(qh, kh) * decay_ref[h]).astype(jnp.bfloat16)
            intra = dot_nn(mix, vh)
            parts = []
            for s in range(sessions):
                parts.append(
                    dot_nn(
                        qh[s * event_count : (s + 1) * event_count],
                        past_ref[first_session + s, h].astype(jnp.bfloat16),
                    )
                )
            retained = intra + jnp.concatenate(parts, axis=0) * factors[h]
            centred = retained - jnp.mean(retained, axis=-1, keepdims=True)
            row_var = jnp.mean(centred * centred, axis=-1, keepdims=True)
            normalised = centred * lax.rsqrt(row_var + 1e-05)
            gated_ref[span, cols] = (jax.nn.silu(gate[:, cols]) * normalised).astype(jnp.bfloat16)
    for copy in out_copies:
        copy.wait()


def state_kernel(chunks, heads, event_count, *refs):
    small_ref, pos_ref, past_hbm = refs[:3]
    sources = refs[3 : 3 + 2 * chunks]
    out_ref, buf_ref, past_ref, kv_ref, sems, past_sems, kv_sems = refs[3 + 2 * chunks :]
    kv_copies = [
        pltpu.make_async_copy(source, kv_ref.at[k], kv_sems.at[k])
        for k, source in enumerate(sources)
    ]
    for copy in kv_copies:
        copy.start()
    sessions, _, head_dim, _ = past_ref.shape
    groups = past_sems.shape[0]
    group = sessions // groups
    past_copies = [
        pltpu.make_async_copy(
            past_hbm.at[pl.ds(k * group, group)],
            past_ref.at[pl.ds(k * group, group)],
            past_sems.at[k],
        )
        for k in range(groups)
    ]
    for copy in past_copies:
        copy.start()
    rows = kv_ref.shape[1]
    key_scale = head_dim ** (-0.5)

    def copy_of(session):
        return pltpu.make_async_copy(
            buf_ref.at[session], out_ref.at[pos_ref[session]], sems.at[session]
        )

    place = lax.broadcasted_iota(jnp.int32, (rows, head_dim), 0) % event_count
    left = (event_count - 1 - place).astype(jnp.float32)
    factors, carries = [], []
    for h in range(heads):
        rate = small_ref[2 + h : 3 + h, :head_dim]
        factors.append(jnp.exp(-rate * left) * key_scale)
        carries.append(jnp.exp(-rate * event_count))
    for c in range(chunks):
        kv_copies[c].wait()
        kv_copies[chunks + c].wait()
        weighted = []
        for h in range(heads):
            cols = slice(h * head_dim, (h + 1) * head_dim)
            weighted.append(
                (kv_ref[c, :, cols].astype(jnp.float32) * factors[h]).astype(jnp.bfloat16)
            )
        for s in range(rows // event_count):
            session = c * (rows // event_count) + s
            if session % group == 0:
                past_copies[session // group].wait()
            span = slice(s * event_count, (s + 1) * event_count)
            for h in range(heads):
                cols = slice(h * head_dim, (h + 1) * head_dim)
                grown = lax.dot_general(
                    weighted[h][span],
                    kv_ref[chunks + c, span, cols],
                    (((0,), (0,)), ((), ())),
                    preferred_element_type=jnp.float32,
                )
                buf_ref[session, h] = (carries[h] * past_ref[session, h] + grown).astype(
                    jnp.bfloat16
                )

            @pl.when(pos_ref[session] >= 0)
            def _():
                copy_of(session).start()

    for session in range(sessions):

        @pl.when(pos_ref[session] >= 0)
        def _():
            copy_of(session).wait()


def unpack_kernel(src_ref, recv_ref, out_ref, buf_ref, sems):
    per_step = out_ref.shape[0]
    step = pl.program_id(0)

    def copy_of(slot):
        return pltpu.make_async_copy(
            recv_ref.at[jnp.maximum(src_ref[slot], 0)], buf_ref.at[slot], sems.at[slot]
        )

    @pl.when(step == 0)
    def _():
        for slot in range(buf_ref.shape[0]):

            @pl.when(src_ref[slot] >= 0)
            def _():
                copy_of(slot).start()

    for i in range(per_step):
        slot = step * per_step + i

        @pl.when(src_ref[slot] >= 0)
        def _():
            copy_of(slot).wait()
            out_ref[i] = buf_ref[slot].astype(jnp.float32)

        @pl.when(src_ref[slot] < 0)
        def _():
            out_ref[i] = jnp.zeros(out_ref.shape[1:], jnp.float32)


def feed_kernel(n_dp, n_tensor, block, base, *refs):
    ids_ref, small_ref, tok_ref = refs[:3]
    gated_hbm = refs[3 : 3 + n_tensor]
    at = 3 + n_tensor
    out_pieces = refs[at : at + n_dp]
    at += n_dp
    pairs = refs[at : at + 2]
    near = refs[at + 2 : at + n_dp]
    far = refs[at + n_dp : at + 2 * n_dp - 2]
    at += 2 * n_dp - 2
    own_hbm, *part_hbm = refs[at : at + n_tensor]
    wo_ref, ffn_ref, res_ref, gated, own_ref, part_ref, hid_ref, act_ref = refs[
        at + n_tensor : -3
    ]
    sems, gated_sems, done_sems = refs[-3:]
    rows, width = own_ref.shape
    me, group = ids_ref[0], ids_ref[2 + n_tensor]
    out_copies = piece_copies(
        out_pieces, wo_ref, sems.at[0], me, lambda piece: piece.at[:, pl.ds(0, wo_ref.shape[1] // n_dp)]
    )
    depth = ffn_ref.shape[1] // n_dp

    def ffn_copy(source, half, k):
        start = pl.multiple_of(jnp.bitwise_xor(me, k) * depth, depth)
        return pltpu.make_async_copy(
            source, ffn_ref.at[half, pl.ds(start, depth)], sems.at[1 + half, k]
        )

    up_copies = [ffn_copy(pairs[k].at[0], 0, k) for k in range(2)]
    down_copies = [ffn_copy(pairs[k].at[1], 1, k) for k in range(2)]
    rest = []
    for k in range(2, n_dp):
        near_rows = near[k - 2].at[pl.ds(0, depth)]
        rest.append(ffn_copy(near_rows, group, k))
        rest.append(ffn_copy(far[k - 2].at[pl.ds(0, depth)], 1 - group, k))
        up_copies.append(ffn_copy(near_rows, 0, k))
        down_copies.append(ffn_copy(near_rows, 1, k))
    gated_copies = [
        pltpu.make_async_copy(source, gated.at[k], gated_sems.at[k])
        for k, source in enumerate(gated_hbm[:-1])
    ]
    done_copies = [pltpu.make_async_copy(own_ref, own_hbm, done_sems.at[0])]
    for k in range(1, n_tensor):
        done_copies.append(
            pltpu.make_async_copy(part_ref.at[k - 1], part_hbm[k - 1], done_sems.at[k])
        )
    here = [gated.at[k] for k in range(n_tensor - 1)] + [gated_hbm[-1]]
    for copy in out_copies + gated_copies:
        copy.start()
    for copy in up_copies[:2] + rest:
        copy.start()
    for copy in out_copies + gated_copies:
        copy.wait()
    for copy in down_copies[:2]:
        copy.start()
    for r in range(0, rows, block):
        span = slice(r, r + block)
        attended = dot_nt(here[0][span], wo_ref[ids_ref[2]])
        for k in range(1, n_tensor):
            attended += dot_nt(here[k][span], wo_ref[ids_ref[2 + k]])
        residual = tok_ref[base + r : base + r + block].astype(jnp.float32) + attended
        res_ref[span] = residual
        hid_ref[span] = rms_scale(residual, small_ref[1:2, :])
    for copy in up_copies:
        copy.wait()
    for r in range(0, rows, block):
        span = slice(r, r + block)
        activated = jax.nn.gelu(dot_nn(hid_ref[span], ffn_ref[0]), approximate=True)
        act_ref[span] = activated.astype(jnp.bfloat16)
    for copy in down_copies:
        copy.wait()

    def term(k):
        start = pl.multiple_of(ids_ref[2 + k] * width, width)
        return dot_nt(act_ref[...], ffn_ref[1, pl.ds(start, width), :])

    mine = pl.ds(pl.multiple_of(ids_ref[1] * width, width), width)
    own_ref[...] = res_ref[:, mine] + term(0)
    done_copies[0].start()
    for k in list(range(2, n_tensor)) + [1]:
        part_ref[k - 1] = term(k).astype(jnp.bfloat16)
        done_copies[k].start()
    for copy in done_copies:
        copy.wait()


def add_kernel(a_ref, b_ref, out_ref):
    total = a_ref[...].astype(jnp.float32) + b_ref[...].astype(jnp.float32)
    out_ref[...] = total.astype(jnp.bfloat16)


def last_kernel(event_count, base, *refs):
    lengths_ref, own_ref, term_ref = refs[:3]
    out_hbm, out_ref, sem = refs[-3:]
    rows, width = own_ref.shape
    place = lax.broadcasted_iota(jnp.int32, (event_count, width), 0)
    for s in range(rows // event_count):
        span = slice(s * event_count, (s + 1) * event_count)
        total = own_ref[span] + term_ref[span].astype(jnp.float32)
        keep = place < lengths_ref[base // event_count + s]
        out_ref[span] = jnp.where(keep, total, 0.0).astype(jnp.bfloat16)
    copy = pltpu.make_async_copy(out_ref, out_hbm.at[pl.ds(base, rows)], sem)
    copy.start()
    copy.wait()


def xor_gather(value, axis, last_bit=1):
    pieces = [value]
    size = lax.axis_size(axis)
    bit = size // 2
    order = [0]
    while bit >= last_bit:
        pairs = [(i, i ^ bit) for i in range(size)]
        arrived = []
        for piece in pieces:
            arrived.append(lax.ppermute(piece, axis, pairs))
        pieces = pieces + arrived
        order = order + [k ^ bit for k in order]
        bit //= 2
    return [pieces[order.index(k)] for k in range(0, size, last_bit)]


def ring_order(size):
    return list(range(0, size, 2)) + list(range(1, size, 2))[::-1]


def ring_pairs(size):
    order = ring_order(size)
    return [(order[i], order[(i + 1) % size]) for i in range(size)]


def ring_sources(size):
    order = ring_order(size)
    return [[order[(order.index(at) - k) % size] for k in range(size)] for at in range(size)]


def any_spec():
    return pl.BlockSpec(memory_space=pl.ANY)


def smem_spec():
    return pl.BlockSpec(memory_space=pltpu.SMEM)


def hbm_spec():
    return pl.BlockSpec(memory_space=pltpu.HBM)


def in_hbm(arrays):
    return [pltpu.with_memory_space_constraint(array, pltpu.HBM) for array in arrays]


def vmem_spec():
    return pl.BlockSpec(memory_space=pltpu.VMEM)


def kernel_call(kernel, in_specs, out_specs, out_shape, scratch, flops, limit_mib=24):
    return pl.pallas_call(
        kernel,
        in_specs=in_specs,
        out_specs=out_specs,
        out_shape=out_shape,
        scratch_shapes=scratch,
        compiler_params=pltpu.CompilerParams(vmem_limit_bytes=limit_mib * 1024 * 1024),
        cost_estimate=pl.CostEstimate(
            flops=flops, bytes_accessed=4 * 1024 * 1024, transcendentals=0
        ),
    )


def per_device(
    tokens, past_states, attn_weights, ffn_weights, norm_gains, head_rates, end_lengths, new_slot
):
    sessions_here = end_lengths.shape[0]
    row_count, width = tokens.shape
    event_count = row_count // sessions_here
    heads_here, head_dim = past_states.shape[1], past_states.shape[3]
    cols_here = heads_here * head_dim
    units_here = ffn_weights.shape[2]
    n_dp, n_tensor = lax.axis_size("dp"), lax.axis_size("tensor")
    dp_at, tensor_at = lax.axis_index("dp"), lax.axis_index("tensor")
    share = width // n_tensor
    pair_cap = max(2, 2 * sessions_here // n_dp)
    slot_count = n_dp * pair_cap
    chunk_rows = row_count // CHUNKS
    block = min(BLOCK_ROWS, chunk_rows)
    ring = ring_pairs(n_tensor)
    bf16, f32 = jnp.bfloat16, jnp.float32
    shape_of = jax.ShapeDtypeStruct

    survive = end_lengths > event_count
    target_dev = new_slot // sessions_here
    session_ids = jnp.arange(sessions_here, dtype=jnp.int32)
    proj_rows = attn_weights.shape[1]
    proj_own = attn_weights[:4].reshape(4 * proj_rows, cols_here)
    proj_pieces = xor_gather(proj_own, "dp")
    note_rows = 16
    notes = jnp.stack([jnp.where(survive, target_dev, -1), new_slot % sessions_here])
    notes = jnp.pad(
        notes.astype(bf16), ((0, note_rows - 2), (0, units_here - sessions_here))
    )
    half_own = lax.dynamic_index_in_dim(
        ffn_weights, lax.axis_index("group"), 0, keepdims=False
    )
    half_own = jnp.concatenate([half_own, notes])
    out_own = lax.all_to_all(
        jnp.broadcast_to(attn_weights[4:], (n_tensor, proj_rows, cols_here)),
        "tensor",
        split_axis=0,
        concat_axis=0,
        tiled=True,
    )
    sources = jnp.array(ring_sources(n_tensor), jnp.int32)[tensor_at]
    places = jnp.stack([dp_at, tensor_at]).astype(jnp.int32)
    group_at = lax.axis_index("group").astype(jnp.int32)
    ids = jnp.concatenate([places, sources, group_at[None]])
    head_decay = lax.dynamic_slice_in_dim(head_rates, tensor_at * heads_here, heads_here)
    small = jnp.concatenate(
        [norm_gains, jnp.broadcast_to(head_decay[:, None], (heads_here, width))]
    )
    out_pieces = xor_gather(out_own, "dp")

    near = xor_gather(half_own, "dp", last_bit=2)[1:]
    swap = [(0, 1), (1, 0)]
    far = []
    for k, piece in enumerate(near):
        far.append(lax.ppermute(piece, "group", swap))
    beside = [(i, i ^ 1) for i in range(n_dp)]

    def to_beside(value):
        return lax.ppermute(value, "dp", beside)

    ffn_pieces = [ffn_weights, to_beside(ffn_weights)]
    noted = [notes[:2, :sessions_here], to_beside(notes[:, :128])[:2, :sessions_here]]
    for name, side in (("near", near), ("far", far)):
        for k, piece in enumerate(side):
            ffn_pieces += [piece, to_beside(piece)]
            if name == "near":
                noted += [
                    side_piece[proj_rows : proj_rows + 2, :sessions_here]
                    for side_piece in ffn_pieces[-2:]
                ]
    earlier = (
        (target_dev[None, :] == target_dev[:, None])
        & survive[None, :]
        & (session_ids[None, :] < session_ids[:, None])
    )
    pair_rank = jnp.sum(earlier.astype(jnp.int32), axis=1)
    send_pos = jnp.where(survive, target_dev * pair_cap + pair_rank, -1)
    meta = jnp.stack(noted)
    meta = meta.astype(jnp.int32)
    from_dev = jnp.bitwise_xor(dp_at, jnp.arange(n_dp, dtype=jnp.int32))
    coming = meta[:, 0] == dp_at
    ahead = coming[:, None, :] & (session_ids[None, None, :] < session_ids[None, :, None])
    rank_all = jnp.sum(ahead.astype(jnp.int32), axis=2)
    from_pos = from_dev[:, None] * pair_cap + rank_all + 1
    lands = meta[:, 1][None] == session_ids[:, None, None]
    recv_src = jnp.sum(jnp.where(lands & coming[None], from_pos[None], 0), axis=(1, 2)) - 1

    rows_shape = shape_of((chunk_rows, cols_here), bf16)
    decay_shape = pltpu.VMEM((heads_here, block, block), f32)
    chunk_sessions = chunk_rows // event_count
    split = (width // n_dp) % 128 == 0
    gated, keys, values = [], [], []
    for c in range(CHUNKS):
        g, k, v = kernel_call(
            functools.partial(project_kernel, n_dp, heads_here, event_count, block, c * chunk_rows),
            [smem_spec()] + [vmem_spec()] * 2 + [hbm_spec()] + [vmem_spec()] * n_dp,
            [vmem_spec()] + [hbm_spec()] * 2,
            [rows_shape] + [pltpu.HBM((chunk_rows, cols_here), bf16)] * 2,
            [
                pltpu.VMEM((chunk_rows, width), bf16),
                pltpu.VMEM((chunk_sessions, heads_here, head_dim, head_dim), f32),
                decay_shape,
                pltpu.VMEM((chunk_rows, cols_here), bf16),
                pltpu.VMEM((chunk_rows, cols_here), bf16),
                pltpu.VMEM((4, 16 if split else width, cols_here), bf16),
                pltpu.SemaphoreType.DMA((3,)),
            ],
            2 * chunk_rows * width * cols_here * 4,
            limit_mib=12,
        )(ids, small, tokens, *in_hbm([past_states]), *proj_pieces)
        gated.append([g])
        keys.append(k)
        values.append(v)
    for _ in range(n_tensor - 1):
        for c in range(CHUNKS):
            gated[c].append(lax.ppermute(gated[c][-1], "tensor", ring))

    packed = kernel_call(
        functools.partial(state_kernel, CHUNKS, heads_here, event_count),
        [vmem_spec(), smem_spec()] + [hbm_spec()] * (1 + 2 * CHUNKS),
        hbm_spec(),
        pltpu.HBM((slot_count, heads_here, head_dim, head_dim), bf16),
        [
            pltpu.VMEM((sessions_here, heads_here, head_dim, head_dim), bf16),
            pltpu.VMEM((sessions_here, heads_here, head_dim, head_dim), f32),
            pltpu.VMEM((2 * CHUNKS, chunk_rows, cols_here), bf16),
            pltpu.SemaphoreType.DMA((sessions_here,)),
            pltpu.SemaphoreType.DMA((4,)),
            pltpu.SemaphoreType.DMA((2 * CHUNKS,)),
        ],
        2 * row_count * head_dim * cols_here,
    )(small, send_pos, *in_hbm([past_states, *keys, *values]))
    received = lax.all_to_all(packed, "dp", split_axis=0, concat_axis=0, tiled=True)

    owns, parts, sums = [], [], []
    for c in range(CHUNKS):
        own, *part = kernel_call(
            functools.partial(feed_kernel, n_dp, n_tensor, block, c * chunk_rows),
            [smem_spec()]
            + [vmem_spec()] * 2
            + [hbm_spec()] * (n_tensor - 1)
            + [vmem_spec()]
            + [hbm_spec()] * (3 * n_dp - 2),
            [hbm_spec()] * n_tensor,
            [pltpu.HBM((chunk_rows, share), f32)]
            + [pltpu.HBM((chunk_rows, share), bf16)] * (n_tensor - 1),
            [
                pltpu.VMEM((n_tensor, width, cols_here), bf16),
                pltpu.VMEM((2, width, units_here), bf16),
                pltpu.VMEM((chunk_rows, width), f32),
                pltpu.VMEM((n_tensor - 1, chunk_rows, cols_here), bf16),
                pltpu.VMEM((chunk_rows, share), f32),
                pltpu.VMEM((n_tensor - 1, chunk_rows, share), bf16),
                pltpu.VMEM((chunk_rows, width), bf16),
                pltpu.VMEM((chunk_rows, units_here), bf16),
                pltpu.SemaphoreType.DMA((3, n_dp)),
                pltpu.SemaphoreType.DMA((n_tensor,)),
                pltpu.SemaphoreType.DMA((n_tensor,)),
            ],
            2 * chunk_rows * width * (width + 2 * units_here),
        )(
            ids,
            small,
            tokens,
            *in_hbm(gated[c][:-1]),
            gated[c][-1],
            *in_hbm(out_pieces + ffn_pieces),
        )
        owns.append(own)
        parts.append(part)
        sums.append(None)
    for hop in range(n_tensor - 1):
        for c in range(CHUNKS):
            mine = parts[c][hop]
            if hop:
                mine = kernel_call(
                    add_kernel,
                    [vmem_spec()] * 2,
                    vmem_spec(),
                    shape_of((chunk_rows, share), bf16),
                    [],
                    0,
                    limit_mib=4,
                )(sums[c], mine)
            sums[c] = lax.ppermute(mine, "tensor", ring)

    so_far = []
    for c in range(CHUNKS):
        so_far = [
            pl.pallas_call(
                functools.partial(last_kernel, event_count, c * chunk_rows),
                in_specs=[smem_spec()] + [vmem_spec()] * 2 + [hbm_spec()] * len(so_far),
                out_specs=hbm_spec(),
                out_shape=shape_of((row_count, share), bf16),
                scratch_shapes=[
                    pltpu.VMEM((chunk_rows, share), bf16),
                    pltpu.SemaphoreType.DMA,
                ],
                input_output_aliases={3: 0} if so_far else {},
                compiler_params=pltpu.CompilerParams(vmem_limit_bytes=8 * 1024 * 1024),
                cost_estimate=pl.CostEstimate(
                    flops=0, bytes_accessed=chunk_rows * share * 8, transcendentals=0
                ),
                name="last",
            )(end_lengths, owns[c], sums[c], *so_far)
        ]
    (next_tokens,) = so_far

    per_step = min(8, sessions_here)
    moved_states = pl.pallas_call(
        unpack_kernel,
        grid=(sessions_here // per_step,),
        in_specs=[smem_spec(), any_spec()],
        out_specs=pl.BlockSpec((per_step, heads_here, head_dim, head_dim), lambda i: (i, 0, 0, 0)),
        out_shape=shape_of(past_states.shape, f32),
        scratch_shapes=[
            pltpu.VMEM((sessions_here, heads_here, head_dim, head_dim), bf16),
            pltpu.SemaphoreType.DMA((sessions_here,)),
        ],
        compiler_params=pltpu.CompilerParams(vmem_limit_bytes=16 * 1024 * 1024),
        cost_estimate=pl.CostEstimate(
            flops=0, bytes_accessed=past_states.size * 6, transcendentals=0
        ),
        name="unpack",
    )(recv_src, received)
    return (next_tokens, moved_states)


def solution(mesh):
    placed = (
        P(("group", "dp"), None),
        P(("group", "dp"), "tensor", None, None),
        P(None, "dp", "tensor"),
        P(None, "dp", "tensor"),
        P(),
        P(),
        P(("group", "dp")),
        P(("group", "dp")),
    )

    return jax.shard_map(
        per_device,
        mesh=mesh,
        in_specs=placed,
        out_specs=(P(("group", "dp"), "tensor"), P(("group", "dp"), "tensor", None, None)),
        check_vma=False,
    )
```

```python
import functools
import jax
import jax.numpy as jnp
from jax import lax
from jax.experimental import pallas as pl
from jax.experimental.pallas import tpu as pltpu
from jax.sharding import PartitionSpec as P

CHUNKS = 2
BLOCK_ROWS = 256


NT = (((1,), (1,)), ((), ()))


def dot_nt(a, b):
    return lax.dot_general(a, b, NT, preferred_element_type=jnp.float32)


def dot_nn(a, b):
    return jnp.dot(a, b, preferred_element_type=jnp.float32)


def rms_scale(values, gain_row):
    meansq = jnp.mean(values * values, axis=-1, keepdims=True)
    return (values * lax.rsqrt(meansq + 1e-05) * gain_row).astype(jnp.bfloat16)


def piece_copies(pieces, dest, sems, me, pick):
    copies = []
    rows = dest.shape[-2] // len(pieces)
    for k, piece in enumerate(pieces):
        start = pl.multiple_of(jnp.bitwise_xor(me, k) * rows, rows)
        copies.append(
            pltpu.make_async_copy(pick(piece), dest.at[..., pl.ds(start, rows), :], sems.at[k])
        )
    return copies


def project_kernel(n_dp, heads, event_count, block, base, *refs):
    rates_ref, gains_hbm, tok_ref, past_hbm = refs[:4]
    pieces = refs[4 : 4 + n_dp]
    gated_ref, key_hbm, value_hbm = refs[4 + n_dp : 7 + n_dp]
    normed_ref, past_ref, decay_ref, key_ref, value_ref, w_ref, gain_ref, sems = refs[7 + n_dp :]
    gain_copy = pltpu.make_async_copy(gains_hbm, gain_ref, sems.at[3])
    gain_copy.start()
    me = lax.axis_index("dp")
    first_head = lax.axis_index("tensor") * heads
    past_copy = pltpu.make_async_copy(
        past_hbm.at[pl.ds(base // event_count, past_ref.shape[0])], past_ref, sems.at[0]
    )
    past_copy.start()
    out_copies = [
        pltpu.make_async_copy(key_ref, key_hbm, sems.at[1]),
        pltpu.make_async_copy(value_ref, value_hbm, sems.at[2]),
    ]
    rows, _ = gated_ref.shape
    head_dim = past_ref.shape[3]
    sessions = block // event_count
    key_scale = head_dim ** (-0.5)
    depth = tok_ref.shape[1] // n_dp
    starts = [pl.multiple_of(jnp.bitwise_xor(me, k) * depth, depth) for k in range(n_dp)]
    split = depth % 128 == 0
    if not split:
        for m in range(4):
            for k in range(n_dp):
                w_ref[m, pl.ds(starts[k], depth), :] = pieces[k][m * depth : (m + 1) * depth]
    at = lax.broadcasted_iota(jnp.int32, (block, block), 0)
    to = lax.broadcasted_iota(jnp.int32, (block, block), 1)
    allowed = (at // event_count == to // event_count) & (at >= to)
    distance = jnp.maximum(at - to, 0).astype(jnp.float32)
    place = lax.broadcasted_iota(jnp.int32, (block, head_dim), 0) % event_count
    since = (place + 1).astype(jnp.float32)
    factors = []
    for h in range(heads):
        rate = rates_ref[first_head + h]
        decay_ref[h] = jnp.where(allowed, jnp.exp(-rate * distance), 0.0) * key_scale
        factors.append(jnp.exp(-rate * since))
    gain_copy.wait()

    def product(span, m):
        if not split:
            return dot_nn(normed_ref[span], w_ref[m])
        total = None
        for k in range(n_dp):
            term = dot_nn(
                normed_ref[span, pl.ds(starts[k], depth)], pieces[k][m * depth : (m + 1) * depth]
            )
            total = term if total is None else total + term
        return total

    for r in range(0, rows, block):
        span = slice(r, r + block)
        normed_ref[span] = rms_scale(
            tok_ref[base + r : base + r + block].astype(jnp.float32), gain_ref[0:1, :]
        )
        query = product(span, 0).astype(jnp.bfloat16)
        keys = product(span, 1).astype(jnp.bfloat16)
        key_ref[span] = keys
        values = product(span, 2).astype(jnp.bfloat16)
        value_ref[span] = values
        gate = product(span, 3)
        if r == 0:
            past_copy.wait()
        if r + block == rows:
            for copy in out_copies:
                copy.start()
        first_session = r // event_count
        for h in range(heads):
            cols = slice(h * head_dim, (h + 1) * head_dim)
            qh, kh, vh = query[:, cols], keys[:, cols], values[:, cols]
            mix = (dot_nt(qh, kh) * decay_ref[h]).astype(jnp.bfloat16)
            intra = dot_nn(mix, vh)
            parts = []
            for s in range(sessions):
                parts.append(
                    dot_nn(
                        qh[s * event_count : (s + 1) * event_count],
                        past_ref[first_session + s, h].astype(jnp.bfloat16),
                    )
                )
            retained = intra + jnp.concatenate(parts, axis=0) * factors[h]
            centred = retained - jnp.mean(retained, axis=-1, keepdims=True)
            row_var = jnp.mean(centred * centred, axis=-1, keepdims=True)
            normalised = centred * lax.rsqrt(row_var + 1e-05)
            gated_ref[span, cols] = (jax.nn.silu(gate[:, cols]) * normalised).astype(jnp.bfloat16)
    for copy in out_copies:
        copy.wait()


def state_kernel(chunks, heads, event_count, *refs):
    rates_ref, pos_ref, past_hbm = refs[:3]
    first_head = lax.axis_index("tensor") * heads
    sources = refs[3 : 3 + 2 * chunks]
    out_ref, buf_ref, past_ref, kv_ref, sems, past_sems, kv_sems = refs[3 + 2 * chunks :]
    kv_copies = [
        pltpu.make_async_copy(source, kv_ref.at[k], kv_sems.at[k])
        for k, source in enumerate(sources)
    ]
    for copy in kv_copies:
        copy.start()
    sessions, _, head_dim, _ = past_ref.shape
    groups = past_sems.shape[0]
    group = sessions // groups
    past_copies = [
        pltpu.make_async_copy(
            past_hbm.at[pl.ds(k * group, group)],
            past_ref.at[pl.ds(k * group, group)],
            past_sems.at[k],
        )
        for k in range(groups)
    ]
    for copy in past_copies:
        copy.start()
    rows = kv_ref.shape[1]
    key_scale = head_dim ** (-0.5)

    def copy_of(session):
        return pltpu.make_async_copy(
            buf_ref.at[session], out_ref.at[pos_ref[session]], sems.at[session]
        )

    place = lax.broadcasted_iota(jnp.int32, (rows, head_dim), 0) % event_count
    left = (event_count - 1 - place).astype(jnp.float32)
    factors, carries = [], []
    for h in range(heads):
        rate = rates_ref[first_head + h]
        factors.append(jnp.exp(-rate * left) * key_scale)
        carries.append(jnp.exp(jnp.full((1, head_dim), -rate * event_count, jnp.float32)))
    for c in range(chunks):
        kv_copies[c].wait()
        kv_copies[chunks + c].wait()
        weighted = []
        for h in range(heads):
            cols = slice(h * head_dim, (h + 1) * head_dim)
            weighted.append(
                (kv_ref[c, :, cols].astype(jnp.float32) * factors[h]).astype(jnp.bfloat16)
            )
        for s in range(rows // event_count):
            session = c * (rows // event_count) + s
            if session % group == 0:
                past_copies[session // group].wait()
            span = slice(s * event_count, (s + 1) * event_count)
            for h in range(heads):
                cols = slice(h * head_dim, (h + 1) * head_dim)
                grown = lax.dot_general(
                    weighted[h][span],
                    kv_ref[chunks + c, span, cols],
                    (((0,), (0,)), ((), ())),
                    preferred_element_type=jnp.float32,
                )
                buf_ref[session, h] = (carries[h] * past_ref[session, h] + grown).astype(
                    jnp.bfloat16
                )

            @pl.when(pos_ref[session] >= 0)
            def _():
                copy_of(session).start()

    for session in range(sessions):

        @pl.when(pos_ref[session] >= 0)
        def _():
            copy_of(session).wait()


def unpack_kernel(src_ref, recv_ref, out_ref, buf_ref, sems):
    per_step = out_ref.shape[0]
    step = pl.program_id(0)

    def copy_of(slot):
        return pltpu.make_async_copy(
            recv_ref.at[jnp.maximum(src_ref[slot], 0)], buf_ref.at[slot], sems.at[slot]
        )

    @pl.when(step == 0)
    def _():
        for slot in range(buf_ref.shape[0]):

            @pl.when(src_ref[slot] >= 0)
            def _():
                copy_of(slot).start()

    for i in range(per_step):
        slot = step * per_step + i

        @pl.when(src_ref[slot] >= 0)
        def _():
            copy_of(slot).wait()
            out_ref[i] = buf_ref[slot].astype(jnp.float32)

        @pl.when(src_ref[slot] < 0)
        def _():
            out_ref[i] = jnp.zeros(out_ref.shape[1:], jnp.float32)


def feed_kernel(n_dp, n_tensor, block, base, *refs):
    gains_hbm, tok_ref = refs[:2]
    gated_hbm = refs[2 : 2 + n_tensor]
    at = 2 + n_tensor
    out_pieces = refs[at : at + n_dp]
    at += n_dp
    pairs = refs[at : at + 2]
    near = refs[at + 2 : at + n_dp]
    far = refs[at + n_dp : at + 2 * n_dp - 2]
    at += 2 * n_dp - 2
    own_hbm, *part_hbm = refs[at : at + n_tensor]
    wo_ref, ffn_ref, res_ref, gated, own_ref, part_ref, hid_ref, act_ref, gain_ref = refs[
        at + n_tensor : -3
    ]
    sems, gated_sems, done_sems = refs[-3:]
    rows, width = own_ref.shape
    me, group, here_at = (lax.axis_index(name) for name in ("dp", "group", "tensor"))
    table = ring_sources(n_tensor)
    sources = []
    for k in range(n_tensor):
        source = table[0][k]
        for at_k in range(1, n_tensor):
            source = jnp.where(here_at == at_k, table[at_k][k], source)
        sources.append(source)
    out_copies = piece_copies(
        out_pieces, wo_ref, sems.at[0], me, lambda piece: piece.at[:, pl.ds(0, wo_ref.shape[1] // n_dp)]
    )
    depth = ffn_ref.shape[1] // n_dp

    def ffn_copy(source, half, k):
        start = pl.multiple_of(jnp.bitwise_xor(me, k) * depth, depth)
        return pltpu.make_async_copy(
            source, ffn_ref.at[half, pl.ds(start, depth)], sems.at[1 + half, k]
        )

    up_copies = [ffn_copy(pairs[k].at[0], 0, k) for k in range(2)]
    down_copies = [ffn_copy(pairs[k].at[1], 1, k) for k in range(2)]
    rest = []
    for k in range(2, n_dp):
        near_rows = near[k - 2].at[pl.ds(0, depth)]
        rest.append(ffn_copy(near_rows, group, k))
        rest.append(ffn_copy(far[k - 2].at[pl.ds(0, depth)], 1 - group, k))
        up_copies.append(ffn_copy(near_rows, 0, k))
        down_copies.append(ffn_copy(near_rows, 1, k))
    gated_copies = [
        pltpu.make_async_copy(source, gated.at[k], gated_sems.at[k])
        for k, source in enumerate(gated_hbm[:-1])
    ]
    gated_copies.append(pltpu.make_async_copy(gains_hbm, gain_ref, gated_sems.at[n_tensor - 1]))
    done_copies = [pltpu.make_async_copy(own_ref, own_hbm, done_sems.at[0])]
    for k in range(1, n_tensor):
        done_copies.append(
            pltpu.make_async_copy(part_ref.at[k - 1], part_hbm[k - 1], done_sems.at[k])
        )
    here = [gated.at[k] for k in range(n_tensor - 1)] + [gated_hbm[-1]]
    for copy in out_copies + gated_copies:
        copy.start()
    for copy in up_copies[:2] + rest:
        copy.start()
    for copy in out_copies + gated_copies:
        copy.wait()
    for copy in down_copies[:2]:
        copy.start()
    for r in range(0, rows, block):
        span = slice(r, r + block)
        attended = dot_nt(here[0][span], wo_ref[sources[0]])
        for k in range(1, n_tensor):
            attended += dot_nt(here[k][span], wo_ref[sources[k]])
        residual = tok_ref[base + r : base + r + block].astype(jnp.float32) + attended
        res_ref[span] = residual
        hid_ref[span] = rms_scale(residual, gain_ref[1:2, :])
    for copy in up_copies:
        copy.wait()
    for r in range(0, rows, block):
        span = slice(r, r + block)
        activated = jax.nn.gelu(dot_nn(hid_ref[span], ffn_ref[0]), approximate=True)
        act_ref[span] = activated.astype(jnp.bfloat16)
    for copy in down_copies:
        copy.wait()

    def term(k):
        start = pl.multiple_of(sources[k] * width, width)
        return dot_nt(act_ref[...], ffn_ref[1, pl.ds(start, width), :])

    mine = pl.ds(pl.multiple_of(here_at * width, width), width)
    own_ref[...] = res_ref[:, mine] + term(0)
    done_copies[0].start()
    for k in list(range(2, n_tensor)) + [1]:
        part_ref[k - 1] = term(k).astype(jnp.bfloat16)
        done_copies[k].start()
    for copy in done_copies:
        copy.wait()


def add_kernel(a_ref, b_ref, out_ref):
    total = a_ref[...].astype(jnp.float32) + b_ref[...].astype(jnp.float32)
    out_ref[...] = total.astype(jnp.bfloat16)


def last_kernel(event_count, base, *refs):
    lengths_ref, own_ref, term_ref = refs[:3]
    out_hbm, out_ref, sem = refs[-3:]
    rows, width = own_ref.shape
    place = lax.broadcasted_iota(jnp.int32, (event_count, width), 0)
    for s in range(rows // event_count):
        span = slice(s * event_count, (s + 1) * event_count)
        total = own_ref[span] + term_ref[span].astype(jnp.float32)
        keep = place < lengths_ref[base // event_count + s]
        out_ref[span] = jnp.where(keep, total, 0.0).astype(jnp.bfloat16)
    copy = pltpu.make_async_copy(out_ref, out_hbm.at[pl.ds(base, rows)], sem)
    copy.start()
    copy.wait()


def xor_gather(value, axis, last_bit=1):
    pieces = [value]
    size = lax.axis_size(axis)
    bit = size // 2
    order = [0]
    while bit >= last_bit:
        pairs = [(i, i ^ bit) for i in range(size)]
        arrived = []
        for piece in pieces:
            arrived.append(lax.ppermute(piece, axis, pairs))
        pieces = pieces + arrived
        order = order + [k ^ bit for k in order]
        bit //= 2
    return [pieces[order.index(k)] for k in range(0, size, last_bit)]


def ring_order(size):
    return list(range(0, size, 2)) + list(range(1, size, 2))[::-1]


def ring_pairs(size):
    order = ring_order(size)
    return [(order[i], order[(i + 1) % size]) for i in range(size)]


def ring_sources(size):
    order = ring_order(size)
    return [[order[(order.index(at) - k) % size] for k in range(size)] for at in range(size)]


def any_spec():
    return pl.BlockSpec(memory_space=pl.ANY)


def smem_spec():
    return pl.BlockSpec(memory_space=pltpu.SMEM)


def hbm_spec():
    return pl.BlockSpec(memory_space=pltpu.HBM)


def in_hbm(arrays):
    return [pltpu.with_memory_space_constraint(array, pltpu.HBM) for array in arrays]


def vmem_spec():
    return pl.BlockSpec(memory_space=pltpu.VMEM)


def kernel_call(kernel, in_specs, out_specs, out_shape, scratch, flops, limit_mib=24):
    return pl.pallas_call(
        kernel,
        in_specs=in_specs,
        out_specs=out_specs,
        out_shape=out_shape,
        scratch_shapes=scratch,
        compiler_params=pltpu.CompilerParams(vmem_limit_bytes=limit_mib * 1024 * 1024),
        cost_estimate=pl.CostEstimate(
            flops=flops, bytes_accessed=4 * 1024 * 1024, transcendentals=0
        ),
    )


def per_device(
    tokens, past_states, attn_weights, ffn_weights, norm_gains, head_rates, end_lengths, new_slot
):
    sessions_here = end_lengths.shape[0]
    row_count, width = tokens.shape
    event_count = row_count // sessions_here
    heads_here, head_dim = past_states.shape[1], past_states.shape[3]
    cols_here = heads_here * head_dim
    units_here = ffn_weights.shape[2]
    n_dp, n_tensor = lax.axis_size("dp"), lax.axis_size("tensor")
    dp_at = lax.axis_index("dp")
    share = width // n_tensor
    pair_cap = max(2, 2 * sessions_here // n_dp)
    slot_count = n_dp * pair_cap
    chunk_rows = row_count // CHUNKS
    block = min(BLOCK_ROWS, chunk_rows)
    ring = ring_pairs(n_tensor)
    bf16, f32 = jnp.bfloat16, jnp.float32
    shape_of = jax.ShapeDtypeStruct

    survive = end_lengths > event_count
    target_dev = new_slot // sessions_here
    session_ids = jnp.arange(sessions_here, dtype=jnp.int32)
    proj_rows = attn_weights.shape[1]
    proj_own = attn_weights[:4].reshape(4 * proj_rows, cols_here)
    proj_pieces = xor_gather(proj_own, "dp")
    note_rows = 16
    notes = jnp.stack([jnp.where(survive, target_dev, -1), new_slot % sessions_here])
    notes = jnp.pad(
        notes.astype(bf16), ((0, note_rows - 2), (0, units_here - sessions_here))
    )
    half_own = lax.dynamic_index_in_dim(
        ffn_weights, lax.axis_index("group"), 0, keepdims=False
    )
    half_own = jnp.concatenate([half_own, notes])
    out_own = lax.all_to_all(
        jnp.broadcast_to(attn_weights[4:], (n_tensor, proj_rows, cols_here)),
        "tensor",
        split_axis=0,
        concat_axis=0,
        tiled=True,
    )
    out_pieces = xor_gather(out_own, "dp")

    near = xor_gather(half_own, "dp", last_bit=2)[1:]
    swap = [(0, 1), (1, 0)]
    far = []
    for k, piece in enumerate(near):
        far.append(lax.ppermute(piece, "group", swap))
    beside = [(i, i ^ 1) for i in range(n_dp)]

    def to_beside(value):
        return lax.ppermute(value, "dp", beside)

    ffn_pieces = [ffn_weights, to_beside(ffn_weights)]
    noted = [notes[:2, :sessions_here], to_beside(notes[:, :128])[:2, :sessions_here]]
    for name, side in (("near", near), ("far", far)):
        for k, piece in enumerate(side):
            ffn_pieces += [piece, to_beside(piece)]
            if name == "near":
                noted += [
                    side_piece[proj_rows : proj_rows + 2, :sessions_here]
                    for side_piece in ffn_pieces[-2:]
                ]
    earlier = (
        (target_dev[None, :] == target_dev[:, None])
        & survive[None, :]
        & (session_ids[None, :] < session_ids[:, None])
    )
    pair_rank = jnp.sum(earlier.astype(jnp.int32), axis=1)
    send_pos = jnp.where(survive, target_dev * pair_cap + pair_rank, -1)
    meta = jnp.stack(noted)
    meta = meta.astype(jnp.int32)
    from_dev = jnp.bitwise_xor(dp_at, jnp.arange(n_dp, dtype=jnp.int32))
    coming = meta[:, 0] == dp_at
    ahead = coming[:, None, :] & (session_ids[None, None, :] < session_ids[None, :, None])
    rank_all = jnp.sum(ahead.astype(jnp.int32), axis=2)
    from_pos = from_dev[:, None] * pair_cap + rank_all + 1
    lands = meta[:, 1][None] == session_ids[:, None, None]
    recv_src = jnp.sum(jnp.where(lands & coming[None], from_pos[None], 0), axis=(1, 2)) - 1

    rows_shape = shape_of((chunk_rows, cols_here), bf16)
    decay_shape = pltpu.VMEM((heads_here, block, block), f32)
    chunk_sessions = chunk_rows // event_count
    split = (width // n_dp) % 128 == 0
    gated, keys, values = [], [], []
    for c in range(CHUNKS):
        g, k, v = kernel_call(
            functools.partial(project_kernel, n_dp, heads_here, event_count, block, c * chunk_rows),
            [smem_spec(), hbm_spec(), vmem_spec(), hbm_spec()] + [vmem_spec()] * n_dp,
            [vmem_spec()] + [hbm_spec()] * 2,
            [rows_shape] + [pltpu.HBM((chunk_rows, cols_here), bf16)] * 2,
            [
                pltpu.VMEM((chunk_rows, width), bf16),
                pltpu.VMEM((chunk_sessions, heads_here, head_dim, head_dim), f32),
                decay_shape,
                pltpu.VMEM((chunk_rows, cols_here), bf16),
                pltpu.VMEM((chunk_rows, cols_here), bf16),
                pltpu.VMEM((4, 16 if split else width, cols_here), bf16),
                pltpu.VMEM(norm_gains.shape, f32),
                pltpu.SemaphoreType.DMA((4,)),
            ],
            2 * chunk_rows * width * cols_here * 4,
            limit_mib=12,
        )(
            *in_hbm([head_rates, norm_gains]),
            tokens,
            *in_hbm([past_states]),
            *proj_pieces,
        )
        gated.append([g])
        keys.append(k)
        values.append(v)
    for _ in range(n_tensor - 1):
        for c in range(CHUNKS):
            gated[c].append(lax.ppermute(gated[c][-1], "tensor", ring))

    packed = kernel_call(
        functools.partial(state_kernel, CHUNKS, heads_here, event_count),
        [smem_spec()] * 2 + [hbm_spec()] * (1 + 2 * CHUNKS),
        hbm_spec(),
        pltpu.HBM((slot_count, heads_here, head_dim, head_dim), bf16),
        [
            pltpu.VMEM((sessions_here, heads_here, head_dim, head_dim), bf16),
            pltpu.VMEM((sessions_here, heads_here, head_dim, head_dim), f32),
            pltpu.VMEM((2 * CHUNKS, chunk_rows, cols_here), bf16),
            pltpu.SemaphoreType.DMA((sessions_here,)),
            pltpu.SemaphoreType.DMA((4,)),
            pltpu.SemaphoreType.DMA((2 * CHUNKS,)),
        ],
        2 * row_count * head_dim * cols_here,
    )(*in_hbm([head_rates]), send_pos, *in_hbm([past_states, *keys, *values]))
    received = lax.all_to_all(packed, "dp", split_axis=0, concat_axis=0, tiled=True)

    owns, parts, sums = [], [], []
    for c in range(CHUNKS):
        own, *part = kernel_call(
            functools.partial(feed_kernel, n_dp, n_tensor, block, c * chunk_rows),
            [hbm_spec(), vmem_spec()]
            + [hbm_spec()] * (n_tensor - 1)
            + [vmem_spec()]
            + [hbm_spec()] * (3 * n_dp - 2),
            [hbm_spec()] * n_tensor,
            [pltpu.HBM((chunk_rows, share), f32)]
            + [pltpu.HBM((chunk_rows, share), bf16)] * (n_tensor - 1),
            [
                pltpu.VMEM((n_tensor, width, cols_here), bf16),
                pltpu.VMEM((2, width, units_here), bf16),
                pltpu.VMEM((chunk_rows, width), f32),
                pltpu.VMEM((n_tensor - 1, chunk_rows, cols_here), bf16),
                pltpu.VMEM((chunk_rows, share), f32),
                pltpu.VMEM((n_tensor - 1, chunk_rows, share), bf16),
                pltpu.VMEM((chunk_rows, width), bf16),
                pltpu.VMEM((chunk_rows, units_here), bf16),
                pltpu.VMEM(norm_gains.shape, f32),
                pltpu.SemaphoreType.DMA((3, n_dp)),
                pltpu.SemaphoreType.DMA((n_tensor,)),
                pltpu.SemaphoreType.DMA((n_tensor,)),
            ],
            2 * chunk_rows * width * (width + 2 * units_here),
        )(
            *in_hbm([norm_gains]),
            tokens,
            *in_hbm(gated[c][:-1]),
            gated[c][-1],
            *in_hbm(out_pieces + ffn_pieces),
        )
        owns.append(own)
        parts.append(part)
        sums.append(None)
    for hop in range(n_tensor - 1):
        for c in range(CHUNKS):
            mine = parts[c][hop]
            if hop:
                mine = kernel_call(
                    add_kernel,
                    [vmem_spec()] * 2,
                    vmem_spec(),
                    shape_of((chunk_rows, share), bf16),
                    [],
                    0,
                    limit_mib=4,
                )(sums[c], mine)
            sums[c] = lax.ppermute(mine, "tensor", ring)

    so_far = []
    for c in range(CHUNKS):
        so_far = [
            pl.pallas_call(
                functools.partial(last_kernel, event_count, c * chunk_rows),
                in_specs=[smem_spec()] + [vmem_spec()] * 2 + [hbm_spec()] * len(so_far),
                out_specs=hbm_spec(),
                out_shape=shape_of((row_count, share), bf16),
                scratch_shapes=[
                    pltpu.VMEM((chunk_rows, share), bf16),
                    pltpu.SemaphoreType.DMA,
                ],
                input_output_aliases={3: 0} if so_far else {},
                compiler_params=pltpu.CompilerParams(vmem_limit_bytes=8 * 1024 * 1024),
                cost_estimate=pl.CostEstimate(
                    flops=0, bytes_accessed=chunk_rows * share * 8, transcendentals=0
                ),
                name="last",
            )(end_lengths, owns[c], sums[c], *so_far)
        ]
    (next_tokens,) = so_far

    per_step = min(8, sessions_here)
    moved_states = pl.pallas_call(
        unpack_kernel,
        grid=(sessions_here // per_step,),
        in_specs=[smem_spec(), any_spec()],
        out_specs=pl.BlockSpec((per_step, heads_here, head_dim, head_dim), lambda i: (i, 0, 0, 0)),
        out_shape=shape_of(past_states.shape, f32),
        scratch_shapes=[
            pltpu.VMEM((sessions_here, heads_here, head_dim, head_dim), bf16),
            pltpu.SemaphoreType.DMA((sessions_here,)),
        ],
        compiler_params=pltpu.CompilerParams(vmem_limit_bytes=16 * 1024 * 1024),
        cost_estimate=pl.CostEstimate(
            flops=0, bytes_accessed=past_states.size * 6, transcendentals=0
        ),
        name="unpack",
    )(recv_src, received)
    return (next_tokens, moved_states)


def solution(mesh):
    placed = (
        P(("group", "dp"), None),
        P(("group", "dp"), "tensor", None, None),
        P(None, "dp", "tensor"),
        P(None, "dp", "tensor"),
        P(),
        P(),
        P(("group", "dp")),
        P(("group", "dp")),
    )

    return jax.shard_map(
        per_device,
        mesh=mesh,
        in_specs=placed,
        out_specs=(P(("group", "dp"), "tensor"), P(("group", "dp"), "tensor", None, None)),
        check_vma=False,
    )
```

```python
import functools
import jax
import jax.numpy as jnp
from jax import lax
from jax.experimental import pallas as pl
from jax.experimental.pallas import tpu as pltpu
from jax.sharding import PartitionSpec as P

CHUNKS = 2
BLOCK_ROWS = 256


NT = (((1,), (1,)), ((), ()))


def dot_nt(a, b):
    return lax.dot_general(a, b, NT, preferred_element_type=jnp.float32)


def dot_nn(a, b):
    return jnp.dot(a, b, preferred_element_type=jnp.float32)


def rms_scale(values, gain_row):
    meansq = jnp.mean(values * values, axis=-1, keepdims=True)
    return (values * lax.rsqrt(meansq + 1e-05) * gain_row).astype(jnp.bfloat16)


def piece_copies(pieces, dest, sems, me, pick):
    copies = []
    rows = dest.shape[-2] // len(pieces)
    for k, piece in enumerate(pieces):
        start = pl.multiple_of(jnp.bitwise_xor(me, k) * rows, rows)
        copies.append(
            pltpu.make_async_copy(pick(piece), dest.at[..., pl.ds(start, rows), :], sems.at[k])
        )
    return copies


def project_kernel(n_dp, heads, event_count, block, base, *refs):
    rates_ref, gains_hbm, tok_ref, past_hbm = refs[:4]
    pieces = refs[4 : 4 + n_dp]
    gated_ref, key_hbm, value_hbm = refs[4 + n_dp : 7 + n_dp]
    normed_ref, past_ref, decay_ref, key_ref, value_ref, w_ref, gain_ref, sems = refs[7 + n_dp :]
    gain_copy = pltpu.make_async_copy(gains_hbm, gain_ref, sems.at[3])
    gain_copy.start()
    me = lax.axis_index("dp")
    first_head = lax.axis_index("tensor") * heads
    past_copy = pltpu.make_async_copy(
        past_hbm.at[pl.ds(base // event_count, past_ref.shape[0])], past_ref, sems.at[0]
    )
    past_copy.start()
    out_copies = [
        pltpu.make_async_copy(key_ref, key_hbm, sems.at[1]),
        pltpu.make_async_copy(value_ref, value_hbm, sems.at[2]),
    ]
    rows, _ = gated_ref.shape
    head_dim = past_ref.shape[3]
    sessions = block // event_count
    key_scale = head_dim ** (-0.5)
    depth = tok_ref.shape[1] // n_dp
    starts = [pl.multiple_of(jnp.bitwise_xor(me, k) * depth, depth) for k in range(n_dp)]
    split = depth % 128 == 0
    if not split:
        for m in range(4):
            for k in range(n_dp):
                w_ref[m, pl.ds(starts[k], depth), :] = pieces[k][m * depth : (m + 1) * depth]
    at = lax.broadcasted_iota(jnp.int32, (block, block), 0)
    to = lax.broadcasted_iota(jnp.int32, (block, block), 1)
    allowed = (at // event_count == to // event_count) & (at >= to)
    distance = jnp.maximum(at - to, 0).astype(jnp.float32)
    place = lax.broadcasted_iota(jnp.int32, (block, head_dim), 0) % event_count
    since = (place + 1).astype(jnp.float32)
    factors = []
    for h in range(heads):
        rate = rates_ref[first_head + h]
        decay_ref[h] = jnp.where(allowed, jnp.exp(-rate * distance), 0.0) * key_scale
        factors.append(jnp.exp(-rate * since))
    gain_copy.wait()

    def product(span, m):
        if not split:
            return dot_nn(normed_ref[span], w_ref[m])
        total = None
        for k in range(n_dp):
            term = dot_nn(
                normed_ref[span, pl.ds(starts[k], depth)], pieces[k][m * depth : (m + 1) * depth]
            )
            total = term if total is None else total + term
        return total

    for r in range(0, rows, block):
        span = slice(r, r + block)
        normed_ref[span] = rms_scale(
            tok_ref[base + r : base + r + block].astype(jnp.float32), gain_ref[0:1, :]
        )
        query = product(span, 0).astype(jnp.bfloat16)
        keys = product(span, 1).astype(jnp.bfloat16)
        key_ref[span] = keys
        values = product(span, 2).astype(jnp.bfloat16)
        value_ref[span] = values
        gate = product(span, 3)
        if r == 0:
            past_copy.wait()
        if r + block == rows:
            for copy in out_copies:
                copy.start()
        first_session = r // event_count
        for h in range(heads):
            cols = slice(h * head_dim, (h + 1) * head_dim)
            qh, kh, vh = query[:, cols], keys[:, cols], values[:, cols]
            mix = (dot_nt(qh, kh) * decay_ref[h]).astype(jnp.bfloat16)
            intra = dot_nn(mix, vh)
            parts = []
            for s in range(sessions):
                parts.append(
                    dot_nn(
                        qh[s * event_count : (s + 1) * event_count],
                        past_ref[first_session + s, h].astype(jnp.bfloat16),
                    )
                )
            retained = intra + jnp.concatenate(parts, axis=0) * factors[h]
            centred = retained - jnp.mean(retained, axis=-1, keepdims=True)
            row_var = jnp.mean(centred * centred, axis=-1, keepdims=True)
            normalised = centred * lax.rsqrt(row_var + 1e-05)
            gated_ref[span, cols] = (jax.nn.silu(gate[:, cols]) * normalised).astype(jnp.bfloat16)
    for copy in out_copies:
        copy.wait()


def state_kernel(chunks, heads, event_count, *refs):
    rates_ref, pos_ref, past_hbm = refs[:3]
    first_head = lax.axis_index("tensor") * heads
    sources = refs[3 : 3 + 2 * chunks]
    out_ref, buf_ref, past_ref, kv_ref, sems, past_sems, kv_sems = refs[3 + 2 * chunks :]
    kv_copies = [
        pltpu.make_async_copy(source, kv_ref.at[k], kv_sems.at[k])
        for k, source in enumerate(sources)
    ]
    for copy in kv_copies:
        copy.start()
    sessions, _, head_dim, _ = past_ref.shape
    groups = past_sems.shape[0]
    group = sessions // groups
    past_copies = [
        pltpu.make_async_copy(
            past_hbm.at[pl.ds(k * group, group)],
            past_ref.at[pl.ds(k * group, group)],
            past_sems.at[k],
        )
        for k in range(groups)
    ]
    for copy in past_copies:
        copy.start()
    rows = kv_ref.shape[1]
    key_scale = head_dim ** (-0.5)

    def copy_of(session):
        return pltpu.make_async_copy(
            buf_ref.at[session], out_ref.at[pos_ref[session]], sems.at[session]
        )

    place = lax.broadcasted_iota(jnp.int32, (rows, head_dim), 0) % event_count
    left = (event_count - 1 - place).astype(jnp.float32)
    factors, carries = [], []
    for h in range(heads):
        rate = rates_ref[first_head + h]
        factors.append(jnp.exp(-rate * left) * key_scale)
        carries.append(jnp.exp(jnp.full((1, head_dim), -rate * event_count, jnp.float32)))
    for c in range(chunks):
        kv_copies[c].wait()
        kv_copies[chunks + c].wait()
        weighted = []
        for h in range(heads):
            cols = slice(h * head_dim, (h + 1) * head_dim)
            weighted.append(
                (kv_ref[c, :, cols].astype(jnp.float32) * factors[h]).astype(jnp.bfloat16)
            )
        for s in range(rows // event_count):
            session = c * (rows // event_count) + s
            if session % group == 0:
                past_copies[session // group].wait()
            span = slice(s * event_count, (s + 1) * event_count)
            for h in range(heads):
                cols = slice(h * head_dim, (h + 1) * head_dim)
                grown = lax.dot_general(
                    weighted[h][span],
                    kv_ref[chunks + c, span, cols],
                    (((0,), (0,)), ((), ())),
                    preferred_element_type=jnp.float32,
                )
                buf_ref[session, h] = (carries[h] * past_ref[session, h] + grown).astype(
                    jnp.bfloat16
                )

            @pl.when(pos_ref[session] >= 0)
            def _():
                copy_of(session).start()

    for session in range(sessions):

        @pl.when(pos_ref[session] >= 0)
        def _():
            copy_of(session).wait()


def unpack_kernel(src_ref, recv_hbm, out_hbm, in_ref, out_ref, in_sems, out_sems):
    slots = in_ref.shape[0]

    def in_copy(slot):
        return pltpu.make_async_copy(
            recv_hbm.at[jnp.maximum(src_ref[slot], 0)], in_ref.at[slot], in_sems.at[slot]
        )

    def out_copy(slot):
        return pltpu.make_async_copy(out_ref.at[slot], out_hbm.at[slot], out_sems.at[slot])

    for slot in range(slots):

        @pl.when(src_ref[slot] >= 0)
        def _():
            in_copy(slot).start()

    for slot in range(slots):

        @pl.when(src_ref[slot] >= 0)
        def _():
            in_copy(slot).wait()
            out_ref[slot] = in_ref[slot].astype(jnp.float32)

        @pl.when(src_ref[slot] < 0)
        def _():
            out_ref[slot] = jnp.zeros(out_ref.shape[1:], jnp.float32)

        out_copy(slot).start()
    for slot in range(slots):
        out_copy(slot).wait()


def feed_kernel(n_dp, n_tensor, block, base, *refs):
    gains_hbm, tok_ref = refs[:2]
    gated_hbm = refs[2 : 2 + n_tensor]
    at = 2 + n_tensor
    out_pieces = refs[at : at + n_dp]
    at += n_dp
    pairs = refs[at : at + 2]
    near = refs[at + 2 : at + n_dp]
    far = refs[at + n_dp : at + 2 * n_dp - 2]
    at += 2 * n_dp - 2
    own_hbm, *part_hbm = refs[at : at + n_tensor]
    wo_ref, ffn_ref, res_ref, gated, own_ref, part_ref, hid_ref, act_ref, gain_ref = refs[
        at + n_tensor : -3
    ]
    sems, gated_sems, done_sems = refs[-3:]
    rows, width = own_ref.shape
    me, group, here_at = (lax.axis_index(name) for name in ("dp", "group", "tensor"))
    table = ring_sources(n_tensor)
    sources = []
    for k in range(n_tensor):
        source = table[0][k]
        for at_k in range(1, n_tensor):
            source = jnp.where(here_at == at_k, table[at_k][k], source)
        sources.append(source)
    out_copies = piece_copies(
        out_pieces, wo_ref, sems.at[0], me, lambda piece: piece.at[:, pl.ds(0, wo_ref.shape[1] // n_dp)]
    )
    depth = ffn_ref.shape[1] // n_dp

    def ffn_copy(source, half, k):
        start = pl.multiple_of(jnp.bitwise_xor(me, k) * depth, depth)
        return pltpu.make_async_copy(
            source, ffn_ref.at[half, pl.ds(start, depth)], sems.at[1 + half, k]
        )

    up_copies = [ffn_copy(pairs[k].at[0], 0, k) for k in range(2)]
    down_copies = [ffn_copy(pairs[k].at[1], 1, k) for k in range(2)]
    rest = []
    for k in range(2, n_dp):
        near_rows = near[k - 2].at[pl.ds(0, depth)]
        rest.append(ffn_copy(near_rows, group, k))
        rest.append(ffn_copy(far[k - 2].at[pl.ds(0, depth)], 1 - group, k))
        up_copies.append(ffn_copy(near_rows, 0, k))
        down_copies.append(ffn_copy(near_rows, 1, k))
    gated_copies = [
        pltpu.make_async_copy(source, gated.at[k], gated_sems.at[k])
        for k, source in enumerate(gated_hbm[:-1])
    ]
    gated_copies.append(pltpu.make_async_copy(gains_hbm, gain_ref, gated_sems.at[n_tensor - 1]))
    done_copies = [pltpu.make_async_copy(own_ref, own_hbm, done_sems.at[0])]
    for k in range(1, n_tensor):
        done_copies.append(
            pltpu.make_async_copy(part_ref.at[k - 1], part_hbm[k - 1], done_sems.at[k])
        )
    here = [gated.at[k] for k in range(n_tensor - 1)] + [gated_hbm[-1]]
    for copy in out_copies + gated_copies:
        copy.start()
    for copy in up_copies[:2] + rest:
        copy.start()
    for copy in out_copies + gated_copies:
        copy.wait()
    for copy in down_copies[:2]:
        copy.start()
    for r in range(0, rows, block):
        span = slice(r, r + block)
        attended = dot_nt(here[0][span], wo_ref[sources[0]])
        for k in range(1, n_tensor):
            attended += dot_nt(here[k][span], wo_ref[sources[k]])
        residual = tok_ref[base + r : base + r + block].astype(jnp.float32) + attended
        res_ref[span] = residual
        hid_ref[span] = rms_scale(residual, gain_ref[1:2, :])
    for copy in up_copies:
        copy.wait()
    for r in range(0, rows, block):
        span = slice(r, r + block)
        activated = jax.nn.gelu(dot_nn(hid_ref[span], ffn_ref[0]), approximate=True)
        act_ref[span] = activated.astype(jnp.bfloat16)
    for copy in down_copies:
        copy.wait()

    def term(k):
        start = pl.multiple_of(sources[k] * width, width)
        return dot_nt(act_ref[...], ffn_ref[1, pl.ds(start, width), :])

    mine = pl.ds(pl.multiple_of(here_at * width, width), width)
    own_ref[...] = res_ref[:, mine] + term(0)
    done_copies[0].start()
    for k in list(range(2, n_tensor)) + [1]:
        part_ref[k - 1] = term(k).astype(jnp.bfloat16)
        done_copies[k].start()
    for copy in done_copies:
        copy.wait()


def add_kernel(a_ref, b_ref, out_ref):
    total = a_ref[...].astype(jnp.float32) + b_ref[...].astype(jnp.float32)
    out_ref[...] = total.astype(jnp.bfloat16)


def last_kernel(event_count, base, *refs):
    lengths_ref, own_ref, term_ref = refs[:3]
    out_hbm, out_ref, sem = refs[-3:]
    rows, width = own_ref.shape
    place = lax.broadcasted_iota(jnp.int32, (event_count, width), 0)
    for s in range(rows // event_count):
        span = slice(s * event_count, (s + 1) * event_count)
        total = own_ref[span] + term_ref[span].astype(jnp.float32)
        keep = place < lengths_ref[base // event_count + s]
        out_ref[span] = jnp.where(keep, total, 0.0).astype(jnp.bfloat16)
    copy = pltpu.make_async_copy(out_ref, out_hbm.at[pl.ds(base, rows)], sem)
    copy.start()
    copy.wait()


def xor_gather(value, axis, last_bit=1):
    pieces = [value]
    size = lax.axis_size(axis)
    bit = size // 2
    order = [0]
    while bit >= last_bit:
        pairs = [(i, i ^ bit) for i in range(size)]
        arrived = []
        for piece in pieces:
            arrived.append(lax.ppermute(piece, axis, pairs))
        pieces = pieces + arrived
        order = order + [k ^ bit for k in order]
        bit //= 2
    return [pieces[order.index(k)] for k in range(0, size, last_bit)]


def ring_order(size):
    return list(range(0, size, 2)) + list(range(1, size, 2))[::-1]


def ring_pairs(size):
    order = ring_order(size)
    return [(order[i], order[(i + 1) % size]) for i in range(size)]


def ring_sources(size):
    order = ring_order(size)
    return [[order[(order.index(at) - k) % size] for k in range(size)] for at in range(size)]


def smem_spec():
    return pl.BlockSpec(memory_space=pltpu.SMEM)


def hbm_spec():
    return pl.BlockSpec(memory_space=pltpu.HBM)


def in_hbm(arrays):
    return [pltpu.with_memory_space_constraint(array, pltpu.HBM) for array in arrays]


def vmem_spec():
    return pl.BlockSpec(memory_space=pltpu.VMEM)


def kernel_call(kernel, in_specs, out_specs, out_shape, scratch, flops, limit_mib=24):
    return pl.pallas_call(
        kernel,
        in_specs=in_specs,
        out_specs=out_specs,
        out_shape=out_shape,
        scratch_shapes=scratch,
        compiler_params=pltpu.CompilerParams(vmem_limit_bytes=limit_mib * 1024 * 1024),
        cost_estimate=pl.CostEstimate(
            flops=flops, bytes_accessed=4 * 1024 * 1024, transcendentals=0
        ),
    )


def per_device(
    tokens, past_states, attn_weights, ffn_weights, norm_gains, head_rates, end_lengths, new_slot
):
    sessions_here = end_lengths.shape[0]
    row_count, width = tokens.shape
    event_count = row_count // sessions_here
    heads_here, head_dim = past_states.shape[1], past_states.shape[3]
    cols_here = heads_here * head_dim
    units_here = ffn_weights.shape[2]
    n_dp, n_tensor = lax.axis_size("dp"), lax.axis_size("tensor")
    dp_at = lax.axis_index("dp")
    share = width // n_tensor
    pair_cap = max(2, 2 * sessions_here // n_dp)
    slot_count = n_dp * pair_cap
    chunk_rows = row_count // CHUNKS
    block = min(BLOCK_ROWS, chunk_rows)
    ring = ring_pairs(n_tensor)
    bf16, f32 = jnp.bfloat16, jnp.float32
    shape_of = jax.ShapeDtypeStruct

    survive = end_lengths > event_count
    target_dev = new_slot // sessions_here
    session_ids = jnp.arange(sessions_here, dtype=jnp.int32)
    proj_rows = attn_weights.shape[1]
    proj_own = attn_weights[:4].reshape(4 * proj_rows, cols_here)
    proj_pieces = xor_gather(proj_own, "dp")
    note_rows = 16
    notes = jnp.stack([jnp.where(survive, target_dev, -1), new_slot % sessions_here])
    notes = jnp.pad(
        notes.astype(bf16), ((0, note_rows - 2), (0, units_here - sessions_here))
    )
    half_own = lax.dynamic_index_in_dim(
        ffn_weights, lax.axis_index("group"), 0, keepdims=False
    )
    half_own = jnp.concatenate([half_own, notes])
    out_own = lax.all_to_all(
        jnp.broadcast_to(attn_weights[4:], (n_tensor, proj_rows, cols_here)),
        "tensor",
        split_axis=0,
        concat_axis=0,
        tiled=True,
    )
    out_pieces = xor_gather(out_own, "dp")

    near = xor_gather(half_own, "dp", last_bit=2)[1:]
    swap = [(0, 1), (1, 0)]
    far = []
    for k, piece in enumerate(near):
        far.append(lax.ppermute(piece, "group", swap))
    beside = [(i, i ^ 1) for i in range(n_dp)]

    def to_beside(value):
        return lax.ppermute(value, "dp", beside)

    ffn_pieces = [ffn_weights, to_beside(ffn_weights)]
    noted = [notes[:2, :sessions_here], to_beside(notes[:, :128])[:2, :sessions_here]]
    for name, side in (("near", near), ("far", far)):
        for k, piece in enumerate(side):
            ffn_pieces += [piece, to_beside(piece)]
            if name == "near":
                noted += [
                    side_piece[proj_rows : proj_rows + 2, :sessions_here]
                    for side_piece in ffn_pieces[-2:]
                ]
    earlier = (
        (target_dev[None, :] == target_dev[:, None])
        & survive[None, :]
        & (session_ids[None, :] < session_ids[:, None])
    )
    pair_rank = jnp.sum(earlier.astype(jnp.int32), axis=1)
    send_pos = jnp.where(survive, target_dev * pair_cap + pair_rank, -1)
    meta = jnp.stack(noted)
    meta = meta.astype(jnp.int32)
    from_dev = jnp.bitwise_xor(dp_at, jnp.arange(n_dp, dtype=jnp.int32))
    coming = meta[:, 0] == dp_at
    ahead = coming[:, None, :] & (session_ids[None, None, :] < session_ids[None, :, None])
    rank_all = jnp.sum(ahead.astype(jnp.int32), axis=2)
    from_pos = from_dev[:, None] * pair_cap + rank_all + 1
    lands = meta[:, 1][None] == session_ids[:, None, None]
    recv_src = jnp.sum(jnp.where(lands & coming[None], from_pos[None], 0), axis=(1, 2)) - 1

    rows_shape = shape_of((chunk_rows, cols_here), bf16)
    decay_shape = pltpu.VMEM((heads_here, block, block), f32)
    chunk_sessions = chunk_rows // event_count
    split = (width // n_dp) % 128 == 0
    gated, keys, values = [], [], []
    for c in range(CHUNKS):
        g, k, v = kernel_call(
            functools.partial(project_kernel, n_dp, heads_here, event_count, block, c * chunk_rows),
            [smem_spec(), hbm_spec(), vmem_spec(), hbm_spec()] + [vmem_spec()] * n_dp,
            [vmem_spec()] + [hbm_spec()] * 2,
            [rows_shape] + [pltpu.HBM((chunk_rows, cols_here), bf16)] * 2,
            [
                pltpu.VMEM((chunk_rows, width), bf16),
                pltpu.VMEM((chunk_sessions, heads_here, head_dim, head_dim), f32),
                decay_shape,
                pltpu.VMEM((chunk_rows, cols_here), bf16),
                pltpu.VMEM((chunk_rows, cols_here), bf16),
                pltpu.VMEM((4, 16 if split else width, cols_here), bf16),
                pltpu.VMEM(norm_gains.shape, f32),
                pltpu.SemaphoreType.DMA((4,)),
            ],
            2 * chunk_rows * width * cols_here * 4,
            limit_mib=12,
        )(
            *in_hbm([head_rates, norm_gains]),
            tokens,
            *in_hbm([past_states]),
            *proj_pieces,
        )
        gated.append([g])
        keys.append(k)
        values.append(v)
    for _ in range(n_tensor - 1):
        for c in range(CHUNKS):
            gated[c].append(lax.ppermute(gated[c][-1], "tensor", ring))

    packed = kernel_call(
        functools.partial(state_kernel, CHUNKS, heads_here, event_count),
        [smem_spec()] * 2 + [hbm_spec()] * (1 + 2 * CHUNKS),
        hbm_spec(),
        pltpu.HBM((slot_count, heads_here, head_dim, head_dim), bf16),
        [
            pltpu.VMEM((sessions_here, heads_here, head_dim, head_dim), bf16),
            pltpu.VMEM((sessions_here, heads_here, head_dim, head_dim), f32),
            pltpu.VMEM((2 * CHUNKS, chunk_rows, cols_here), bf16),
            pltpu.SemaphoreType.DMA((sessions_here,)),
            pltpu.SemaphoreType.DMA((4,)),
            pltpu.SemaphoreType.DMA((2 * CHUNKS,)),
        ],
        2 * row_count * head_dim * cols_here,
    )(*in_hbm([head_rates]), send_pos, *in_hbm([past_states, *keys, *values]))
    received = lax.all_to_all(packed, "dp", split_axis=0, concat_axis=0, tiled=True)

    owns, parts, sums = [], [], []
    for c in range(CHUNKS):
        own, *part = kernel_call(
            functools.partial(feed_kernel, n_dp, n_tensor, block, c * chunk_rows),
            [hbm_spec(), vmem_spec()]
            + [hbm_spec()] * (n_tensor - 1)
            + [vmem_spec()]
            + [hbm_spec()] * (3 * n_dp - 2),
            [hbm_spec()] * n_tensor,
            [pltpu.HBM((chunk_rows, share), f32)]
            + [pltpu.HBM((chunk_rows, share), bf16)] * (n_tensor - 1),
            [
                pltpu.VMEM((n_tensor, width, cols_here), bf16),
                pltpu.VMEM((2, width, units_here), bf16),
                pltpu.VMEM((chunk_rows, width), f32),
                pltpu.VMEM((n_tensor - 1, chunk_rows, cols_here), bf16),
                pltpu.VMEM((chunk_rows, share), f32),
                pltpu.VMEM((n_tensor - 1, chunk_rows, share), bf16),
                pltpu.VMEM((chunk_rows, width), bf16),
                pltpu.VMEM((chunk_rows, units_here), bf16),
                pltpu.VMEM(norm_gains.shape, f32),
                pltpu.SemaphoreType.DMA((3, n_dp)),
                pltpu.SemaphoreType.DMA((n_tensor,)),
                pltpu.SemaphoreType.DMA((n_tensor,)),
            ],
            2 * chunk_rows * width * (width + 2 * units_here),
        )(
            *in_hbm([norm_gains]),
            tokens,
            *in_hbm(gated[c][:-1]),
            gated[c][-1],
            *in_hbm(out_pieces + ffn_pieces),
        )
        owns.append(own)
        parts.append(part)
        sums.append(None)
    for hop in range(n_tensor - 1):
        for c in range(CHUNKS):
            mine = parts[c][hop]
            if hop:
                mine = kernel_call(
                    add_kernel,
                    [vmem_spec()] * 2,
                    vmem_spec(),
                    shape_of((chunk_rows, share), bf16),
                    [],
                    0,
                    limit_mib=4,
                )(sums[c], mine)
            sums[c] = lax.ppermute(mine, "tensor", ring)

    so_far = []
    for c in range(CHUNKS):
        so_far = [
            pl.pallas_call(
                functools.partial(last_kernel, event_count, c * chunk_rows),
                in_specs=[smem_spec()] + [vmem_spec()] * 2 + [hbm_spec()] * len(so_far),
                out_specs=hbm_spec(),
                out_shape=shape_of((row_count, share), bf16),
                scratch_shapes=[
                    pltpu.VMEM((chunk_rows, share), bf16),
                    pltpu.SemaphoreType.DMA,
                ],
                input_output_aliases={3: 0} if so_far else {},
                compiler_params=pltpu.CompilerParams(vmem_limit_bytes=8 * 1024 * 1024),
                cost_estimate=pl.CostEstimate(
                    flops=0, bytes_accessed=chunk_rows * share * 8, transcendentals=0
                ),
                name="last",
            )(end_lengths, owns[c], sums[c], *so_far)
        ]
    (next_tokens,) = so_far

    state_shape = (sessions_here, heads_here, head_dim, head_dim)
    moved_states = kernel_call(
        unpack_kernel,
        [smem_spec(), hbm_spec()],
        hbm_spec(),
        shape_of(state_shape, f32),
        [
            pltpu.VMEM(state_shape, bf16),
            pltpu.VMEM(state_shape, f32),
            pltpu.SemaphoreType.DMA((sessions_here,)),
            pltpu.SemaphoreType.DMA((sessions_here,)),
        ],
        0,
        limit_mib=16,
    )(recv_src, *in_hbm([received]))
    return (next_tokens, moved_states)


def solution(mesh):
    placed = (
        P(("group", "dp"), None),
        P(("group", "dp"), "tensor", None, None),
        P(None, "dp", "tensor"),
        P(None, "dp", "tensor"),
        P(),
        P(),
        P(("group", "dp")),
        P(("group", "dp")),
    )

    return jax.shard_map(
        per_device,
        mesh=mesh,
        in_specs=placed,
        out_specs=(P(("group", "dp"), "tensor"), P(("group", "dp"), "tensor", None, None)),
        check_vma=False,
    )
```

```python
import functools
import jax
import jax.numpy as jnp
from jax import lax
from jax.experimental import pallas as pl
from jax.experimental.pallas import tpu as pltpu
from jax.sharding import PartitionSpec as P

CHUNKS = 2
BLOCK_ROWS = 256


NT = (((1,), (1,)), ((), ()))


def dot_nt(a, b):
    return lax.dot_general(a, b, NT, preferred_element_type=jnp.float32)


def dot_nn(a, b):
    return jnp.dot(a, b, preferred_element_type=jnp.float32)


def rms_scale(values, gain_row):
    meansq = jnp.mean(values * values, axis=-1, keepdims=True)
    return (values * lax.rsqrt(meansq + 1e-05) * gain_row).astype(jnp.bfloat16)


def piece_copies(pieces, dest, sems, me, pick):
    copies = []
    rows = dest.shape[-2] // len(pieces)
    for k, piece in enumerate(pieces):
        start = pl.multiple_of(jnp.bitwise_xor(me, k) * rows, rows)
        copies.append(
            pltpu.make_async_copy(pick(piece), dest.at[..., pl.ds(start, rows), :], sems.at[k])
        )
    return copies


def project_kernel(n_dp, heads, event_count, block, base, *refs):
    rates_ref, gains_hbm, tok_ref, past_hbm = refs[:4]
    pieces = refs[4 : 4 + n_dp]
    gated_ref, key_hbm, value_hbm = refs[4 + n_dp : 7 + n_dp]
    normed_ref, past_ref, decay_ref, key_ref, value_ref, w_ref, gain_ref, sems = refs[7 + n_dp :]
    gain_copy = pltpu.make_async_copy(gains_hbm, gain_ref, sems.at[3])
    gain_copy.start()
    me = lax.axis_index("dp")
    first_head = lax.axis_index("tensor") * heads
    past_copy = pltpu.make_async_copy(
        past_hbm.at[pl.ds(base // event_count, past_ref.shape[0])], past_ref, sems.at[0]
    )
    past_copy.start()
    out_copies = [
        pltpu.make_async_copy(key_ref, key_hbm, sems.at[1]),
        pltpu.make_async_copy(value_ref, value_hbm, sems.at[2]),
    ]
    rows, _ = gated_ref.shape
    head_dim = past_ref.shape[3]
    sessions = block // event_count
    key_scale = head_dim ** (-0.5)
    depth = tok_ref.shape[1] // n_dp
    starts = [pl.multiple_of(jnp.bitwise_xor(me, k) * depth, depth) for k in range(n_dp)]
    split = depth % 128 == 0
    if not split:
        for m in range(4):
            for k in range(n_dp):
                w_ref[m, pl.ds(starts[k], depth), :] = pieces[k][m * depth : (m + 1) * depth]
    at = lax.broadcasted_iota(jnp.int32, (block, block), 0)
    to = lax.broadcasted_iota(jnp.int32, (block, block), 1)
    allowed = (at // event_count == to // event_count) & (at >= to)
    distance = jnp.maximum(at - to, 0).astype(jnp.float32)
    place = lax.broadcasted_iota(jnp.int32, (block, head_dim), 0) % event_count
    since = (place + 1).astype(jnp.float32)
    factors = []
    for h in range(heads):
        rate = rates_ref[first_head + h]
        decay_ref[h] = jnp.where(allowed, jnp.exp(-rate * distance), 0.0) * key_scale
        factors.append(jnp.exp(-rate * since))
    gain_copy.wait()

    def product(span, m):
        if not split:
            return dot_nn(normed_ref[span], w_ref[m])
        total = None
        for k in range(n_dp):
            term = dot_nn(
                normed_ref[span, pl.ds(starts[k], depth)], pieces[k][m * depth : (m + 1) * depth]
            )
            total = term if total is None else total + term
        return total

    for r in range(0, rows, block):
        span = slice(r, r + block)
        normed_ref[span] = rms_scale(
            tok_ref[base + r : base + r + block].astype(jnp.float32), gain_ref[0:1, :]
        )
        query = product(span, 0).astype(jnp.bfloat16)
        keys = product(span, 1).astype(jnp.bfloat16)
        key_ref[span] = keys
        values = product(span, 2).astype(jnp.bfloat16)
        value_ref[span] = values
        gate = product(span, 3)
        if r == 0:
            past_copy.wait()
        if r + block == rows:
            for copy in out_copies:
                copy.start()
        first_session = r // event_count
        for h in range(heads):
            cols = slice(h * head_dim, (h + 1) * head_dim)
            qh, kh, vh = query[:, cols], keys[:, cols], values[:, cols]
            mix = (dot_nt(qh, kh) * decay_ref[h]).astype(jnp.bfloat16)
            intra = dot_nn(mix, vh)
            parts = []
            for s in range(sessions):
                parts.append(
                    dot_nn(
                        qh[s * event_count : (s + 1) * event_count],
                        past_ref[first_session + s, h].astype(jnp.bfloat16),
                    )
                )
            retained = intra + jnp.concatenate(parts, axis=0) * factors[h]
            centred = retained - jnp.mean(retained, axis=-1, keepdims=True)
            row_var = jnp.mean(centred * centred, axis=-1, keepdims=True)
            normalised = centred * lax.rsqrt(row_var + 1e-05)
            gated_ref[span, cols] = (jax.nn.silu(gate[:, cols]) * normalised).astype(jnp.bfloat16)
    for copy in out_copies:
        copy.wait()


def state_kernel(chunks, heads, event_count, *refs):
    rates_ref, pos_ref, past_hbm = refs[:3]
    first_head = lax.axis_index("tensor") * heads
    sources = refs[3 : 3 + 2 * chunks]
    out_ref, buf_ref, past_ref, kv_ref, sems, past_sems, kv_sems = refs[3 + 2 * chunks :]
    kv_copies = [
        pltpu.make_async_copy(source, kv_ref.at[k], kv_sems.at[k])
        for k, source in enumerate(sources)
    ]
    for copy in kv_copies:
        copy.start()
    sessions, _, head_dim, _ = past_ref.shape
    groups = past_sems.shape[0]
    group = sessions // groups
    past_copies = [
        pltpu.make_async_copy(
            past_hbm.at[pl.ds(k * group, group)],
            past_ref.at[pl.ds(k * group, group)],
            past_sems.at[k],
        )
        for k in range(groups)
    ]
    for copy in past_copies:
        copy.start()
    rows = kv_ref.shape[1]
    key_scale = head_dim ** (-0.5)

    def copy_of(session):
        return pltpu.make_async_copy(
            buf_ref.at[session], out_ref.at[pos_ref[session]], sems.at[session]
        )

    place = lax.broadcasted_iota(jnp.int32, (rows, head_dim), 0) % event_count
    left = (event_count - 1 - place).astype(jnp.float32)
    factors, carries = [], []
    for h in range(heads):
        rate = rates_ref[first_head + h]
        factors.append(jnp.exp(-rate * left) * key_scale)
        carries.append(jnp.exp(jnp.full((1, head_dim), -rate * event_count, jnp.float32)))
    for c in range(chunks):
        kv_copies[c].wait()
        kv_copies[chunks + c].wait()
        weighted = []
        for h in range(heads):
            cols = slice(h * head_dim, (h + 1) * head_dim)
            weighted.append(
                (kv_ref[c, :, cols].astype(jnp.float32) * factors[h]).astype(jnp.bfloat16)
            )
        for s in range(rows // event_count):
            session = c * (rows // event_count) + s
            if session % group == 0:
                past_copies[session // group].wait()
            span = slice(s * event_count, (s + 1) * event_count)
            for h in range(heads):
                cols = slice(h * head_dim, (h + 1) * head_dim)
                grown = lax.dot_general(
                    weighted[h][span],
                    kv_ref[chunks + c, span, cols],
                    (((0,), (0,)), ((), ())),
                    preferred_element_type=jnp.float32,
                )
                buf_ref[session, h] = (carries[h] * past_ref[session, h] + grown).astype(
                    jnp.bfloat16
                )

            @pl.when(pos_ref[session] >= 0)
            def _():
                copy_of(session).start()

    for session in range(sessions):

        @pl.when(pos_ref[session] >= 0)
        def _():
            copy_of(session).wait()


def unpack_kernel(src_ref, recv_hbm, out_hbm, in_ref, out_ref, in_sems, out_sems):
    slots = in_ref.shape[0]

    def in_copy(slot):
        return pltpu.make_async_copy(
            recv_hbm.at[jnp.maximum(src_ref[slot], 0)], in_ref.at[slot], in_sems.at[slot]
        )

    def out_copy(slot):
        return pltpu.make_async_copy(out_ref.at[slot], out_hbm.at[slot], out_sems.at[slot])

    for slot in range(slots):

        @pl.when(src_ref[slot] >= 0)
        def _():
            in_copy(slot).start()

    for slot in range(slots):

        @pl.when(src_ref[slot] >= 0)
        def _():
            in_copy(slot).wait()
            out_ref[slot] = in_ref[slot].astype(jnp.float32)

        @pl.when(src_ref[slot] < 0)
        def _():
            out_ref[slot] = jnp.zeros(out_ref.shape[1:], jnp.float32)

        out_copy(slot).start()
    for slot in range(slots):
        out_copy(slot).wait()


def feed_kernel(n_dp, n_tensor, block, base, *refs):
    gains_hbm, tok_ref = refs[:2]
    gated_hbm = refs[2 : 2 + n_tensor]
    at = 2 + n_tensor
    if base == 0:
        out_pieces = refs[at : at + n_dp]
        at += n_dp
        pairs = refs[at : at + 2]
        near = refs[at + 2 : at + n_dp]
        far = refs[at + n_dp : at + 2 * n_dp - 2]
        at += 2 * n_dp - 2
        own_hbm, *part_hbm = refs[at : at + n_tensor]
        wo_ref, ffn_ref = refs[at + n_tensor : at + n_tensor + 2]
        at += n_tensor + 2
    else:
        wo_ref, ffn_ref = refs[at : at + 2]
        own_hbm, *part_hbm = refs[at + 2 : at + 2 + n_tensor]
        at += n_tensor + 2
    res_ref, gated, own_ref, part_ref, hid_ref, act_ref, gain_ref = refs[at:-3]
    sems, gated_sems, done_sems = refs[-3:]
    rows, width = own_ref.shape
    me, group, here_at = (lax.axis_index(name) for name in ("dp", "group", "tensor"))
    table = ring_sources(n_tensor)
    sources = []
    for k in range(n_tensor):
        source = table[0][k]
        for at_k in range(1, n_tensor):
            source = jnp.where(here_at == at_k, table[at_k][k], source)
        sources.append(source)
    depth = ffn_ref.shape[1] // n_dp

    def ffn_copy(source, half, k):
        start = pl.multiple_of(jnp.bitwise_xor(me, k) * depth, depth)
        return pltpu.make_async_copy(
            source, ffn_ref.at[half, pl.ds(start, depth)], sems.at[1 + half, k]
        )

    out_copies, up_copies, down_copies, rest = [], [], [], []
    if base == 0:
        out_copies = piece_copies(
            out_pieces, wo_ref, sems.at[0], me, lambda piece: piece.at[:, pl.ds(0, depth)]
        )
        up_copies = [ffn_copy(pairs[k].at[0], 0, k) for k in range(2)]
        down_copies = [ffn_copy(pairs[k].at[1], 1, k) for k in range(2)]
        for k in range(2, n_dp):
            near_rows = near[k - 2].at[pl.ds(0, depth)]
            rest.append(ffn_copy(near_rows, group, k))
            rest.append(ffn_copy(far[k - 2].at[pl.ds(0, depth)], 1 - group, k))
            up_copies.append(ffn_copy(near_rows, 0, k))
            down_copies.append(ffn_copy(near_rows, 1, k))
    gated_copies = [
        pltpu.make_async_copy(source, gated.at[k], gated_sems.at[k])
        for k, source in enumerate(gated_hbm[:-1])
    ]
    gated_copies.append(pltpu.make_async_copy(gains_hbm, gain_ref, gated_sems.at[n_tensor - 1]))
    done_copies = [pltpu.make_async_copy(own_ref, own_hbm, done_sems.at[0])]
    for k in range(1, n_tensor):
        done_copies.append(
            pltpu.make_async_copy(part_ref.at[k - 1], part_hbm[k - 1], done_sems.at[k])
        )
    here = [gated.at[k] for k in range(n_tensor - 1)] + [gated_hbm[-1]]
    for copy in out_copies + gated_copies:
        copy.start()
    for copy in up_copies[:2] + rest:
        copy.start()
    for copy in out_copies + gated_copies:
        copy.wait()
    for copy in down_copies[:2]:
        copy.start()
    for r in range(0, rows, block):
        span = slice(r, r + block)
        attended = dot_nt(here[0][span], wo_ref[sources[0]])
        for k in range(1, n_tensor):
            attended += dot_nt(here[k][span], wo_ref[sources[k]])
        residual = tok_ref[base + r : base + r + block].astype(jnp.float32) + attended
        res_ref[span] = residual
        hid_ref[span] = rms_scale(residual, gain_ref[1:2, :])
    for copy in up_copies:
        copy.wait()
    for r in range(0, rows, block):
        span = slice(r, r + block)
        activated = jax.nn.gelu(dot_nn(hid_ref[span], ffn_ref[0]), approximate=True)
        act_ref[span] = activated.astype(jnp.bfloat16)
    for copy in down_copies:
        copy.wait()

    def term(k):
        start = pl.multiple_of(sources[k] * width, width)
        return dot_nt(act_ref[...], ffn_ref[1, pl.ds(start, width), :])

    mine = pl.ds(pl.multiple_of(here_at * width, width), width)
    own_ref[...] = res_ref[:, mine] + term(0)
    done_copies[0].start()
    for k in list(range(2, n_tensor)) + [1]:
        part_ref[k - 1] = term(k).astype(jnp.bfloat16)
        done_copies[k].start()
    for copy in done_copies:
        copy.wait()


def add_kernel(a_ref, b_ref, out_ref):
    total = a_ref[...].astype(jnp.float32) + b_ref[...].astype(jnp.float32)
    out_ref[...] = total.astype(jnp.bfloat16)


def last_kernel(event_count, base, *refs):
    lengths_ref, own_ref, term_ref = refs[:3]
    out_hbm, out_ref, sem = refs[-3:]
    rows, width = own_ref.shape
    place = lax.broadcasted_iota(jnp.int32, (event_count, width), 0)
    for s in range(rows // event_count):
        span = slice(s * event_count, (s + 1) * event_count)
        total = own_ref[span] + term_ref[span].astype(jnp.float32)
        keep = place < lengths_ref[base // event_count + s]
        out_ref[span] = jnp.where(keep, total, 0.0).astype(jnp.bfloat16)
    copy = pltpu.make_async_copy(out_ref, out_hbm.at[pl.ds(base, rows)], sem)
    copy.start()
    copy.wait()


def xor_gather(value, axis, last_bit=1):
    pieces = [value]
    size = lax.axis_size(axis)
    bit = size // 2
    order = [0]
    while bit >= last_bit:
        pairs = [(i, i ^ bit) for i in range(size)]
        arrived = []
        for piece in pieces:
            arrived.append(lax.ppermute(piece, axis, pairs))
        pieces = pieces + arrived
        order = order + [k ^ bit for k in order]
        bit //= 2
    return [pieces[order.index(k)] for k in range(0, size, last_bit)]


def ring_order(size):
    return list(range(0, size, 2)) + list(range(1, size, 2))[::-1]


def ring_pairs(size):
    order = ring_order(size)
    return [(order[i], order[(i + 1) % size]) for i in range(size)]


def ring_sources(size):
    order = ring_order(size)
    return [[order[(order.index(at) - k) % size] for k in range(size)] for at in range(size)]


def smem_spec():
    return pl.BlockSpec(memory_space=pltpu.SMEM)


def hbm_spec():
    return pl.BlockSpec(memory_space=pltpu.HBM)


def in_hbm(arrays):
    return [pltpu.with_memory_space_constraint(array, pltpu.HBM) for array in arrays]


def vmem_spec():
    return pl.BlockSpec(memory_space=pltpu.VMEM)


def kernel_call(kernel, in_specs, out_specs, out_shape, scratch, flops, limit_mib=24):
    return pl.pallas_call(
        kernel,
        in_specs=in_specs,
        out_specs=out_specs,
        out_shape=out_shape,
        scratch_shapes=scratch,
        compiler_params=pltpu.CompilerParams(vmem_limit_bytes=limit_mib * 1024 * 1024),
        cost_estimate=pl.CostEstimate(
            flops=flops, bytes_accessed=4 * 1024 * 1024, transcendentals=0
        ),
    )


def per_device(
    tokens, past_states, attn_weights, ffn_weights, norm_gains, head_rates, end_lengths, new_slot
):
    sessions_here = end_lengths.shape[0]
    row_count, width = tokens.shape
    event_count = row_count // sessions_here
    heads_here, head_dim = past_states.shape[1], past_states.shape[3]
    cols_here = heads_here * head_dim
    units_here = ffn_weights.shape[2]
    n_dp, n_tensor = lax.axis_size("dp"), lax.axis_size("tensor")
    dp_at = lax.axis_index("dp")
    share = width // n_tensor
    pair_cap = max(2, 2 * sessions_here // n_dp)
    slot_count = n_dp * pair_cap
    chunk_rows = row_count // CHUNKS
    block = min(BLOCK_ROWS, chunk_rows)
    ring = ring_pairs(n_tensor)
    bf16, f32 = jnp.bfloat16, jnp.float32
    shape_of = jax.ShapeDtypeStruct

    survive = end_lengths > event_count
    target_dev = new_slot // sessions_here
    session_ids = jnp.arange(sessions_here, dtype=jnp.int32)
    proj_rows = attn_weights.shape[1]
    proj_own = attn_weights[:4].reshape(4 * proj_rows, cols_here)
    proj_pieces = xor_gather(proj_own, "dp")
    note_rows = 16
    notes = jnp.stack([jnp.where(survive, target_dev, -1), new_slot % sessions_here])
    notes = jnp.pad(
        notes.astype(bf16), ((0, note_rows - 2), (0, units_here - sessions_here))
    )
    half_own = lax.dynamic_index_in_dim(
        ffn_weights, lax.axis_index("group"), 0, keepdims=False
    )
    half_own = jnp.concatenate([half_own, notes])
    out_own = lax.all_to_all(
        jnp.broadcast_to(attn_weights[4:], (n_tensor, proj_rows, cols_here)),
        "tensor",
        split_axis=0,
        concat_axis=0,
        tiled=True,
    )
    out_pieces = xor_gather(out_own, "dp")

    near = xor_gather(half_own, "dp", last_bit=2)[1:]
    swap = [(0, 1), (1, 0)]
    far = []
    for k, piece in enumerate(near):
        far.append(lax.ppermute(piece, "group", swap))
    beside = [(i, i ^ 1) for i in range(n_dp)]

    def to_beside(value):
        return lax.ppermute(value, "dp", beside)

    ffn_pieces = [ffn_weights, to_beside(ffn_weights)]
    noted = [notes[:2, :sessions_here], to_beside(notes[:, :128])[:2, :sessions_here]]
    for name, side in (("near", near), ("far", far)):
        for k, piece in enumerate(side):
            ffn_pieces += [piece, to_beside(piece)]
            if name == "near":
                noted += [
                    side_piece[proj_rows : proj_rows + 2, :sessions_here]
                    for side_piece in ffn_pieces[-2:]
                ]
    earlier = (
        (target_dev[None, :] == target_dev[:, None])
        & survive[None, :]
        & (session_ids[None, :] < session_ids[:, None])
    )
    pair_rank = jnp.sum(earlier.astype(jnp.int32), axis=1)
    send_pos = jnp.where(survive, target_dev * pair_cap + pair_rank, -1)
    meta = jnp.stack(noted)
    meta = meta.astype(jnp.int32)
    from_dev = jnp.bitwise_xor(dp_at, jnp.arange(n_dp, dtype=jnp.int32))
    coming = meta[:, 0] == dp_at
    ahead = coming[:, None, :] & (session_ids[None, None, :] < session_ids[None, :, None])
    rank_all = jnp.sum(ahead.astype(jnp.int32), axis=2)
    from_pos = from_dev[:, None] * pair_cap + rank_all + 1
    lands = meta[:, 1][None] == session_ids[:, None, None]
    recv_src = jnp.sum(jnp.where(lands & coming[None], from_pos[None], 0), axis=(1, 2)) - 1

    rows_shape = shape_of((chunk_rows, cols_here), bf16)
    decay_shape = pltpu.VMEM((heads_here, block, block), f32)
    chunk_sessions = chunk_rows // event_count
    split = (width // n_dp) % 128 == 0
    gated, keys, values = [], [], []
    for c in range(CHUNKS):
        g, k, v = kernel_call(
            functools.partial(project_kernel, n_dp, heads_here, event_count, block, c * chunk_rows),
            [smem_spec(), hbm_spec(), vmem_spec(), hbm_spec()] + [vmem_spec()] * n_dp,
            [vmem_spec()] + [hbm_spec()] * 2,
            [rows_shape] + [pltpu.HBM((chunk_rows, cols_here), bf16)] * 2,
            [
                pltpu.VMEM((chunk_rows, width), bf16),
                pltpu.VMEM((chunk_sessions, heads_here, head_dim, head_dim), f32),
                decay_shape,
                pltpu.VMEM((chunk_rows, cols_here), bf16),
                pltpu.VMEM((chunk_rows, cols_here), bf16),
                pltpu.VMEM((4, 16 if split else width, cols_here), bf16),
                pltpu.VMEM(norm_gains.shape, f32),
                pltpu.SemaphoreType.DMA((4,)),
            ],
            2 * chunk_rows * width * cols_here * 4,
            limit_mib=12,
        )(
            *in_hbm([head_rates, norm_gains]),
            tokens,
            *in_hbm([past_states]),
            *proj_pieces,
        )
        gated.append([g])
        keys.append(k)
        values.append(v)
    for _ in range(n_tensor - 1):
        for c in range(CHUNKS):
            gated[c].append(lax.ppermute(gated[c][-1], "tensor", ring))

    packed = kernel_call(
        functools.partial(state_kernel, CHUNKS, heads_here, event_count),
        [smem_spec()] * 2 + [hbm_spec()] * (1 + 2 * CHUNKS),
        hbm_spec(),
        pltpu.HBM((slot_count, heads_here, head_dim, head_dim), bf16),
        [
            pltpu.VMEM((sessions_here, heads_here, head_dim, head_dim), bf16),
            pltpu.VMEM((sessions_here, heads_here, head_dim, head_dim), f32),
            pltpu.VMEM((2 * CHUNKS, chunk_rows, cols_here), bf16),
            pltpu.SemaphoreType.DMA((sessions_here,)),
            pltpu.SemaphoreType.DMA((4,)),
            pltpu.SemaphoreType.DMA((2 * CHUNKS,)),
        ],
        2 * row_count * head_dim * cols_here,
    )(*in_hbm([head_rates]), send_pos, *in_hbm([past_states, *keys, *values]))
    received = lax.all_to_all(packed, "dp", split_axis=0, concat_axis=0, tiled=True)

    owns, parts, sums = [], [], []
    for c in range(CHUNKS):
        weight_shapes = [
            pltpu.VMEM((n_tensor, width, cols_here), bf16),
            pltpu.VMEM((2, width, units_here), bf16),
        ]
        first = c == 0
        outs = kernel_call(
            functools.partial(feed_kernel, n_dp, n_tensor, block, c * chunk_rows),
            [hbm_spec(), vmem_spec()]
            + [hbm_spec()] * (n_tensor - 1)
            + [vmem_spec()]
            + ([hbm_spec()] * (3 * n_dp - 2) if first else [vmem_spec()] * 2),
            [hbm_spec()] * n_tensor + ([vmem_spec()] * 2 if first else []),
            [pltpu.HBM((chunk_rows, share), f32)]
            + [pltpu.HBM((chunk_rows, share), bf16)] * (n_tensor - 1)
            + (weight_shapes if first else []),
            [
                pltpu.VMEM((chunk_rows, width), f32),
                pltpu.VMEM((n_tensor - 1, chunk_rows, cols_here), bf16),
                pltpu.VMEM((chunk_rows, share), f32),
                pltpu.VMEM((n_tensor - 1, chunk_rows, share), bf16),
                pltpu.VMEM((chunk_rows, width), bf16),
                pltpu.VMEM((chunk_rows, units_here), bf16),
                pltpu.VMEM(norm_gains.shape, f32),
                pltpu.SemaphoreType.DMA((3, n_dp)),
                pltpu.SemaphoreType.DMA((n_tensor,)),
                pltpu.SemaphoreType.DMA((n_tensor,)),
            ],
            2 * chunk_rows * width * (width + 2 * units_here),
        )(
            *in_hbm([norm_gains]),
            tokens,
            *in_hbm(gated[c][:-1]),
            gated[c][-1],
            *(in_hbm(out_pieces + ffn_pieces) if first else whole),
        )
        if first:
            whole = outs[n_tensor:]
        own, *part = outs[:n_tensor]
        owns.append(own)
        parts.append(part)
        sums.append(None)
    for hop in range(n_tensor - 1):
        for c in range(CHUNKS):
            mine = parts[c][hop]
            if hop:
                mine = kernel_call(
                    add_kernel,
                    [vmem_spec()] * 2,
                    vmem_spec(),
                    shape_of((chunk_rows, share), bf16),
                    [],
                    0,
                    limit_mib=4,
                )(sums[c], mine)
            sums[c] = lax.ppermute(mine, "tensor", ring)

    so_far = []
    for c in range(CHUNKS):
        so_far = [
            pl.pallas_call(
                functools.partial(last_kernel, event_count, c * chunk_rows),
                in_specs=[smem_spec()] + [vmem_spec()] * 2 + [hbm_spec()] * len(so_far),
                out_specs=hbm_spec(),
                out_shape=shape_of((row_count, share), bf16),
                scratch_shapes=[
                    pltpu.VMEM((chunk_rows, share), bf16),
                    pltpu.SemaphoreType.DMA,
                ],
                input_output_aliases={3: 0} if so_far else {},
                compiler_params=pltpu.CompilerParams(vmem_limit_bytes=8 * 1024 * 1024),
                cost_estimate=pl.CostEstimate(
                    flops=0, bytes_accessed=chunk_rows * share * 8, transcendentals=0
                ),
                name="last",
            )(end_lengths, owns[c], sums[c], *so_far)
        ]
    (next_tokens,) = so_far

    state_shape = (sessions_here, heads_here, head_dim, head_dim)
    moved_states = kernel_call(
        unpack_kernel,
        [smem_spec(), hbm_spec()],
        hbm_spec(),
        shape_of(state_shape, f32),
        [
            pltpu.VMEM(state_shape, bf16),
            pltpu.VMEM(state_shape, f32),
            pltpu.SemaphoreType.DMA((sessions_here,)),
            pltpu.SemaphoreType.DMA((sessions_here,)),
        ],
        0,
        limit_mib=16,
    )(recv_src, *in_hbm([received]))
    return (next_tokens, moved_states)


def solution(mesh):
    placed = (
        P(("group", "dp"), None),
        P(("group", "dp"), "tensor", None, None),
        P(None, "dp", "tensor"),
        P(None, "dp", "tensor"),
        P(),
        P(),
        P(("group", "dp")),
        P(("group", "dp")),
    )

    return jax.shard_map(
        per_device,
        mesh=mesh,
        in_specs=placed,
        out_specs=(P(("group", "dp"), "tensor"), P(("group", "dp"), "tensor", None, None)),
        check_vma=False,
    )
```

```python
import functools
import jax
import jax.numpy as jnp
from jax import lax
from jax.experimental import pallas as pl
from jax.experimental.pallas import tpu as pltpu
from jax.sharding import PartitionSpec as P

CHUNKS = 2
BLOCK_ROWS = 256


NT = (((1,), (1,)), ((), ()))


def dot_nt(a, b):
    return lax.dot_general(a, b, NT, preferred_element_type=jnp.float32)


def dot_nn(a, b):
    return jnp.dot(a, b, preferred_element_type=jnp.float32)


def rms_scale(values, gain_row):
    meansq = jnp.mean(values * values, axis=-1, keepdims=True)
    return (values * lax.rsqrt(meansq + 1e-05) * gain_row).astype(jnp.bfloat16)


def piece_copies(pieces, dest, sems, me, pick):
    copies = []
    rows = dest.shape[-2] // len(pieces)
    for k, piece in enumerate(pieces):
        start = pl.multiple_of(jnp.bitwise_xor(me, k) * rows, rows)
        copies.append(
            pltpu.make_async_copy(pick(piece), dest.at[..., pl.ds(start, rows), :], sems.at[k])
        )
    return copies


def project_kernel(n_dp, heads, event_count, block, base, *refs):
    rates_ref, gains_hbm, tok_ref, past_hbm = refs[:4]
    pieces = refs[4 : 4 + n_dp]
    gated_ref, key_hbm, value_hbm = refs[4 + n_dp : 7 + n_dp]
    normed_ref, past_ref, decay_ref, key_ref, value_ref, w_ref, gain_ref, sems = refs[7 + n_dp :]
    gain_copy = pltpu.make_async_copy(gains_hbm, gain_ref, sems.at[3])
    gain_copy.start()
    me = lax.axis_index("dp")
    first_head = lax.axis_index("tensor") * heads
    past_copy = pltpu.make_async_copy(
        past_hbm.at[pl.ds(base // event_count, past_ref.shape[0])], past_ref, sems.at[0]
    )
    past_copy.start()
    out_copies = [
        pltpu.make_async_copy(key_ref, key_hbm, sems.at[1]),
        pltpu.make_async_copy(value_ref, value_hbm, sems.at[2]),
    ]
    rows, _ = gated_ref.shape
    head_dim = past_ref.shape[3]
    sessions = block // event_count
    key_scale = head_dim ** (-0.5)
    depth = tok_ref.shape[1] // n_dp
    starts = [pl.multiple_of(jnp.bitwise_xor(me, k) * depth, depth) for k in range(n_dp)]
    split = depth % 128 == 0
    if not split:
        for m in range(4):
            for k in range(n_dp):
                w_ref[m, pl.ds(starts[k], depth), :] = pieces[k][m * depth : (m + 1) * depth]
    at = lax.broadcasted_iota(jnp.int32, (block, block), 0)
    to = lax.broadcasted_iota(jnp.int32, (block, block), 1)
    allowed = (at // event_count == to // event_count) & (at >= to)
    distance = jnp.maximum(at - to, 0).astype(jnp.float32)
    place = lax.broadcasted_iota(jnp.int32, (block, head_dim), 0) % event_count
    since = (place + 1).astype(jnp.float32)
    factors = []
    for h in range(heads):
        rate = rates_ref[first_head + h]
        decay_ref[h] = jnp.where(allowed, jnp.exp(-rate * distance), 0.0) * key_scale
        factors.append(jnp.exp(-rate * since))
    gain_copy.wait()

    def product(span, m):
        if not split:
            return dot_nn(normed_ref[span], w_ref[m])
        total = None
        for k in range(n_dp):
            term = dot_nn(
                normed_ref[span, pl.ds(starts[k], depth)], pieces[k][m * depth : (m + 1) * depth]
            )
            total = term if total is None else total + term
        return total

    for r in range(0, rows, block):
        span = slice(r, r + block)
        normed_ref[span] = rms_scale(
            tok_ref[base + r : base + r + block].astype(jnp.float32), gain_ref[0:1, :]
        )
        query = product(span, 0).astype(jnp.bfloat16)
        keys = product(span, 1).astype(jnp.bfloat16)
        key_ref[span] = keys
        values = product(span, 2).astype(jnp.bfloat16)
        value_ref[span] = values
        gate = product(span, 3)
        if r == 0:
            past_copy.wait()
        if r + block == rows:
            for copy in out_copies:
                copy.start()
        first_session = r // event_count
        for h in range(heads):
            cols = slice(h * head_dim, (h + 1) * head_dim)
            qh, kh, vh = query[:, cols], keys[:, cols], values[:, cols]
            mix = (dot_nt(qh, kh) * decay_ref[h]).astype(jnp.bfloat16)
            intra = dot_nn(mix, vh)
            parts = []
            for s in range(sessions):
                parts.append(
                    dot_nn(
                        qh[s * event_count : (s + 1) * event_count],
                        past_ref[first_session + s, h].astype(jnp.bfloat16),
                    )
                )
            retained = intra + jnp.concatenate(parts, axis=0) * factors[h]
            centred = retained - jnp.mean(retained, axis=-1, keepdims=True)
            row_var = jnp.mean(centred * centred, axis=-1, keepdims=True)
            normalised = centred * lax.rsqrt(row_var + 1e-05)
            gated_ref[span, cols] = (jax.nn.silu(gate[:, cols]) * normalised).astype(jnp.bfloat16)
    for copy in out_copies:
        copy.wait()


def state_kernel(chunks, heads, event_count, *refs):
    rates_ref, pos_ref, past_hbm = refs[:3]
    first_head = lax.axis_index("tensor") * heads
    sources = refs[3 : 3 + 2 * chunks]
    out_ref, buf_ref, past_ref, kv_ref, sems, past_sems, kv_sems = refs[3 + 2 * chunks :]
    kv_copies = [
        pltpu.make_async_copy(source, kv_ref.at[k], kv_sems.at[k])
        for k, source in enumerate(sources)
    ]
    for copy in kv_copies:
        copy.start()
    sessions, _, head_dim, _ = past_ref.shape
    groups = past_sems.shape[0]
    group = sessions // groups
    past_copies = [
        pltpu.make_async_copy(
            past_hbm.at[pl.ds(k * group, group)],
            past_ref.at[pl.ds(k * group, group)],
            past_sems.at[k],
        )
        for k in range(groups)
    ]
    for copy in past_copies:
        copy.start()
    rows = kv_ref.shape[1]
    key_scale = head_dim ** (-0.5)

    def copy_of(session):
        return pltpu.make_async_copy(
            buf_ref.at[session], out_ref.at[pos_ref[session]], sems.at[session]
        )

    place = lax.broadcasted_iota(jnp.int32, (rows, head_dim), 0) % event_count
    left = (event_count - 1 - place).astype(jnp.float32)
    factors, carries = [], []
    for h in range(heads):
        rate = rates_ref[first_head + h]
        factors.append(jnp.exp(-rate * left) * key_scale)
        carries.append(jnp.exp(jnp.full((1, head_dim), -rate * event_count, jnp.float32)))
    for c in range(chunks):
        kv_copies[c].wait()
        kv_copies[chunks + c].wait()
        weighted = []
        for h in range(heads):
            cols = slice(h * head_dim, (h + 1) * head_dim)
            weighted.append(
                (kv_ref[c, :, cols].astype(jnp.float32) * factors[h]).astype(jnp.bfloat16)
            )
        for s in range(rows // event_count):
            session = c * (rows // event_count) + s
            if session % group == 0:
                past_copies[session // group].wait()
            span = slice(s * event_count, (s + 1) * event_count)
            for h in range(heads):
                cols = slice(h * head_dim, (h + 1) * head_dim)
                grown = lax.dot_general(
                    weighted[h][span],
                    kv_ref[chunks + c, span, cols],
                    (((0,), (0,)), ((), ())),
                    preferred_element_type=jnp.float32,
                )
                buf_ref[session, h] = (carries[h] * past_ref[session, h] + grown).astype(
                    jnp.bfloat16
                )

            @pl.when(pos_ref[session] >= 0)
            def _():
                copy_of(session).start()

    for session in range(sessions):

        @pl.when(pos_ref[session] >= 0)
        def _():
            copy_of(session).wait()


def unpack_kernel(src_ref, recv_hbm, out_hbm, in_ref, out_ref, in_sems, out_sems):
    slots = in_ref.shape[0]

    def in_copy(slot):
        return pltpu.make_async_copy(
            recv_hbm.at[jnp.maximum(src_ref[slot], 0)], in_ref.at[slot], in_sems.at[slot]
        )

    def out_copy(slot):
        return pltpu.make_async_copy(out_ref.at[slot], out_hbm.at[slot], out_sems.at[slot])

    for slot in range(slots):

        @pl.when(src_ref[slot] >= 0)
        def _():
            in_copy(slot).start()

    for slot in range(slots):

        @pl.when(src_ref[slot] >= 0)
        def _():
            in_copy(slot).wait()
            out_ref[slot] = in_ref[slot].astype(jnp.float32)

        @pl.when(src_ref[slot] < 0)
        def _():
            out_ref[slot] = jnp.zeros(out_ref.shape[1:], jnp.float32)

        out_copy(slot).start()
    for slot in range(slots):
        out_copy(slot).wait()


def collect_kernel(n_dp, *refs):
    out_pieces = refs[:n_dp]
    pairs = refs[n_dp : n_dp + 2]
    near = refs[n_dp + 2 : 2 * n_dp]
    far = refs[2 * n_dp : 3 * n_dp - 2]
    wo_ref, ffn_ref, sems = refs[3 * n_dp - 2 :]
    me, group = lax.axis_index("dp"), lax.axis_index("group")
    depth = ffn_ref.shape[1] // n_dp

    def ffn_copy(source, half, k):
        start = pl.multiple_of(jnp.bitwise_xor(me, k) * depth, depth)
        return pltpu.make_async_copy(
            source, ffn_ref.at[half, pl.ds(start, depth)], sems.at[1 + half, k]
        )

    copies = piece_copies(
        out_pieces, wo_ref, sems.at[0], me, lambda piece: piece.at[:, pl.ds(0, depth)]
    )
    for k in range(2):
        copies += [ffn_copy(pairs[k].at[half], half, k) for half in range(2)]
    for k in range(2, n_dp):
        copies.append(ffn_copy(near[k - 2].at[pl.ds(0, depth)], group, k))
        copies.append(ffn_copy(far[k - 2].at[pl.ds(0, depth)], 1 - group, k))
    for copy in copies:
        copy.start()
    for copy in copies:
        copy.wait()


def feed_kernel(n_tensor, block, base, *refs):
    gains_hbm, tok_ref = refs[:2]
    gated_hbm = refs[2 : 2 + n_tensor]
    at = 2 + n_tensor
    wo_ref, ffn_ref = refs[at : at + 2]
    own_hbm, *part_hbm = refs[at + 2 : at + 2 + n_tensor]
    at += n_tensor + 2
    res_ref, gated, own_ref, part_ref, hid_ref, act_ref, gain_ref = refs[at:-2]
    gated_sems, done_sems = refs[-2:]
    rows, width = own_ref.shape
    here_at = lax.axis_index("tensor")
    table = ring_sources(n_tensor)
    sources = []
    for k in range(n_tensor):
        source = table[0][k]
        for at_k in range(1, n_tensor):
            source = jnp.where(here_at == at_k, table[at_k][k], source)
        sources.append(source)
    gated_copies = [
        pltpu.make_async_copy(source, gated.at[k], gated_sems.at[k])
        for k, source in enumerate(gated_hbm[:-1])
    ]
    gated_copies.append(pltpu.make_async_copy(gains_hbm, gain_ref, gated_sems.at[n_tensor - 1]))
    done_copies = [pltpu.make_async_copy(own_ref, own_hbm, done_sems.at[0])]
    for k in range(1, n_tensor):
        done_copies.append(
            pltpu.make_async_copy(part_ref.at[k - 1], part_hbm[k - 1], done_sems.at[k])
        )
    here = [gated.at[k] for k in range(n_tensor - 1)] + [gated_hbm[-1]]
    for copy in gated_copies:
        copy.start()
    for copy in gated_copies:
        copy.wait()
    for r in range(0, rows, block):
        span = slice(r, r + block)
        attended = dot_nt(here[0][span], wo_ref[sources[0]])
        for k in range(1, n_tensor):
            attended += dot_nt(here[k][span], wo_ref[sources[k]])
        residual = tok_ref[base + r : base + r + block].astype(jnp.float32) + attended
        res_ref[span] = residual
        hid_ref[span] = rms_scale(residual, gain_ref[1:2, :])
    for r in range(0, rows, block):
        span = slice(r, r + block)
        activated = jax.nn.gelu(dot_nn(hid_ref[span], ffn_ref[0]), approximate=True)
        act_ref[span] = activated.astype(jnp.bfloat16)

    def term(k):
        start = pl.multiple_of(sources[k] * width, width)
        return dot_nt(act_ref[...], ffn_ref[1, pl.ds(start, width), :])

    mine = pl.ds(pl.multiple_of(here_at * width, width), width)
    own_ref[...] = res_ref[:, mine] + term(0)
    done_copies[0].start()
    for k in list(range(2, n_tensor)) + [1]:
        part_ref[k - 1] = term(k).astype(jnp.bfloat16)
        done_copies[k].start()
    for copy in done_copies:
        copy.wait()


def add_kernel(a_ref, b_ref, out_ref):
    total = a_ref[...].astype(jnp.float32) + b_ref[...].astype(jnp.float32)
    out_ref[...] = total.astype(jnp.bfloat16)


def last_kernel(event_count, base, *refs):
    lengths_ref, own_ref, term_ref = refs[:3]
    out_hbm, out_ref, sem = refs[-3:]
    rows, width = own_ref.shape
    place = lax.broadcasted_iota(jnp.int32, (event_count, width), 0)
    for s in range(rows // event_count):
        span = slice(s * event_count, (s + 1) * event_count)
        total = own_ref[span] + term_ref[span].astype(jnp.float32)
        keep = place < lengths_ref[base // event_count + s]
        out_ref[span] = jnp.where(keep, total, 0.0).astype(jnp.bfloat16)
    copy = pltpu.make_async_copy(out_ref, out_hbm.at[pl.ds(base, rows)], sem)
    copy.start()
    copy.wait()


def xor_gather(value, axis, last_bit=1):
    pieces = [value]
    size = lax.axis_size(axis)
    bit = size // 2
    order = [0]
    while bit >= last_bit:
        pairs = [(i, i ^ bit) for i in range(size)]
        arrived = []
        for piece in pieces:
            arrived.append(lax.ppermute(piece, axis, pairs))
        pieces = pieces + arrived
        order = order + [k ^ bit for k in order]
        bit //= 2
    return [pieces[order.index(k)] for k in range(0, size, last_bit)]


def ring_order(size):
    return list(range(0, size, 2)) + list(range(1, size, 2))[::-1]


def ring_pairs(size):
    order = ring_order(size)
    return [(order[i], order[(i + 1) % size]) for i in range(size)]


def ring_sources(size):
    order = ring_order(size)
    return [[order[(order.index(at) - k) % size] for k in range(size)] for at in range(size)]


def smem_spec():
    return pl.BlockSpec(memory_space=pltpu.SMEM)


def hbm_spec():
    return pl.BlockSpec(memory_space=pltpu.HBM)


def in_hbm(arrays):
    return [pltpu.with_memory_space_constraint(array, pltpu.HBM) for array in arrays]


def vmem_spec():
    return pl.BlockSpec(memory_space=pltpu.VMEM)


def kernel_call(kernel, in_specs, out_specs, out_shape, scratch, flops, limit_mib=24):
    return pl.pallas_call(
        kernel,
        in_specs=in_specs,
        out_specs=out_specs,
        out_shape=out_shape,
        scratch_shapes=scratch,
        compiler_params=pltpu.CompilerParams(vmem_limit_bytes=limit_mib * 1024 * 1024),
        cost_estimate=pl.CostEstimate(
            flops=flops, bytes_accessed=4 * 1024 * 1024, transcendentals=0
        ),
    )


def per_device(
    tokens, past_states, attn_weights, ffn_weights, norm_gains, head_rates, end_lengths, new_slot
):
    sessions_here = end_lengths.shape[0]
    row_count, width = tokens.shape
    event_count = row_count // sessions_here
    heads_here, head_dim = past_states.shape[1], past_states.shape[3]
    cols_here = heads_here * head_dim
    units_here = ffn_weights.shape[2]
    n_dp, n_tensor = lax.axis_size("dp"), lax.axis_size("tensor")
    dp_at = lax.axis_index("dp")
    share = width // n_tensor
    pair_cap = max(2, 2 * sessions_here // n_dp)
    slot_count = n_dp * pair_cap
    chunk_rows = row_count // CHUNKS
    block = min(BLOCK_ROWS, chunk_rows)
    ring = ring_pairs(n_tensor)
    bf16, f32 = jnp.bfloat16, jnp.float32
    shape_of = jax.ShapeDtypeStruct

    survive = end_lengths > event_count
    target_dev = new_slot // sessions_here
    session_ids = jnp.arange(sessions_here, dtype=jnp.int32)
    proj_rows = attn_weights.shape[1]
    proj_own = attn_weights[:4].reshape(4 * proj_rows, cols_here)
    proj_pieces = xor_gather(proj_own, "dp")
    note_rows = 16
    notes = jnp.stack([jnp.where(survive, target_dev, -1), new_slot % sessions_here])
    notes = jnp.pad(
        notes.astype(bf16), ((0, note_rows - 2), (0, units_here - sessions_here))
    )
    half_own = lax.dynamic_index_in_dim(
        ffn_weights, lax.axis_index("group"), 0, keepdims=False
    )
    half_own = jnp.concatenate([half_own, notes])
    out_own = lax.all_to_all(
        jnp.broadcast_to(attn_weights[4:], (n_tensor, proj_rows, cols_here)),
        "tensor",
        split_axis=0,
        concat_axis=0,
        tiled=True,
    )
    out_pieces = xor_gather(out_own, "dp")

    near = xor_gather(half_own, "dp", last_bit=2)[1:]
    swap = [(0, 1), (1, 0)]
    far = []
    for k, piece in enumerate(near):
        far.append(lax.ppermute(piece, "group", swap))
    beside = [(i, i ^ 1) for i in range(n_dp)]

    def to_beside(value):
        return lax.ppermute(value, "dp", beside)

    ffn_pieces = [ffn_weights, to_beside(ffn_weights)]
    noted = [notes[:2, :sessions_here], to_beside(notes[:, :128])[:2, :sessions_here]]
    for name, side in (("near", near), ("far", far)):
        for k, piece in enumerate(side):
            ffn_pieces += [piece, to_beside(piece)]
            if name == "near":
                noted += [
                    side_piece[proj_rows : proj_rows + 2, :sessions_here]
                    for side_piece in ffn_pieces[-2:]
                ]
    earlier = (
        (target_dev[None, :] == target_dev[:, None])
        & survive[None, :]
        & (session_ids[None, :] < session_ids[:, None])
    )
    pair_rank = jnp.sum(earlier.astype(jnp.int32), axis=1)
    send_pos = jnp.where(survive, target_dev * pair_cap + pair_rank, -1)
    meta = jnp.stack(noted)
    meta = meta.astype(jnp.int32)
    from_dev = jnp.bitwise_xor(dp_at, jnp.arange(n_dp, dtype=jnp.int32))
    coming = meta[:, 0] == dp_at
    ahead = coming[:, None, :] & (session_ids[None, None, :] < session_ids[None, :, None])
    rank_all = jnp.sum(ahead.astype(jnp.int32), axis=2)
    from_pos = from_dev[:, None] * pair_cap + rank_all + 1
    lands = meta[:, 1][None] == session_ids[:, None, None]
    recv_src = jnp.sum(jnp.where(lands & coming[None], from_pos[None], 0), axis=(1, 2)) - 1

    rows_shape = shape_of((chunk_rows, cols_here), bf16)
    decay_shape = pltpu.VMEM((heads_here, block, block), f32)
    chunk_sessions = chunk_rows // event_count
    split = (width // n_dp) % 128 == 0
    gated, keys, values = [], [], []
    for c in range(CHUNKS):
        g, k, v = kernel_call(
            functools.partial(project_kernel, n_dp, heads_here, event_count, block, c * chunk_rows),
            [smem_spec(), hbm_spec(), vmem_spec(), hbm_spec()] + [vmem_spec()] * n_dp,
            [vmem_spec()] + [hbm_spec()] * 2,
            [rows_shape] + [pltpu.HBM((chunk_rows, cols_here), bf16)] * 2,
            [
                pltpu.VMEM((chunk_rows, width), bf16),
                pltpu.VMEM((chunk_sessions, heads_here, head_dim, head_dim), f32),
                decay_shape,
                pltpu.VMEM((chunk_rows, cols_here), bf16),
                pltpu.VMEM((chunk_rows, cols_here), bf16),
                pltpu.VMEM((4, 16 if split else width, cols_here), bf16),
                pltpu.VMEM(norm_gains.shape, f32),
                pltpu.SemaphoreType.DMA((4,)),
            ],
            2 * chunk_rows * width * cols_here * 4,
            limit_mib=12,
        )(
            *in_hbm([head_rates, norm_gains]),
            tokens,
            *in_hbm([past_states]),
            *proj_pieces,
        )
        gated.append([g])
        keys.append(k)
        values.append(v)
    for _ in range(n_tensor - 1):
        for c in range(CHUNKS):
            gated[c].append(lax.ppermute(gated[c][-1], "tensor", ring))

    packed = kernel_call(
        functools.partial(state_kernel, CHUNKS, heads_here, event_count),
        [smem_spec()] * 2 + [hbm_spec()] * (1 + 2 * CHUNKS),
        hbm_spec(),
        pltpu.HBM((slot_count, heads_here, head_dim, head_dim), bf16),
        [
            pltpu.VMEM((sessions_here, heads_here, head_dim, head_dim), bf16),
            pltpu.VMEM((sessions_here, heads_here, head_dim, head_dim), f32),
            pltpu.VMEM((2 * CHUNKS, chunk_rows, cols_here), bf16),
            pltpu.SemaphoreType.DMA((sessions_here,)),
            pltpu.SemaphoreType.DMA((4,)),
            pltpu.SemaphoreType.DMA((2 * CHUNKS,)),
        ],
        2 * row_count * head_dim * cols_here,
    )(*in_hbm([head_rates]), send_pos, *in_hbm([past_states, *keys, *values]))
    received = lax.all_to_all(packed, "dp", split_axis=0, concat_axis=0, tiled=True)

    whole = kernel_call(
        functools.partial(collect_kernel, n_dp),
        [hbm_spec()] * (3 * n_dp - 2),
        [vmem_spec()] * 2,
        [pltpu.VMEM((n_tensor, width, cols_here), bf16), pltpu.VMEM((2, width, units_here), bf16)],
        [pltpu.SemaphoreType.DMA((3, n_dp))],
        0,
        limit_mib=8,
    )(*in_hbm(out_pieces + ffn_pieces))
    owns, parts, sums = [], [], []
    for c in range(CHUNKS):
        outs = kernel_call(
            functools.partial(feed_kernel, n_tensor, block, c * chunk_rows),
            [hbm_spec(), vmem_spec()]
            + [hbm_spec()] * (n_tensor - 1)
            + [vmem_spec()] * 3,
            [hbm_spec()] * n_tensor,
            [pltpu.HBM((chunk_rows, share), f32)]
            + [pltpu.HBM((chunk_rows, share), bf16)] * (n_tensor - 1),
            [
                pltpu.VMEM((chunk_rows, width), f32),
                pltpu.VMEM((n_tensor - 1, chunk_rows, cols_here), bf16),
                pltpu.VMEM((chunk_rows, share), f32),
                pltpu.VMEM((n_tensor - 1, chunk_rows, share), bf16),
                pltpu.VMEM((chunk_rows, width), bf16),
                pltpu.VMEM((chunk_rows, units_here), bf16),
                pltpu.VMEM(norm_gains.shape, f32),
                pltpu.SemaphoreType.DMA((n_tensor,)),
                pltpu.SemaphoreType.DMA((n_tensor,)),
            ],
            2 * chunk_rows * width * (width + 2 * units_here),
        )(
            *in_hbm([norm_gains]),
            tokens,
            *in_hbm(gated[c][:-1]),
            gated[c][-1],
            *whole,
        )
        own, *part = outs[:n_tensor]
        owns.append(own)
        parts.append(part)
        sums.append(None)
    for hop in range(n_tensor - 1):
        for c in range(CHUNKS):
            mine = parts[c][hop]
            if hop:
                mine = kernel_call(
                    add_kernel,
                    [vmem_spec()] * 2,
                    vmem_spec(),
                    shape_of((chunk_rows, share), bf16),
                    [],
                    0,
                    limit_mib=4,
                )(sums[c], mine)
            sums[c] = lax.ppermute(mine, "tensor", ring)

    so_far = []
    for c in range(CHUNKS):
        so_far = [
            pl.pallas_call(
                functools.partial(last_kernel, event_count, c * chunk_rows),
                in_specs=[smem_spec()] + [vmem_spec()] * 2 + [hbm_spec()] * len(so_far),
                out_specs=hbm_spec(),
                out_shape=shape_of((row_count, share), bf16),
                scratch_shapes=[
                    pltpu.VMEM((chunk_rows, share), bf16),
                    pltpu.SemaphoreType.DMA,
                ],
                input_output_aliases={3: 0} if so_far else {},
                compiler_params=pltpu.CompilerParams(vmem_limit_bytes=8 * 1024 * 1024),
                cost_estimate=pl.CostEstimate(
                    flops=0, bytes_accessed=chunk_rows * share * 8, transcendentals=0
                ),
                name="last",
            )(end_lengths, owns[c], sums[c], *so_far)
        ]
    (next_tokens,) = so_far

    state_shape = (sessions_here, heads_here, head_dim, head_dim)
    moved_states = kernel_call(
        unpack_kernel,
        [smem_spec(), hbm_spec()],
        hbm_spec(),
        shape_of(state_shape, f32),
        [
            pltpu.VMEM(state_shape, bf16),
            pltpu.VMEM(state_shape, f32),
            pltpu.SemaphoreType.DMA((sessions_here,)),
            pltpu.SemaphoreType.DMA((sessions_here,)),
        ],
        0,
        limit_mib=16,
    )(recv_src, *in_hbm([received]))
    return (next_tokens, moved_states)


def solution(mesh):
    placed = (
        P(("group", "dp"), None),
        P(("group", "dp"), "tensor", None, None),
        P(None, "dp", "tensor"),
        P(None, "dp", "tensor"),
        P(),
        P(),
        P(("group", "dp")),
        P(("group", "dp")),
    )

    return jax.shard_map(
        per_device,
        mesh=mesh,
        in_specs=placed,
        out_specs=(P(("group", "dp"), "tensor"), P(("group", "dp"), "tensor", None, None)),
        check_vma=False,
    )
```
